32 devices in a mesh: dp: 16 (over z, y, x), tensor: 2 (over core).
Axes of the slice: x: 2, y: 2, z: 4, core: 2. Of those that a mesh axis runs over, the one named last changes fastest.
Arguments:
- block_input: bfloat16 [16384, 1024], P('dp'), may hold values from -6 to 6
- w_query: bfloat16 [1024, 1024], P(None, 'tensor'), may hold values from -0.1875 to 0.1875
- w_key: bfloat16 [1024, 1024], P(None, 'tensor'), may hold values from -0.1875 to 0.1875
- w_value: bfloat16 [1024, 1024], P(None, 'tensor'), may hold values from -0.1875 to 0.1875
- w_out: bfloat16 [1024, 1024], P('tensor'), may hold values from -0.375 to 0.375
- w_gate: bfloat16 [1024, 4096], P(None, 'tensor'), may hold values from -0.1875 to 0.1875
- w_up: bfloat16 [1024, 4096], P(None, 'tensor'), may hold values from -0.1875 to 0.1875
- w_down: bfloat16 [4096, 1024], P('tensor'), may hold values from -0.09375 to 0.09375
- gain_attn: bfloat16 [1024], replicated, may hold values from 0.25 to 1.75
- gain_ffn: bfloat16 [1024], replicated, may hold values from 0.25 to 1.75
- item_lengths: int32 [32], P('dp'), may hold values from 0 to 32, as said below
- cotangent: bfloat16 [16384, 1024], P('dp'), may hold values from -6 to 6
Outputs:
- block_output: bfloat16 [16384, 1024], P('dp')
- grad_input: bfloat16 [16384, 1024], P('dp')
- grad_query: float32 [1024, 1024], P('dp', 'tensor')
- grad_key: float32 [1024, 1024], P('dp', 'tensor')
- grad_value: float32 [1024, 1024], P('dp', 'tensor')
- grad_out: float32 [1024, 1024], P('tensor', 'dp')
- grad_gate: float32 [1024, 4096], P('dp', 'tensor')
- grad_up: float32 [1024, 4096], P('dp', 'tensor')
- grad_down: float32 [4096, 1024], P('tensor', 'dp')
- grad_gain_attn: float32 [1024], P('dp')
- grad_gain_ffn: float32 [1024], P('dp')
The draws below stay inside these ranges and needn't reach their ends.
Inputs may be any that keep to these rules, and one draw needn't show every extreme that they name: `item_lengths`: frames used in each item slot of 32 frames: slot s of an index of dp holds its frames s * 32 to s * 32 + length - 1, the rest of the slot is padding; a length of 0 is an empty slot. Some slot is full in every draw.
All inputs are finite; a program needn't handle non-finite values.
Results may differ from the reference program's by a relative error of at most 0.02.
Values may be sent and summed in bfloat16 or wider, within the bound.
No kernel may reach another device: no remote copies, remote signals or barrier semaphores. Data moves between devices by JAX's collectives and lax.ppermute only.
A program may use at most 128 MiB of HBM per device.

```python
import math
import jax
import jax.numpy as jnp
from jax import lax

D = 1024
HEADS = 16
HD = 64
FF = 4096
POS = 16
SLOT = 32
ITEMS = 2
FR_DEV = 64
GROUPS = 16
FRAMES = 1024


def draw_item_lengths(key, part):
    folded = jax.random.fold_in(key, 11)
    first_key, second_key = jax.random.split(folded)
    total_slots = GROUPS * ITEMS
    base = jax.random.randint(first_key, (total_slots,), 0, SLOT + 1)
    chosen = jax.random.randint(second_key, (), 0, total_slots)
    return jnp.where(jnp.arange(total_slots) == chosen, SLOT, base).astype(jnp.int32)


def raised(array, own_key, source, target, shards_of, factor):
    def block_of(position):
        return (jnp.arange(array.shape[position]) // (array.shape[position] // shards_of)).reshape((-1,) + (1,) * (array.ndim - 1 - position))

    one_side = jax.random.permutation(own_key, shards_of)[block_of(target)]
    other_side = (block_of(target) + shards_of // 2) % shards_of
    return jnp.where((block_of(source) == one_side) | (block_of(source) == other_side), factor * array, array)


def block_scale(stream_key, dims, shards, least, largest):
    def one(dim, blocks):
        steps = jax.random.uniform(jax.random.fold_in(jax.random.fold_in(stream_key, 6), dim), (blocks,), jnp.float32, least / len(shards), largest / len(shards))
        return jnp.repeat(jnp.exp(steps), dims[dim] // blocks).reshape((-1,) + (1,) * (len(dims) - dim - 1))

    loudness = one(*shards[0])
    for cut in shards[1:]:
        loudness = loudness * one(*cut)
    return loudness


def normal_values(stream_key, extent, width, most, cuts=(), held_as=jnp.bfloat16):
    values = jax.random.normal(stream_key, extent, jnp.float32) * width
    if len(cuts) > 0:
        values = block_scale(stream_key, extent, cuts, -0.22, 0.18) * values
    return jnp.clip(values, min=-most, max=most).astype(held_as)


def bell_draw_with(key, extent, spread, reach, cuts, heavy, held_as=jnp.bfloat16):
    array = spread * jax.random.normal(key, extent, jnp.float32)
    if cuts:
        array = array * block_scale(key, extent, cuts, -0.22, 0.18)
    return jnp.clip(raised(array, jax.random.fold_in(key, 3), *heavy), -reach, reach).astype(held_as)


def setup_inputs(seed: int = 0) -> dict:
    splits = jax.random.split(jax.random.key(seed), 13)
    return {
        "block_input": normal_values(splits[0], (FRAMES * POS, D), 1.0, 6.0, ((0, 16),)),
        "w_query": normal_values(splits[1], (D, HEADS * HD), D ** -0.5, 0.1875, ((1, 2),)),
        "w_key": normal_values(splits[2], (D, HEADS * HD), D ** -0.5, 0.1875, ((1, 2),)),
        "w_value": normal_values(splits[3], (D, HEADS * HD), D ** -0.5, 0.1875, ((1, 2),)),
        "w_out": normal_values(splits[4], (HEADS * HD, D), (HEADS * HD // 4) ** -0.5, 0.375, ((0, 2),)),
        "w_gate": normal_values(splits[5], (D, FF), D ** -0.5, 0.1875, ((1, 2),)),
        "w_up": normal_values(splits[6], (D, FF), D ** -0.5, 0.1875, ((1, 2),)),
        "w_down": normal_values(splits[7], (FF, D), FF ** -0.5, 0.09375, ((0, 2),)),
        "gain_attn": jnp.clip(1.0 + 0.15 * jax.random.normal(splits[8], (D,), jnp.float32), 0.25, 1.75).astype(jnp.bfloat16),
        "gain_ffn": jnp.clip(1.0 + 0.15 * jax.random.normal(splits[9], (D,), jnp.float32), 0.25, 1.75).astype(jnp.bfloat16),
        "item_lengths": draw_item_lengths(jax.random.fold_in(splits[12], 71), 0),
        "cotangent": bell_draw_with(splits[11], (FRAMES * POS, D), 1.0, 6.0, ((0, 16),), (0, 1, 16, 2.0)),
    }


@jax.custom_vjp
def low(v):
    return lax.optimization_barrier(v.astype(jnp.bfloat16)).astype(jnp.float32)

@jax.custom_vjp
def low_back(v):
    return v

def low_keep(v):
    return (low(v), None)

def low_pass(kept, grad):
    return (grad,)

def back_keep(v):
    return (v, None)

def back_low(kept, grad):
    return (low(grad),)
low.defvjp(low_keep, low_pass)
low_back.defvjp(back_keep, back_low)
epsilon = 1e-05
precise = lax.Precision.HIGHEST

def precise_product(left_side, right_side):
    return jnp.dot(left_side, right_side, precision=precise, preferred_element_type=jnp.float32)

def rms_scale(token_rows, gain_vec):
    inverse = lax.rsqrt(lax.optimization_barrier(jnp.mean(token_rows * token_rows, axis=-1, keepdims=True)) + epsilon)
    return token_rows * inverse * gain_vec

def forward(params, token_rows):
    w_query, w_key, w_value, w_out, w_gate, w_up, w_down, gain_attn, gain_ffn = params
    frames = token_rows.shape[0] // POS
    normed = low(rms_scale(token_rows, gain_attn))
    query_heads = low_back(low(precise_product(normed, w_query))).reshape(frames, POS, HEADS, HD)
    key_heads = low_back(low(precise_product(normed, w_key))).reshape(frames, POS, HEADS, HD)
    value_heads = low_back(low(precise_product(normed, w_value))).reshape(frames, POS, HEADS, HD)
    scores = jnp.einsum('fqhd,fkhd->fhqk', query_heads, key_heads, precision=precise) * (1.0 / math.sqrt(HD))
    scores = low_back(scores)
    causal = jnp.arange(POS)[:, None] >= jnp.arange(POS)[None, :]
    scores = jnp.where(causal, scores, -1e+30)
    probs = low(jax.nn.softmax(scores, axis=-1))
    mixed = jnp.einsum('fhqk,fkhd->fqhd', probs, value_heads, precision=precise)
    mixed = low_back(low(mixed.reshape(token_rows.shape[0], HEADS * HD)))
    branch = low_back(precise_product(mixed, w_out))
    middle = token_rows + branch
    normed_two = low(rms_scale(middle, gain_ffn))
    gate_pre = low_back(precise_product(normed_two, w_gate))
    up_pre = low_back(precise_product(normed_two, w_up))
    hidden = low(jax.nn.silu(gate_pre) * up_pre)
    result = low_back(precise_product(hidden, w_down))
    return middle + result

def reference(block_input, w_query, w_key, w_value, w_out, w_gate, w_up, w_down, gain_attn, gain_ffn, item_lengths, cotangent):
    params = tuple((weight_arr.astype(jnp.float32) for weight_arr in (w_query, w_key, w_value, w_out, w_gate, w_up, w_down, gain_attn, gain_ffn)))
    group_tokens = FR_DEV * POS
    inputs = block_input.astype(jnp.float32).reshape(GROUPS, group_tokens, D)
    frame_index = jnp.arange(FR_DEV, dtype=jnp.int32)
    slot_index = frame_index // SLOT
    offset = frame_index % SLOT
    lengths_grid = item_lengths.reshape(GROUPS, ITEMS)
    live = (offset[None, :] < lengths_grid[:, slot_index]).astype(jnp.float32)
    token_live = jnp.repeat(live, POS, axis=1)
    seeds = cotangent.astype(jnp.float32).reshape(GROUPS, group_tokens, D) * token_live[:, :, None]

    def one_group(totals, pieces):
        group_rows, group_seed = pieces
        outputs, pullback = jax.vjp(forward, params, group_rows)
        param_grads, input_grad = pullback(group_seed)
        totals = jax.tree.map(jnp.add, totals, param_grads)
        return (totals, (outputs.astype(jnp.bfloat16), input_grad.astype(jnp.bfloat16)))
    zero_grads = tuple((jnp.zeros_like(weight_arr) for weight_arr in params))
    totals, (outputs, input_grads) = lax.scan(one_group, zero_grads, (inputs, seeds))
    return (outputs.reshape(FRAMES * POS, D), input_grads.reshape(FRAMES * POS, D), totals[0], totals[1], totals[2], totals[3], totals[4], totals[5], totals[6], totals[7], totals[8])
```

```python
import math

import jax
import jax.numpy as jnp
from jax import lax
from jax.sharding import PartitionSpec as P

HD = 64
POS = 16
SLOT = 32
LANES = 128


epsilon = 1e-05


def plain_product(left_side, right_side):
    return jnp.dot(left_side, right_side, preferred_element_type=jnp.float32)


def left_product(left_side, right_side):
    return lax.dot_general(
        left_side, right_side, (((0,), (0,)), ((), ())), preferred_element_type=jnp.float32
    )


def right_product(left_side, right_side):
    return lax.dot_general(
        left_side, right_side, (((1,), (1,)), ((), ())), preferred_element_type=jnp.float32
    )


def norm_parts(token_rows, gain_vec):
    inverse = lax.rsqrt(jnp.mean(token_rows * token_rows, axis=1, keepdims=True) + epsilon)
    scaled = token_rows * inverse
    return (scaled * gain_vec, scaled, inverse)


def norm_back(upstream, scaled, inverse, gain_vec):
    weighted = upstream * gain_vec
    return inverse * (weighted - scaled * jnp.mean(weighted * scaled, axis=1, keepdims=True))


def swap(array, axis, size, bit):
    return lax.ppermute(array, axis, [(i, i ^ bit) for i in range(size)])


def sum_over(partial, axis, size):
    bit = 1
    total = partial
    while bit < size:
        low = total.astype(jnp.bfloat16)
        total = low.astype(jnp.float32) + swap(low, axis, size, bit).astype(jnp.float32)
        bit *= 2
    return total


def scatter_sum(full, axis, size, bits):
    me = lax.axis_index(axis)
    rows, columns = full.shape
    block = full.astype(jnp.bfloat16).reshape(size, rows // size, columns)
    left = [1 << k for k in range(size.bit_length() - 1)]
    for bit in bits:
        inner = math.prod([2 for b in left if b < bit])
        block = block.reshape(-1, 2, inner, rows // size, columns)
        mine = (me // bit) % 2
        send = lax.dynamic_index_in_dim(block, 1 - mine, axis=1, keepdims=False)
        keep = lax.dynamic_index_in_dim(block, mine, axis=1, keepdims=False)
        came = swap(send, axis, size, bit)
        block = (keep.astype(jnp.float32) + came.astype(jnp.float32)).astype(jnp.bfloat16)
        left.remove(bit)
    return block.reshape(rows // size, columns).astype(jnp.float32)


def body_of(dp, tensor):
    n_bits = dp.bit_length() - 1
    all_bits = [1 << k for k in range(n_bits)]

    def order(start):
        return all_bits[start:] + all_bits[:start]

    def body(
        block_input,
        w_query,
        w_key,
        w_value,
        w_out,
        w_gate,
        w_up,
        w_down,
        gain_attn,
        gain_ffn,
        item_lengths,
        cotangent,
    ):
        token_count = block_input.shape[0]
        frames = token_count // POS
        local_heads = w_query.shape[1] // HD
        score_scale = 1.0 / math.sqrt(HD)
        inputs = block_input.astype(jnp.float32)
        gain_one = gain_attn.astype(jnp.float32)
        gain_two = gain_ffn.astype(jnp.float32)
        normed_pre, scaled_one, inverse_one = norm_parts(inputs, gain_one)
        normed = normed_pre.astype(jnp.bfloat16)
        query_flat = plain_product(normed, w_query).astype(jnp.bfloat16)
        key_flat = plain_product(normed, w_key).astype(jnp.bfloat16)
        value_flat = plain_product(normed, w_value).astype(jnp.bfloat16)
        query_heads = query_flat.reshape(frames, POS, local_heads, HD)
        key_heads = key_flat.reshape(frames, POS, local_heads, HD)
        value_heads = value_flat.reshape(frames, POS, local_heads, HD)
        scores = (
            jnp.einsum(
                "fqhd,fkhd->fhqk", query_heads, key_heads, preferred_element_type=jnp.float32
            )
            * score_scale
        )
        causal = lax.broadcasted_iota(jnp.int32, (POS, POS), 0) >= lax.broadcasted_iota(
            jnp.int32, (POS, POS), 1
        )
        scores = jnp.where(causal, scores, -1e30)
        probs = jax.nn.softmax(scores, axis=-1)
        probs_low = probs.astype(jnp.bfloat16)
        mixed_heads = jnp.einsum(
            "fhqk,fkhd->fqhd", probs_low, value_heads, preferred_element_type=jnp.float32
        )
        mixed = mixed_heads.reshape(token_count, local_heads * HD).astype(jnp.bfloat16)
        middle = inputs + sum_over(plain_product(mixed, w_out), "tensor", tensor)
        normed_mid, scaled_two, inverse_two = norm_parts(middle, gain_two)
        normed_two = normed_mid.astype(jnp.bfloat16)
        gate_pre = plain_product(normed_two, w_gate)
        up_pre = plain_product(normed_two, w_up)
        silu_gate = jax.nn.silu(gate_pre)
        hidden = (silu_gate * up_pre).astype(jnp.bfloat16)
        slot_count = item_lengths.shape[0]
        slot_index = lax.broadcasted_iota(jnp.int32, (frames, slot_count), 0) // SLOT
        item_ids = lax.broadcasted_iota(jnp.int32, (frames, slot_count), 1)
        frame_length = jnp.sum(jnp.where(slot_index == item_ids, item_lengths[None, :], 0), axis=1)
        offset = jnp.arange(frames, dtype=jnp.int32) % SLOT
        live_frames = (offset < frame_length).astype(jnp.float32)
        token_live = jnp.repeat(live_frames, POS)
        seed_rows = cotangent.astype(jnp.float32) * token_live[:, None]
        seed_low = seed_rows.astype(jnp.bfloat16)
        down_sum = scatter_sum(left_product(seed_low, hidden), "dp", dp, order(0))
        grad_hidden = right_product(seed_low, w_down)
        sigmoid_gate = jax.nn.sigmoid(gate_pre)
        grad_gate_pre = (
            grad_hidden * up_pre * (sigmoid_gate * (1.0 + gate_pre * (1.0 - sigmoid_gate)))
        ).astype(jnp.bfloat16)
        grad_up_pre = (grad_hidden * silu_gate).astype(jnp.bfloat16)
        gate_sum = scatter_sum(left_product(normed_two, grad_gate_pre), "dp", dp, order(1))
        up_sum = scatter_sum(left_product(normed_two, grad_up_pre), "dp", dp, order(2))
        partial_normed_two = right_product(grad_gate_pre, w_gate) + right_product(
            grad_up_pre, w_up
        )
        grad_normed_two = sum_over(partial_normed_two, "tensor", tensor)
        grad_gain_two = jnp.sum(grad_normed_two * scaled_two, axis=0)
        grad_middle = seed_rows + norm_back(grad_normed_two, scaled_two, inverse_two, gain_two)
        middle_low = grad_middle.astype(jnp.bfloat16)
        grad_out = left_product(middle_low, mixed)
        grad_mixed = (
            right_product(middle_low, w_out)
            .astype(jnp.bfloat16)
            .reshape(frames, POS, local_heads, HD)
        )
        grad_probs = jnp.einsum(
            "fqhd,fkhd->fhqk", grad_mixed, value_heads, preferred_element_type=jnp.float32
        )
        grad_values = jnp.einsum(
            "fhqk,fqhd->fkhd", probs_low, grad_mixed, preferred_element_type=jnp.float32
        ).astype(jnp.bfloat16)
        grad_scores = (
            probs * (grad_probs - jnp.sum(grad_probs * probs, axis=-1, keepdims=True))
        ).astype(jnp.bfloat16)
        grad_queries = (
            jnp.einsum(
                "fhqk,fkhd->fqhd", grad_scores, key_heads, preferred_element_type=jnp.float32
            )
            * score_scale
        ).astype(jnp.bfloat16)
        grad_keys = (
            jnp.einsum(
                "fhqk,fqhd->fkhd", grad_scores, query_heads, preferred_element_type=jnp.float32
            )
            * score_scale
        ).astype(jnp.bfloat16)
        flat_width = local_heads * HD
        grad_queries = grad_queries.reshape(token_count, flat_width)
        grad_keys = grad_keys.reshape(token_count, flat_width)
        grad_values = grad_values.reshape(token_count, flat_width)
        grads_qk = left_product(normed, jnp.concatenate([grad_queries, grad_keys], axis=1))
        qk_sum = scatter_sum(grads_qk, "dp", dp, order(0))
        grad_value = left_product(normed, grad_values)
        partial_normed = (
            right_product(grad_queries, w_query)
            + right_product(grad_keys, w_key)
            + right_product(grad_values, w_value)
        )
        grad_normed = sum_over(partial_normed, "tensor", tensor)
        grad_gain_one = jnp.sum(grad_normed * scaled_one, axis=0)
        grad_input = (
            grad_middle + norm_back(grad_normed, scaled_one, inverse_one, gain_one)
        ).astype(jnp.bfloat16)
        gains = jnp.concatenate(
            [
                grad_gain_one[:, None],
                grad_gain_two[:, None],
                jnp.zeros((grad_gain_one.shape[0], LANES - 2), jnp.float32),
            ],
            axis=1,
        )
        vog_sum = scatter_sum(
            jnp.concatenate([grad_value, grad_out, gains], axis=1), "dp", dp, order(1)
        )
        block_output = (
            middle + sum_over(plain_product(hidden, w_down), "tensor", tensor)
        ).astype(jnp.bfloat16)
        return (
            block_output,
            grad_input,
            qk_sum[:, :flat_width],
            qk_sum[:, flat_width:],
            vog_sum[:, :flat_width],
            vog_sum[:, flat_width : 2 * flat_width].T,
            gate_sum,
            up_sum,
            down_sum.T,
            vog_sum[:, 2 * flat_width],
            vog_sum[:, 2 * flat_width + 1],
        )

    return body


def solution(mesh):
    placed = (
        P("dp", None),
        P(None, "tensor"),
        P(None, "tensor"),
        P(None, "tensor"),
        P("tensor", None),
        P(None, "tensor"),
        P(None, "tensor"),
        P("tensor", None),
        P(),
        P(),
        P("dp"),
        P("dp", None),
    )
    return jax.shard_map(
        body_of(mesh.shape["dp"], mesh.shape["tensor"]),
        mesh=mesh,
        in_specs=placed,
        out_specs=(
            P("dp", None),
            P("dp", None),
            P("dp", "tensor"),
            P("dp", "tensor"),
            P("dp", "tensor"),
            P("tensor", "dp"),
            P("dp", "tensor"),
            P("dp", "tensor"),
            P("tensor", "dp"),
            P("dp"),
            P("dp"),
        ),
        check_vma=False,
    )
```

```python
import functools
import math

import jax
import jax.numpy as jnp
from jax import lax
from jax.experimental import pallas as pl
from jax.experimental.pallas import tpu as pltpu
from jax.sharding import PartitionSpec as P

HD = 64
POS = 16
SLOT = 32
LANES = 128
TILE = 128
MIB = 1 << 20

epsilon = 1e-05
f32 = jnp.float32
bf16 = jnp.bfloat16
SCALE = 1.0 / math.sqrt(HD)


def nn(left, right):
    return lax.dot_general(left, right, (((1,), (0,)), ((), ())), preferred_element_type=f32)


def nt(left, right):
    return lax.dot_general(left, right, (((1,), (1,)), ((), ())), preferred_element_type=f32)


def tn(left, right):
    return lax.dot_general(left, right, (((0,), (0,)), ((), ())), preferred_element_type=f32)


def call(body, name, grid, ins, outs, scratch=(), vmem=40, scalars=0, aliases=None, cost=None):
    return pl.pallas_call(
        body,
        grid_spec=pltpu.PrefetchScalarGridSpec(
            num_scalar_prefetch=scalars,
            grid=grid,
            in_specs=ins,
            out_specs=[spec for spec, _, _ in outs],
            scratch_shapes=scratch,
        ),
        out_shape=[jax.ShapeDtypeStruct(shape, dtype) for _, shape, dtype in outs],
        input_output_aliases=aliases or {},
        compiler_params=pltpu.CompilerParams(vmem_limit_bytes=vmem * MIB),
        cost_estimate=pl.CostEstimate(
            flops=int(cost[0]), bytes_accessed=int(cost[1]), transcendentals=0
        ),
        name=name,
    )


def rows_of(block, width):
    return pl.BlockSpec((block, width), lambda i, *_: (i, 0))


def whole(*shape):
    return pl.BlockSpec(shape, lambda *_: (0,) * len(shape))


def inverse_rms(values):
    return lax.rsqrt(jnp.mean(values * values, axis=1, keepdims=True) + epsilon)


def put_transposed(ref, me, values):
    parts, depth, _ = ref.shape
    turned = values.T
    for g in range(parts):
        ref[g ^ me] = turned[g * depth : (g + 1) * depth]


def pair_mask():
    rows = lax.broadcasted_iota(jnp.int32, (TILE, 2 * TILE), 0)
    keys = lax.broadcasted_iota(jnp.int32, (TILE, 2 * TILE), 1) & (TILE - 1)
    return (rows // POS == keys // POS) & (keys <= rows)


def two_heads(values):
    first = lax.broadcasted_iota(jnp.int32, values.shape, 1) < HD
    zero = jnp.zeros_like(values)
    return jnp.concatenate(
        [jnp.where(first, values, zero), jnp.where(first, zero, values)], axis=0
    )


def one_pair(values):
    first = lax.broadcasted_iota(jnp.int32, (TILE, LANES), 1) < HD
    return jnp.where(first, values[:TILE], values[TILE:])


def per_head(op, values):
    both = [
        jnp.broadcast_to(op(values[:, s : s + TILE], axis=1, keepdims=True), (TILE, TILE))
        for s in (0, TILE)
    ]
    return jnp.concatenate(both, axis=1)


def probs_of(queries, keys, mask):
    scores = jnp.where(mask, nt(queries, keys) * SCALE, -1e30)
    powers = jnp.exp(scores - per_head(jnp.max, scores))
    return powers / per_head(jnp.sum, powers)


def pairs_of(rows, width):
    return [
        (pl.ds(t * TILE, TILE), pl.ds(p * LANES, LANES))
        for t in range(rows // TILE)
        for p in range(width // LANES)
    ]


def attention_body(x_ref, gain_ref, wq_ref, wk_ref, wv_ref, wo_ref, q_ref, k_ref, v_ref, m_ref, part_ref):
    values = x_ref[...].astype(f32)
    normed = (values * inverse_rms(values) * gain_ref[...].astype(f32)).astype(bf16)
    q_ref[...] = nn(normed, wq_ref[...]).astype(bf16)
    k_ref[...] = nn(normed, wk_ref[...]).astype(bf16)
    v_ref[...] = nn(normed, wv_ref[...]).astype(bf16)
    mask = pair_mask()
    for at in pairs_of(*q_ref.shape):
        probs = probs_of(q_ref[at], two_heads(k_ref[at]), mask)
        m_ref[at] = nn(probs.astype(bf16), two_heads(v_ref[at])).astype(bf16)
    part_ref[...] = nn(m_ref[...], wo_ref[...]).astype(bf16)


def attention(x, gain, wq, wk, wv, wo):
    rows, width = x.shape
    heads = wq.shape[1]
    block = 512
    outs = [(rows_of(block, heads), (rows, heads), bf16)] * 4
    outs += [(rows_of(block, width), (rows, width), bf16)]
    return call(
        attention_body,
        "attention_forward",
        (rows // block,),
        [rows_of(block, width), whole(1, width)]
        + [whole(width, heads)] * 3
        + [whole(heads, width)],
        outs,
        vmem=58,
        cost=(8 * rows * width * heads, 12 * MIB),
    )(x, gain, wq, wk, wv, wo)


def seed_body(lengths_ref, me_ref, cot_ref, seed_ref, turned_ref):
    block = cot_ref.shape[0]
    first = pl.program_id(0) * block
    length = lengths_ref[first // (SLOT * POS)]
    row = lax.broadcasted_iota(jnp.int32, cot_ref.shape, 0) + first % (SLOT * POS)
    cot = cot_ref[...].astype(f32)
    seed = jnp.where(row // POS < length, cot, 0.0).astype(bf16)
    seed_ref[...] = seed
    put_transposed(turned_ref, me_ref[0], seed)


def turned_out(parts, depth, rows, block):
    return (
        pl.BlockSpec((parts, depth, block), lambda i, *_: (0, 0, i)),
        (parts, depth, rows),
        bf16,
    )


def seeds(lengths, me, cot, parts):
    rows, width = cot.shape
    block = 256
    return call(
        seed_body,
        "seed_rows",
        (rows // block,),
        [rows_of(block, width)],
        [
            (rows_of(block, width), (rows, width), bf16),
            turned_out(parts, width // parts, rows, block),
        ],
        vmem=16,
        scalars=2,
        cost=(4 * rows * width, 6 * MIB),
    )(lengths, me, cot)


def middle_body(me_ref, x_ref, own_ref, peer_ref, gain_ref, middle_ref, normed_ref, turned_ref):
    middle = x_ref[...].astype(f32) + (own_ref[...].astype(f32) + peer_ref[...].astype(f32))
    middle_ref[...] = middle
    normed = (middle * inverse_rms(middle) * gain_ref[...].astype(f32)).astype(bf16)
    normed_ref[...] = normed
    put_transposed(turned_ref, me_ref[0], normed)


def middles(me, x, own, peer, gain, parts):
    rows, width = x.shape
    block = 256
    return call(
        middle_body,
        "middle_rows",
        (rows // block,),
        [rows_of(block, width)] * 3 + [whole(1, width)],
        [
            (rows_of(block, width), (rows, width), f32),
            (rows_of(block, width), (rows, width), bf16),
            turned_out(parts, width // parts, rows, block),
        ],
        vmem=24,
        scalars=1,
        cost=(8 * rows * width, 14 * MIB),
    )(me, x, own, peer, gain)


def places(parts, bits):
    count = len(bits)
    return [
        sum(bit for n, bit in enumerate(bits) if place >> (count - 1 - n) & 1)
        for place in range(parts)
    ]


def put_pieces(keep_ref, send_ref, column, values, order, first):
    half, _, depth, _ = keep_ref.shape
    low = values.astype(bf16)
    for n in range(values.shape[0] // depth):
        place = order.index(first + n)
        ref, at = (keep_ref, place) if place < half else (send_ref, place - half)
        for c in range(values.shape[1] // LANES):
            ref[at, column + c] = low[
                n * depth : (n + 1) * depth, c * LANES : (c + 1) * LANES
            ]


def product_pieces(keep_ref, send_ref, column, turned_ref, right, order):
    parts, depth, rows = turned_ref.shape
    group = max(1, 256 // depth)
    for first in range(0, parts, group):
        left = turned_ref[pl.ds(first, group)].reshape(group * depth, rows)
        put_pieces(keep_ref, send_ref, column, nn(left, right), order, first)


def hidden_body(order, first_call, *refs):
    (n_ref, nt_ref, s_ref, st_ref, wg_ref, wu_ref, wd_ref) = refs[:7]
    h_ref, gg_ref, gu_ref, keep_ref, send_ref = refs[7 if first_call else 10 :]
    rows = n_ref.shape[0]
    step = 256
    for r in range(0, rows, step):
        at = pl.ds(r, step)
        gate = nn(n_ref[at], wg_ref[...])
        up = nn(n_ref[at], wu_ref[...])
        back = nt(s_ref[at], wd_ref[...])
        sig = 1.0 / (1.0 + jnp.exp(-gate))
        silu = gate * sig
        h_ref[at] = (silu * up).astype(bf16)
        gg_ref[at] = (back * up * (sig * (1.0 + gate * (1.0 - sig)))).astype(bf16)
        gu_ref[at] = (back * silu).astype(bf16)
    columns = h_ref.shape[1] // LANES
    product_pieces(keep_ref, send_ref, 0, nt_ref, gg_ref[...], order)
    product_pieces(keep_ref, send_ref, columns, nt_ref, gu_ref[...], order)
    product_pieces(keep_ref, send_ref, 2 * columns, st_ref, h_ref[...], order)


def hidden_chunk(chunk, chunks, order, normed, normed_t, seed, seed_t, wg, wu, wd, earlier):
    rows, width = normed.shape
    parts, depth, _ = normed_t.shape
    hidden = wg.shape[1]
    share = hidden // chunks
    block = min(256, share)
    steps = share // block
    groups = 3 * block // LANES
    columns = pl.BlockSpec((rows, block), lambda j: (0, chunk * steps + j))
    w_columns = pl.BlockSpec((width, block), lambda j: (0, chunk * steps + j))
    w_rows = pl.BlockSpec((block, width), lambda j: (chunk * steps + j, 0))
    resident = pl.BlockSpec(memory_space=pltpu.VMEM)
    pieces = (
        pl.BlockSpec((parts // 2, groups, depth, LANES), lambda j: (0, j, 0, 0)),
        (parts // 2, steps * groups, depth, LANES),
        bf16,
    )
    ins = [resident] * 4 + [w_columns, w_columns, w_rows]
    args = [normed, normed_t, seed, seed_t, wg, wu, wd]
    aliases = {}
    if earlier is not None:
        ins += [pl.BlockSpec(memory_space=pl.ANY)] * 3
        aliases = {7: 0, 8: 1, 9: 2}
        args += list(earlier)
    return call(
        functools.partial(hidden_body, order, earlier is None),
        "hidden_units",
        (steps,),
        ins,
        [(columns, (rows, hidden), bf16)] * 3 + [pieces, pieces],
        vmem=40,
        aliases=aliases,
        cost=(12 * rows * width * share, 20 * MIB),
    )(*args)


def back_body(gg_ref, gu_ref, wg_ref, wu_ref, part_ref, total_ref):
    step = pl.program_id(0)
    new = nt(gg_ref[...], wg_ref[...]) + nt(gu_ref[...], wu_ref[...])

    @pl.when(step == 0)
    def _():
        total_ref[...] = new

    @pl.when(step > 0)
    def _():
        total_ref[...] += new

    @pl.when(step == pl.num_programs(0) - 1)
    def _():
        part_ref[...] = total_ref[...].astype(bf16)


def normed_two_back(gg, gu, wg, wu):
    rows, hidden = gg.shape
    width = wg.shape[0]
    block = min(512, hidden)
    columns = lambda n: pl.BlockSpec((n, block), lambda j: (0, j))
    return call(
        back_body,
        "normed_two_back",
        (hidden // block,),
        [columns(rows)] * 2 + [columns(width)] * 2,
        [(whole(rows, width), (rows, width), bf16)],
        scratch=[pltpu.VMEM((rows, width), f32)],
        vmem=40,
        cost=(4 * rows * width * hidden, 18 * MIB),
    )(gg, gu, wg, wu)[0]


def attention_back_body(
    me_ref, x_ref, mid_ref, own_ref, peer_ref, seed_ref, q_ref, k_ref, v_ref, g1_ref, g2_ref,
    wq_ref, wk_ref, wv_ref, wo_ref,
    gm_ref, gmt_ref, nt_ref, gqkv_ref, part_ref, gain_ref, mixed_ref,
):
    heads = q_ref.shape[1]
    upstream = own_ref[...].astype(f32) + peer_ref[...].astype(f32)
    middle = mid_ref[...]
    inverse = inverse_rms(middle)
    scaled = middle * inverse
    gain_part = jnp.sum(upstream * scaled, axis=0, keepdims=True)

    @pl.when(pl.program_id(0) == 0)
    def _():
        gain_ref[...] = gain_part

    @pl.when(pl.program_id(0) > 0)
    def _():
        gain_ref[...] += gain_part

    weighted = upstream * g2_ref[...].astype(f32)
    grad_middle = seed_ref[...].astype(f32) + inverse * (
        weighted - scaled * jnp.mean(weighted * scaled, axis=1, keepdims=True)
    )
    gm_ref[...] = grad_middle
    low = grad_middle.astype(bf16)
    mixed_ref[...] = nt(low, wo_ref[...]).astype(bf16)
    put_transposed(gmt_ref, me_ref[0], low)
    mask = pair_mask()
    for at in pairs_of(*q_ref.shape):
        rows, lanes = at
        queries, grads = q_ref[at], mixed_ref[at]
        keys, values = two_heads(k_ref[at]), two_heads(v_ref[at])
        probs = probs_of(queries, keys, mask)
        grad_probs = nt(grads, values)
        grad_values = one_pair(tn(probs.astype(bf16), grads))
        inner = per_head(jnp.sum, grad_probs * probs)
        grad_scores = (probs * (grad_probs - inner)).astype(bf16)
        grad_queries = nn(grad_scores, keys) * SCALE
        grad_keys = one_pair(tn(grad_scores, queries)) * SCALE
        for n, grad in enumerate((grad_queries, grad_keys, grad_values)):
            gqkv_ref[rows, pl.ds(n * heads + lanes.start, LANES)] = grad.astype(bf16)
    part = nt(gqkv_ref[:, :heads], wq_ref[...])
    part += nt(gqkv_ref[:, heads : 2 * heads], wk_ref[...])
    part += nt(gqkv_ref[:, 2 * heads :], wv_ref[...])
    part_ref[...] = part.astype(bf16)
    inputs = x_ref[...].astype(f32)
    normed = (inputs * inverse_rms(inputs) * g1_ref[...].astype(f32)).astype(bf16)
    put_transposed(nt_ref, me_ref[0], normed)


def attention_back(me, x, middle, own, peer, seed, q, k, v, g1, g2, wq, wk, wv, wo, parts):
    rows, width = x.shape
    heads = q.shape[1]
    block = 256
    turned = turned_out(parts, width // parts, rows, block)
    return call(
        attention_back_body,
        "attention_backward",
        (rows // block,),
        [rows_of(block, width)] * 5
        + [rows_of(block, heads)] * 3
        + [whole(1, width)] * 2
        + [whole(width, heads)] * 3
        + [whole(heads, width)],
        [
            (rows_of(block, width), (rows, width), f32),
            turned,
            turned,
            (rows_of(block, 3 * heads), (rows, 3 * heads), bf16),
            (rows_of(block, width), (rows, width), bf16),
            (whole(1, width), (1, width), f32),
        ],
        scratch=[pltpu.VMEM((block, heads), bf16)],
        vmem=40,
        scalars=1,
        cost=(8 * rows * width * heads, 30 * MIB),
    )(me, x, middle, own, peer, seed, q, k, v, g1, g2, wq, wk, wv, wo)


def columns_body(order, turned_ref, right_ref, keep_ref, send_ref):
    product_pieces(keep_ref, send_ref, 0, turned_ref, right_ref[...], order)


def query_key_pieces(order, normed_t, gqkv, heads):
    parts, depth, rows = normed_t.shape
    block = min(256, heads)
    steps = 2 * heads // block
    groups = block // LANES
    pieces = (
        pl.BlockSpec((parts // 2, groups, depth, LANES), lambda j: (0, j, 0, 0)),
        (parts // 2, steps * groups, depth, LANES),
        bf16,
    )
    return call(
        functools.partial(columns_body, order),
        "query_key_grads",
        (steps,),
        [
            pl.BlockSpec(memory_space=pltpu.VMEM),
            pl.BlockSpec((rows, block), lambda j: (0, j)),
        ],
        [pieces, pieces],
        vmem=24,
        cost=(4 * rows * parts * depth * heads, 6 * MIB),
    )(normed_t, gqkv)


def value_out_body(order, me_ref, nt_ref, mt_ref, gv_ref, m_ref, g1_ref, g2_ref, keep_ref, send_ref):
    heads = m_ref.shape[1]
    groups = heads // LANES
    product_pieces(keep_ref, send_ref, 0, nt_ref, gv_ref[...], order)
    product_pieces(keep_ref, send_ref, groups, mt_ref, m_ref[...], order)
    row = lax.broadcasted_iota(jnp.int32, (LANES, g1_ref.shape[1]), 0)
    both = jnp.where(row == 0, g1_ref[...], jnp.where(row == 1, g2_ref[...], 0.0))
    turned = both.T.astype(bf16)
    half, _, depth, _ = keep_ref.shape
    bits = [order[1 << n] for n in reversed(range((2 * half).bit_length() - 1))]
    for g in range(2 * half):
        relative = g ^ me_ref[0]
        place = 0
        for bit in bits:
            place = 2 * place + (relative & bit != 0).astype(jnp.int32)
        piece = turned[g * depth : (g + 1) * depth]

        @pl.when(place < half)
        def _():
            keep_ref[jnp.minimum(place, half - 1), 2 * groups] = piece

        @pl.when(place >= half)
        def _():
            send_ref[jnp.maximum(place - half, 0), 2 * groups] = piece


def value_out_pieces(order, me, normed_t, middle_t, gqkv, mixed, gain_one, gain_two):
    parts, depth, rows = normed_t.shape
    heads = mixed.shape[1]
    groups = 2 * heads // LANES + 1
    shape = (parts // 2, groups, depth, LANES)
    return call(
        functools.partial(value_out_body, order),
        "value_out_grads",
        (1,),
        [
            whole(parts, depth, rows),
            whole(parts, depth, rows),
            pl.BlockSpec((rows, heads), lambda *_: (0, 2)),
            whole(rows, heads),
            whole(1, parts * depth),
            whole(1, parts * depth),
        ],
        [(whole(*shape), shape, bf16)] * 2,
        vmem=40,
        scalars=1,
        cost=(4 * rows * parts * depth * heads, 10 * MIB),
    )(me, normed_t, middle_t, gqkv, mixed, gain_one, gain_two)


def input_grad_body(x_ref, gm_ref, own_ref, peer_ref, gain_ref, out_ref, sum_ref):
    inputs = x_ref[...].astype(f32)
    inverse = inverse_rms(inputs)
    scaled = inputs * inverse
    upstream = own_ref[...].astype(f32) + peer_ref[...].astype(f32)
    part = jnp.sum(upstream * scaled, axis=0, keepdims=True)

    @pl.when(pl.program_id(0) == 0)
    def _():
        sum_ref[...] = part

    @pl.when(pl.program_id(0) > 0)
    def _():
        sum_ref[...] += part

    weighted = upstream * gain_ref[...].astype(f32)
    out_ref[...] = (
        gm_ref[...]
        + inverse * (weighted - scaled * jnp.mean(weighted * scaled, axis=1, keepdims=True))
    ).astype(bf16)


def input_grad(x, grad_middle, own, peer, gain):
    rows, width = x.shape
    block = 256
    return call(
        input_grad_body,
        "input_grad",
        (rows // block,),
        [rows_of(block, width)] * 4 + [whole(1, width)],
        [(rows_of(block, width), (rows, width), bf16), (whole(1, width), (1, width), f32)],
        vmem=24,
        cost=(10 * rows * width, 12 * MIB),
    )(x, grad_middle, own, peer, gain)


def total_of(refs):
    total = refs[0][0].astype(f32)
    for ref in refs[1:]:
        total += ref[0].astype(f32)
    return total


def last_hidden_body(count, first_call, *refs):
    total = total_of(refs[:count])
    gate_ref, up_ref, down_ref = refs[count if first_call else count + 3 :]
    third = total.shape[0] // 3
    for c in range(third):
        at = slice(c * LANES, (c + 1) * LANES)
        gate_ref[:, at] = total[c]
        up_ref[:, at] = total[third + c]
        down_ref[at, :] = total[2 * third + c].T


def last_hidden(chunk, chunks, steps, arrays, hidden, earlier):
    _, groups, depth, _ = arrays[0].shape
    share = groups // steps
    block = share // 3 * LANES
    ins = [pl.BlockSpec((1, share, depth, LANES), lambda j: (0, j, 0, 0))] * len(arrays)
    args = list(arrays)
    aliases = {}
    if earlier is not None:
        ins += [pl.BlockSpec(memory_space=pl.ANY)] * 3
        aliases = {len(arrays) + n: n for n in range(3)}
        args += list(earlier)
    wide = (
        pl.BlockSpec((depth, block), lambda j: (0, chunk * steps + j)),
        (depth, hidden),
        f32,
    )
    tall = (
        pl.BlockSpec((block, depth), lambda j: (chunk * steps + j, 0)),
        (hidden, depth),
        f32,
    )
    return call(
        functools.partial(last_hidden_body, len(arrays), earlier is None),
        "hidden_grads_out",
        (steps,),
        ins,
        [wide, wide, tall],
        vmem=16,
        aliases=aliases,
        cost=(6 * groups * depth * LANES, MIB),
    )(*args)


def last_query_key_body(count, *refs):
    total = total_of(refs[:count])
    half = total.shape[0] // 2
    for c in range(half):
        at = slice(c * LANES, (c + 1) * LANES)
        refs[count][:, at] = total[c]
        refs[count + 1][:, at] = total[half + c]


def last_value_out_body(count, *refs):
    total = total_of(refs[:count])
    value_ref, out_ref, gain_ref = refs[count:]
    half = total.shape[0] // 2
    for c in range(half):
        at = slice(c * LANES, (c + 1) * LANES)
        value_ref[:, at] = total[c]
        out_ref[at, :] = total[half + c].T
    gain_ref[...] = total[2 * half].T


def last_few(body, name, arrays, shapes):
    _, groups, depth, _ = arrays[0].shape
    return call(
        functools.partial(body, len(arrays)),
        name,
        (1,),
        [pl.BlockSpec((1, groups, depth, LANES), lambda j: (0, 0, 0, 0))] * len(arrays),
        [(whole(*shape), shape, f32) for shape in shapes],
        vmem=16,
        cost=(6 * groups * depth * LANES, MIB),
    )(*arrays)


def swap(array, axis, size, bit):
    return lax.ppermute(array, axis, [(i, i ^ bit) for i in range(size)])


def both_shares(partial, size):
    bit = 1
    while 2 * bit < size:
        other = swap(partial, "tensor", size, bit)
        partial = (partial.astype(f32) + other.astype(f32)).astype(bf16)
        bit *= 2
    return partial, swap(partial, "tensor", size, bit)


def scattered(keep, send, size, bits):
    arrays = [keep]
    half = size // 2
    for n, bit in enumerate(bits):
        arrays.append(swap(send, "dp", size, bit))
        half //= 2
        if half:
            total = arrays[0][half : 2 * half].astype(f32)
            for array in arrays[1:]:
                total += array[half : 2 * half].astype(f32)
            send = total.astype(bf16)
    return arrays


def body_of(dp, tensor):
    n_bits = dp.bit_length() - 1
    all_bits = [1 << k for k in range(n_bits)]

    def order(*start):
        return [1 << k for k in start] + [b for b in all_bits if b.bit_length() - 1 not in start]

    bits_of = [order(0, 1), order(1, 0), order(2, 3), order(1, 0), order(0, 1), order(1, 0)]

    def body(
        block_input,
        w_query,
        w_key,
        w_value,
        w_out,
        w_gate,
        w_up,
        w_down,
        gain_attn,
        gain_ffn,
        item_lengths,
        cotangent,
    ):
        rows, width = block_input.shape
        heads = w_query.shape[1]
        hidden_units = w_gate.shape[1]
        chunks = 4
        me = lax.axis_index("dp").astype(jnp.int32).reshape(1)
        gain_one = gain_attn.reshape(1, width)
        gain_two = gain_ffn.reshape(1, width)
        q, k, v, mixed, part = attention(block_input, gain_one, w_query, w_key, w_value, w_out)
        own, peer = both_shares(part, tensor)
        seed, seed_t = seeds(item_lengths, me, cotangent, dp)
        middle, normed_two, normed_two_t = middles(me, block_input, own, peer, gain_two, dp)
        acts = None
        pieces = []
        for c in range(chunks):
            out = hidden_chunk(
                c,
                chunks,
                places(dp, bits_of[c]),
                normed_two,
                normed_two_t,
                seed,
                seed_t,
                w_gate,
                w_up,
                w_down,
                acts,
            )
            acts = out[:3]
            pieces.append(scattered(out[3], out[4], dp, bits_of[c]))
        hidden, grad_gate_pre, grad_up_pre = acts
        own, peer = both_shares(
            normed_two_back(grad_gate_pre, grad_up_pre, w_gate, w_up), tensor
        )
        down = nn(hidden, w_down).astype(bf16)
        down_own, down_peer = both_shares(down, tensor)
        grad_middle, middle_t, normed_t, gqkv, part, gain_two_sum = attention_back(
            me, block_input, middle, own, peer, seed, q, k, v, gain_one, gain_two,
            w_query, w_key, w_value, w_out, dp,
        )
        own, peer = both_shares(part, tensor)
        keep, send = query_key_pieces(places(dp, bits_of[4]), normed_t, gqkv, heads)
        qk = scattered(keep, send, dp, bits_of[4])
        grad_input, gain_one_sum = input_grad(block_input, grad_middle, own, peer, gain_one)
        keep, send = value_out_pieces(
            places(dp, bits_of[5]), me, normed_t, middle_t, gqkv, mixed, gain_one_sum, gain_two_sum
        )
        vo = scattered(keep, send, dp, bits_of[5])
        block_output = (
            middle + (down_own.astype(f32) + down_peer.astype(f32))
        ).astype(bf16)
        grads = None
        steps = hidden_units // chunks // min(256, hidden_units // chunks)
        for c in range(chunks):
            grads = last_hidden(c, chunks, steps, pieces[c], hidden_units, grads)
        depth = width // dp
        grad_query, grad_key = last_few(
            last_query_key_body, "query_key_out", qk, [(depth, heads)] * 2
        )
        grad_value, grad_out, gains = last_few(
            last_value_out_body,
            "value_out_out",
            vo,
            [(depth, heads), (heads, depth), (LANES, depth)],
        )
        return (
            block_output,
            grad_input,
            grad_query,
            grad_key,
            grad_value,
            grad_out,
            *grads,
            gains[0],
            gains[1],
        )

    return body


def solution(mesh):
    placed = (
        P("dp", None),
        P(None, "tensor"),
        P(None, "tensor"),
        P(None, "tensor"),
        P("tensor", None),
        P(None, "tensor"),
        P(None, "tensor"),
        P("tensor", None),
        P(),
        P(),
        P("dp"),
        P("dp", None),
    )
    return jax.shard_map(
        body_of(mesh.shape["dp"], mesh.shape["tensor"]),
        mesh=mesh,
        in_specs=placed,
        out_specs=(
            P("dp", None),
            P("dp", None),
            P("dp", "tensor"),
            P("dp", "tensor"),
            P("dp", "tensor"),
            P("tensor", "dp"),
            P("dp", "tensor"),
            P("dp", "tensor"),
            P("tensor", "dp"),
            P("dp"),
            P("dp"),
        ),
        check_vma=False,
    )
```

```python
import functools
import math

import jax
import jax.numpy as jnp
from jax import lax
from jax.experimental import pallas as pl
from jax.experimental.pallas import tpu as pltpu
from jax.sharding import PartitionSpec as P

HD = 64
POS = 16
SLOT = 32
LANES = 128
TILE = 128
MIB = 1 << 20
HALVES = 2
COST = 1e-6

epsilon = 1e-05
f32 = jnp.float32
bf16 = jnp.bfloat16
SCALE = 1.0 / math.sqrt(HD)
ANYWHERE = jax.ShapeDtypeStruct


def nn(left, right):
    return lax.dot_general(left, right, (((1,), (0,)), ((), ())), preferred_element_type=f32)


def nt(left, right):
    return lax.dot_general(left, right, (((1,), (1,)), ((), ())), preferred_element_type=f32)


def tn(left, right):
    return lax.dot_general(left, right, (((0,), (0,)), ((), ())), preferred_element_type=f32)


def call(body, name, grid, ins, outs, scratch=(), vmem=40, scalars=0, aliases=None, cost=None, far=()):
    kernel = pl.pallas_call(
        body,
        grid_spec=pltpu.PrefetchScalarGridSpec(
            num_scalar_prefetch=scalars,
            grid=grid,
            in_specs=ins,
            out_specs=[spec for spec, *_ in outs],
            scratch_shapes=scratch,
        ),
        out_shape=[
            (where[0] if where else pltpu.HBM)(shape, dtype) for _, shape, dtype, *where in outs
        ],
        input_output_aliases=aliases or {},
        compiler_params=pltpu.CompilerParams(vmem_limit_bytes=vmem * MIB),
        cost_estimate=pl.CostEstimate(
            flops=int(cost[0] * COST), bytes_accessed=int(cost[1] * COST), transcendentals=0
        ),
        name=name,
    )

    def run(*args):
        return kernel(
            *(
                pltpu.with_memory_space_constraint(arg, pltpu.HBM) if n - scalars in far else arg
                for n, arg in enumerate(args)
            )
        )

    return run


def rows_of(block, width):
    return pl.BlockSpec((block, width), lambda i, *_: (i, 0))


def whole(*shape):
    return pl.BlockSpec(shape, lambda *_: (0,) * len(shape))


def row_of(gain_ref):
    return gain_ref[...].astype(f32).reshape(1, -1)


def inverse_rms(values):
    return lax.rsqrt(jnp.mean(values * values, axis=1, keepdims=True) + epsilon)


def put_transposed(ref, me, values):
    parts, depth, _ = ref.shape
    turned = values.T
    for g in range(parts):
        ref[g ^ me] = turned[g * depth : (g + 1) * depth]


def pair_mask():
    rows = lax.broadcasted_iota(jnp.int32, (TILE, 2 * TILE), 0)
    keys = lax.broadcasted_iota(jnp.int32, (TILE, 2 * TILE), 1) & (TILE - 1)
    return (rows // POS == keys // POS) & (keys <= rows)


def two_heads(values):
    first = lax.broadcasted_iota(jnp.int32, values.shape, 1) < HD
    zero = jnp.zeros_like(values)
    return jnp.concatenate(
        [jnp.where(first, values, zero), jnp.where(first, zero, values)], axis=0
    )


def one_pair(values):
    first = lax.broadcasted_iota(jnp.int32, (TILE, LANES), 1) < HD
    return jnp.where(first, values[:TILE], values[TILE:])


def per_head(op, values):
    both = [
        jnp.broadcast_to(op(values[:, s : s + TILE], axis=1, keepdims=True), (TILE, TILE))
        for s in (0, TILE)
    ]
    return jnp.concatenate(both, axis=1)


def probs_of(queries, keys, mask):
    scores = jnp.where(mask, nt(queries, keys) * SCALE, -1e30)
    powers = jnp.exp(scores - per_head(jnp.max, scores))
    return powers / per_head(jnp.sum, powers)


def pairs_of(rows, width):
    return [
        (pl.ds(t * TILE, TILE), pl.ds(p * LANES, LANES))
        for t in range(rows // TILE)
        for p in range(width // LANES)
    ]


def wide(lanes):
    return pl.ds(lanes.start // LANES * 2 * TILE, 2 * TILE)


def attention_body(
    x_ref, gain_ref, wq_ref, wk_ref, wv_ref, wo_ref, q_ref, k_ref, v_ref, m_ref, p_ref, part_ref
):
    normed = normed_of(x_ref, gain_ref)
    q_ref[...] = nn(normed, wq_ref[...]).astype(bf16)
    k_ref[...] = nn(normed, wk_ref[...]).astype(bf16)
    v_ref[...] = nn(normed, wv_ref[...]).astype(bf16)
    mask = pair_mask()
    for at in pairs_of(*q_ref.shape):
        probs = probs_of(q_ref[at], two_heads(k_ref[at]), mask).astype(bf16)
        p_ref[at[0], wide(at[1])] = probs
        m_ref[at] = nn(probs, two_heads(v_ref[at])).astype(bf16)
    part_ref[...] = nn(m_ref[...], wo_ref[...]).astype(bf16)


def attention(x, gain, wq, wk, wv, wo):
    rows, width = x.shape
    heads = wq.shape[1]
    block = 512
    outs = [(rows_of(block, heads), (rows, heads), bf16)] * 4
    spread = 2 * TILE * heads // LANES
    outs += [(rows_of(block, spread), (rows, spread), bf16)]
    outs += [(rows_of(block, width), (rows, width), bf16, ANYWHERE)]
    return call(
        attention_body,
        "attention_forward",
        (rows // block,),
        [rows_of(block, width), whole(width)]
        + [whole(width, heads)] * 3
        + [whole(heads, width)],
        outs,
        vmem=58,
        cost=(8 * rows * width * heads, 12 * MIB),
        far=(0, 2, 3, 4, 5),
    )(x, gain, wq, wk, wv, wo)


def seed_body(lengths_ref, me_ref, cot_ref, x_ref, gain_ref, seed_ref, turned_ref, normed_ref):
    block = cot_ref.shape[0]
    first = pl.program_id(0) * block
    length = lengths_ref[first // (SLOT * POS)]
    row = lax.broadcasted_iota(jnp.int32, cot_ref.shape, 0) + first % (SLOT * POS)
    cot = cot_ref[...].astype(f32)
    seed = jnp.where(row // POS < length, cot, 0.0).astype(bf16)
    seed_ref[...] = seed
    put_transposed(turned_ref, me_ref[0], seed)
    put_transposed(normed_ref, me_ref[0], normed_of(x_ref, gain_ref))


def normed_of(x_ref, gain_ref):
    values = x_ref[...].astype(f32)
    return (values * inverse_rms(values) * row_of(gain_ref)).astype(bf16)


def turned_out(parts, depth, rows, block):
    return (
        pl.BlockSpec((parts, depth, block), lambda i, *_: (0, 0, i)),
        (parts, depth, rows),
        bf16,
    )


def seeds(lengths, me, cot, x, gain, parts):
    rows, width = cot.shape
    block = 256
    turned = turned_out(parts, width // parts, rows, block)
    return call(
        seed_body,
        "seed_rows",
        (rows // block,),
        [rows_of(block, width)] * 2 + [whole(width)],
        [(rows_of(block, width), (rows, width), bf16, pltpu.VMEM), (*turned, pltpu.VMEM), turned],
        vmem=16,
        scalars=2,
        far=(0, 1),
        cost=(4 * rows * width, 6 * MIB),
    )(lengths, me, cot, x, gain)


def middle_body(me_ref, x_ref, own_ref, peer_ref, gain_ref, middle_ref, normed_ref, turned_ref):
    middle = x_ref[...].astype(f32) + (own_ref[...].astype(f32) + peer_ref[...].astype(f32))
    middle_ref[...] = middle
    normed = (middle * inverse_rms(middle) * row_of(gain_ref)).astype(bf16)
    normed_ref[...] = normed
    put_transposed(turned_ref, me_ref[0], normed)


def middles(me, x, own, peer, gain, parts):
    rows, width = x.shape
    block = 256
    return call(
        middle_body,
        "middle_rows",
        (rows // block,),
        [rows_of(block, width)] * 3 + [whole(width)],
        [
            (rows_of(block, width), (rows, width), f32),
            (rows_of(block, width), (rows, width), bf16, pltpu.VMEM),
            (*turned_out(parts, width // parts, rows, block), pltpu.VMEM),
        ],
        vmem=24,
        scalars=1,
        cost=(8 * rows * width, 14 * MIB),
    )(me, x, own, peer, gain)


def places(parts, bits):
    count = len(bits)
    return [
        sum(bit for n, bit in enumerate(bits) if place >> (count - 1 - n) & 1)
        for place in range(parts)
    ]


def put_pieces(keep_ref, send_ref, column, values, order, first):
    half, _, depth, _ = keep_ref.shape
    low = values.astype(bf16)
    for n in range(values.shape[0] // depth):
        place = order.index(first + n)
        ref, at = (keep_ref, place) if place < half else (send_ref, place - half)
        for c in range(values.shape[1] // LANES):
            ref[at, column + c] = low[
                n * depth : (n + 1) * depth, c * LANES : (c + 1) * LANES
            ]


def product_pieces(keep_ref, send_ref, column, turned_ref, right, order):
    parts, depth, rows = turned_ref.shape
    group = max(1, 256 // depth)
    for first in range(0, parts, group):
        left = turned_ref[pl.ds(first, group)].reshape(group * depth, rows)
        put_pieces(keep_ref, send_ref, column, nn(left, right), order, first)


def resident():
    return pl.BlockSpec(memory_space=pltpu.VMEM)


def hidden_body(order, first, block, first_call, *refs):
    (n_ref, nt_ref, s_ref, st_ref, wg_ref, wu_ref, wd_ref) = refs[:7]
    h_ref, gg_ref, gu_ref, keep_ref, send_ref = refs[7 if first_call else 10 :]
    rows = n_ref.shape[0]
    step = min(256, rows)
    here = pl.ds(pl.multiple_of(first + pl.program_id(0) * block, block), block)
    for r in range(0, rows, step):
        at = pl.ds(r, step)
        gate = nn(n_ref[at], wg_ref[:, here])
        up = nn(n_ref[at], wu_ref[:, here])
        back = nt(s_ref[at], wd_ref[here])
        sig = 1.0 / (1.0 + jnp.exp(-gate))
        silu = gate * sig
        h_ref[at, here] = (silu * up).astype(bf16)
        gg_ref[at, here] = (back * up * (sig * (1.0 + gate * (1.0 - sig)))).astype(bf16)
        gu_ref[at, here] = (back * silu).astype(bf16)
    columns = block // LANES
    product_pieces(keep_ref, send_ref, 0, nt_ref, gg_ref[:, here], order)
    product_pieces(keep_ref, send_ref, columns, nt_ref, gu_ref[:, here], order)
    product_pieces(keep_ref, send_ref, 2 * columns, st_ref, h_ref[:, here], order)


def hidden_chunk(first, steps, block, order, normed, normed_t, seed, seed_t, wg, wu, wd, earlier):
    rows, width = normed.shape
    parts, depth, _ = normed_t.shape
    hidden = wg.shape[1]
    groups = 3 * block // LANES
    pieces = (
        pl.BlockSpec((parts // 2, groups, depth, LANES), lambda j: (0, j, 0, 0)),
        (parts // 2, steps * groups, depth, LANES),
        bf16,
    )
    args = [normed, normed_t, seed, seed_t, wg, wu, wd]
    aliases = {}
    if earlier is not None:
        aliases = {7: 0, 8: 1, 9: 2}
        args += list(earlier)
    return call(
        functools.partial(hidden_body, order, first, block, earlier is None),
        "hidden_units",
        (steps,),
        [resident()] * len(args),
        [(resident(), (rows, hidden), bf16, pltpu.VMEM)] * 3 + [pieces, (*pieces, ANYWHERE)],
        vmem=20,
        aliases=aliases,
        cost=(12 * rows * width * block * steps, 20 * MIB),
    )(*args)


def back_body(first, gg_ref, gu_ref, wg_ref, wu_ref, part_ref):
    here = pl.ds(first, part_ref.shape[0])
    part_ref[...] = (
        nt(gg_ref[here], wg_ref[...]) + nt(gu_ref[here], wu_ref[...])
    ).astype(bf16)


def normed_two_back(half, gg, gu, wg, wu):
    rows, hidden = gg.shape
    rows //= HALVES
    width = wg.shape[0]
    block = 256
    weights = pl.BlockSpec((block, hidden), lambda j: (j, 0))
    return call(
        functools.partial(back_body, half * rows),
        "normed_two_back",
        (width // block,),
        [resident()] * 2 + [weights] * 2,
        [(pl.BlockSpec((rows, block), lambda j: (0, j)), (rows, width), bf16, ANYWHERE)],
        vmem=20,
        cost=(4 * rows * width * hidden, 14 * MIB),
    )(gg, gu, wg, wu)[0]


def down_body(h_ref, wd_ref, part_ref):
    part_ref[...] = nn(h_ref[...], wd_ref[...]).astype(bf16)


def hidden_down(hidden, wd):
    rows, units = hidden.shape
    width = wd.shape[1]
    block = 256
    return call(
        down_body,
        "hidden_down",
        (width // block,),
        [resident(), pl.BlockSpec((units, block), lambda j: (0, j))],
        [(pl.BlockSpec((rows, block), lambda j: (0, j)), (rows, width), bf16, ANYWHERE)],
        vmem=20,
        cost=(2 * rows * width * units, 10 * MIB),
    )(hidden, wd)[0]


def add_up(ref, part):
    @pl.when(pl.program_id(0) == 0)
    def _():
        ref[...] = part

    @pl.when(pl.program_id(0) > 0)
    def _():
        ref[...] += part


def middle_back_body(me_ref, mid_ref, own_ref, peer_ref, seed_ref, gain_ref, wo_ref, *refs):
    turned_ref, mixed_ref, grad_ref, sum_ref = refs[-4:]
    upstream = own_ref[...].astype(f32) + peer_ref[...].astype(f32)
    middle = mid_ref[...]
    inverse = inverse_rms(middle)
    scaled = middle * inverse
    add_up(sum_ref, jnp.sum(upstream * scaled, axis=0, keepdims=True))
    weighted = upstream * row_of(gain_ref)
    grad_middle = seed_ref[...].astype(f32) + inverse * (
        weighted - scaled * jnp.mean(weighted * scaled, axis=1, keepdims=True)
    )
    grad_ref[...] = grad_middle
    low = grad_middle.astype(bf16)
    mixed_ref[...] = nt(low, wo_ref[...]).astype(bf16)
    put_transposed(turned_ref, me_ref[0], low)


def middle_back(half, me, middle, own, peer, seed, gain, wo, parts, earlier):
    rows, width = middle.shape
    heads = wo.shape[0]
    share = rows // HALVES
    block = 256
    steps = share // block
    depth = width // parts
    there = lambda n: pl.BlockSpec((block, n), lambda i, *_: (half * steps + i, 0))
    ins = [there(width)] + [rows_of(block, width)] * 2 + [there(width)]
    ins += [whole(width), whole(heads, width)]
    args = [me, middle, own, peer, seed, gain, wo]
    aliases = {}
    if earlier is not None:
        ins += [pl.BlockSpec(memory_space=pl.ANY)] * 2
        aliases = {len(args) + n: n for n in range(2)}
        args += list(earlier)
    return call(
        middle_back_body,
        "middle_backward",
        (steps,),
        ins,
        [
            (
                pl.BlockSpec((parts, depth, block), lambda i, *_: (0, 0, half * steps + i)),
                (parts, depth, rows),
                bf16,
            ),
            (there(heads), (rows, heads), bf16),
            (rows_of(block, width), (share, width), f32),
            (whole(1, width), (1, width), f32),
        ],
        vmem=24,
        scalars=1,
        aliases=aliases,
        cost=(2 * share * width * heads, 9 * MIB),
    )(*args)


def attention_back_body(q_ref, k_ref, v_ref, p_ref, mixed_ref, wq_ref, wk_ref, wv_ref, *refs):
    gqkv_ref, part_ref = refs[-2:]
    heads = q_ref.shape[1]
    for at in pairs_of(*q_ref.shape):
        rows, lanes = at
        queries, grads = q_ref[at], mixed_ref[at]
        keys, values = two_heads(k_ref[at]), two_heads(v_ref[at])
        low = p_ref[rows, wide(lanes)]
        probs = low.astype(f32)
        grad_probs = nt(grads, values)
        grad_values = one_pair(tn(low, grads))
        inner = per_head(jnp.sum, grad_probs * probs)
        grad_scores = (probs * (grad_probs - inner)).astype(bf16)
        grad_queries = nn(grad_scores, keys) * SCALE
        grad_keys = one_pair(tn(grad_scores, queries)) * SCALE
        for n, grad in enumerate((grad_queries, grad_keys, grad_values)):
            gqkv_ref[rows, pl.ds(n * heads + lanes.start, LANES)] = grad.astype(bf16)
    part = nt(gqkv_ref[:, :heads], wq_ref[...])
    part += nt(gqkv_ref[:, heads : 2 * heads], wk_ref[...])
    part += nt(gqkv_ref[:, 2 * heads :], wv_ref[...])
    part_ref[...] = part.astype(bf16)


def attention_back(half, q, k, v, probs, grad_mixed, wq, wk, wv, earlier):
    rows, heads = q.shape
    width = wq.shape[0]
    share = rows // HALVES
    block = 256
    steps = share // block
    there = lambda n: pl.BlockSpec((block, n), lambda i: (half * steps + i, 0))
    ins = [there(heads)] * 3 + [there(probs.shape[1]), there(heads)] + [whole(width, heads)] * 3
    args = [q, k, v, probs, grad_mixed, wq, wk, wv]
    aliases = {}
    if earlier is not None:
        ins.append(pl.BlockSpec(memory_space=pl.ANY))
        aliases = {len(args): 0}
        args.append(earlier)
    return call(
        attention_back_body,
        "attention_backward",
        (steps,),
        ins,
        [
            (there(3 * heads), (rows, 3 * heads), bf16, ANYWHERE),
            (rows_of(block, width), (share, width), bf16, ANYWHERE),
        ],
        vmem=32,
        aliases=aliases,
        cost=(6 * share * width * heads, 9 * MIB),
    )(*args)


def pieces_body(order, turned_ref, right_ref, *refs):
    keep_ref, send_ref = refs[-2:]
    groups = right_ref.shape[1] // LANES
    product_pieces(keep_ref, send_ref, 0, turned_ref, right_ref[...], order)
    if len(refs) == 2:
        return
    me_ref, gain_ref = refs[:2]
    row = lax.broadcasted_iota(jnp.int32, (LANES, gain_ref.shape[1]), 0)
    turned = jnp.where(row == 0, gain_ref[...], 0.0).T.astype(bf16)
    half, _, depth, _ = keep_ref.shape
    bits = [order[1 << n] for n in reversed(range((2 * half).bit_length() - 1))]
    for g in range(2 * half):
        relative = g ^ me_ref[0]
        place = 0
        for bit in bits:
            place = 2 * place + (relative & bit != 0).astype(jnp.int32)
        piece = turned[g * depth : (g + 1) * depth]

        @pl.when(place < half)
        def _():
            keep_ref[jnp.minimum(place, half - 1), groups] = piece

        @pl.when(place >= half)
        def _():
            send_ref[jnp.maximum(place - half, 0), groups] = piece


def pieces_of(order, turned, right, column, heads, *gain):
    parts, depth, rows = turned.shape
    groups = heads // LANES + bool(gain)
    shape = (parts // 2, groups, depth, LANES)
    ins = [
        whole(parts, depth, rows),
        pl.BlockSpec((rows, heads), lambda j: (0, column)),
    ]
    if gain:
        ins += [pl.BlockSpec(memory_space=pltpu.SMEM), whole(1, parts * depth)]
    return call(
        functools.partial(pieces_body, order),
        "head_grads",
        (1,),
        ins,
        [(whole(*shape), shape, bf16), (whole(*shape), shape, bf16, ANYWHERE)],
        vmem=24,
        cost=(2 * rows * parts * depth * heads, 5 * MIB),
    )(turned, right, *gain)


def input_grad_body(x_ref, gm_ref, own_ref, peer_ref, gain_ref, *refs):
    out_ref, sum_ref = refs[-2:]
    inputs = x_ref[...].astype(f32)
    inverse = inverse_rms(inputs)
    scaled = inputs * inverse
    upstream = own_ref[...].astype(f32) + peer_ref[...].astype(f32)
    add_up(sum_ref, jnp.sum(upstream * scaled, axis=0, keepdims=True))
    weighted = upstream * row_of(gain_ref)
    out_ref[...] = (
        gm_ref[...]
        + inverse * (weighted - scaled * jnp.mean(weighted * scaled, axis=1, keepdims=True))
    ).astype(bf16)


def input_grad(half, x, grad_middle, own, peer, gain, earlier):
    rows, width = x.shape
    share = rows // HALVES
    block = 256
    steps = share // block
    there = pl.BlockSpec((block, width), lambda i: (half * steps + i, 0))
    ins = [there] + [rows_of(block, width)] * 3 + [whole(width)]
    args = [x, grad_middle, own, peer, gain]
    aliases = {}
    if earlier is not None:
        ins.append(pl.BlockSpec(memory_space=pl.ANY))
        args.append(earlier)
        aliases = {5: 0}
    return call(
        input_grad_body,
        "input_grad",
        (steps,),
        ins,
        [(there, (rows, width), bf16), (whole(1, width), (1, width), f32)],
        vmem=24,
        aliases=aliases,
        cost=(10 * share * width, 6 * MIB),
    )(*args)


def total_of(refs):
    total = refs[0][0].astype(f32)
    for ref in refs[1:]:
        total += ref[0].astype(f32)
    return total


def last_hidden_body(count, first_call, *refs):
    total = total_of(refs[:count])
    gate_ref, up_ref, down_ref = refs[count if first_call else count + 3 :]
    third = total.shape[0] // 3
    for c in range(third):
        at = slice(c * LANES, (c + 1) * LANES)
        gate_ref[:, at] = total[c]
        up_ref[:, at] = total[third + c]
        down_ref[:, at] = total[2 * third + c]


def last_hidden(chunk, chunks, steps, arrays, hidden, earlier):
    _, groups, depth, _ = arrays[0].shape
    share = groups // steps
    block = share // 3 * LANES
    ins = [pl.BlockSpec((1, share, depth, LANES), lambda j: (0, j, 0, 0))] * len(arrays)
    args = list(arrays)
    aliases = {}
    if earlier is not None:
        ins += [pl.BlockSpec(memory_space=pl.ANY)] * 3
        aliases = {len(arrays) + n: n for n in range(3)}
        args += list(earlier)
    wide = (
        pl.BlockSpec((depth, block), lambda j: (0, chunk * steps + j)),
        (depth, hidden),
        f32,
    )
    return call(
        functools.partial(last_hidden_body, len(arrays), earlier is None),
        "hidden_grads_out",
        (steps,),
        ins,
        [wide] * 3,
        vmem=16,
        aliases=aliases,
        cost=(6 * groups * depth * LANES, MIB),
    )(*args)


def last_head_body(count, *refs):
    total = total_of(refs[:count])
    grad_ref = refs[count]
    groups = grad_ref.shape[1] // LANES
    for c in range(groups):
        grad_ref[:, c * LANES : (c + 1) * LANES] = total[c]
    if len(refs) > count + 1:
        refs[count + 1][...] = total[groups].T


def last_head(arrays, heads, gain=False):
    _, groups, depth, _ = arrays[0].shape
    shapes = [(depth, heads)]
    if gain:
        shapes.append((LANES, depth))
    return call(
        functools.partial(last_head_body, len(arrays)),
        "head_grads_out",
        (1,),
        [pl.BlockSpec((1, groups, depth, LANES), lambda j: (0, 0, 0, 0))] * len(arrays),
        [(whole(*shape), shape, f32) for shape in shapes],
        vmem=16,
        cost=(6 * groups * depth * LANES, MIB),
    )(*arrays)


def block_output_body(mid_ref, own_ref, peer_ref, out_ref):
    out_ref[...] = (
        mid_ref[...] + (own_ref[...].astype(f32) + peer_ref[...].astype(f32))
    ).astype(bf16)


def block_outputs(middle, own, peer):
    rows, width = middle.shape
    block = 256
    return call(
        block_output_body,
        "block_output",
        (rows // block,),
        [rows_of(block, width)] * 3,
        [(rows_of(block, width), (rows, width), bf16)],
        vmem=16,
        cost=(3 * rows * width, 10 * MIB),
    )(middle, own, peer)[0]


def swap(array, axis, size, bit):
    return lax.ppermute(array, axis, [(i, i ^ bit) for i in range(size)])


def both_shares(partial, size):
    bit = 1
    while 2 * bit < size:
        other = swap(partial, "tensor", size, bit)
        partial = (partial.astype(f32) + other.astype(f32)).astype(bf16)
        bit *= 2
    return partial, swap(partial, "tensor", size, bit)


def after(value, *others):
    return lax.optimization_barrier((value, *others))[0]


def next_send_body(*refs):
    total = refs[0][...].astype(f32)
    for ref in refs[1:-1]:
        total += ref[...].astype(f32)
    refs[-1][...] = total.astype(bf16)


def next_send(half, arrays):
    _, *rest = arrays[0].shape
    block = max(1, half // 2)
    steps = half // block
    return call(
        next_send_body,
        "next_send",
        (steps,),
        [pl.BlockSpec((block, *rest), lambda i: (steps + i, 0, 0, 0))] * len(arrays),
        [(pl.BlockSpec((block, *rest), lambda i: (i, 0, 0, 0)), (half, *rest), bf16, ANYWHERE)],
        vmem=16,
        cost=(half * math.prod(rest), MIB),
    )(*arrays)[0]


class Line:
    def __init__(self):
        self.last = None

    def __call__(self, kernel, first, *rest, head=()):
        if self.last is not None:
            first = after(first, self.last)
        out = kernel(*head, first, *rest)
        self.last = jax.tree.leaves(out)[-1]
        return out


class Halving:
    def __init__(self, line, pieces, size, bits):
        self.line, self.size, self.bits = line, size, list(bits)
        self.arrays = [pieces[0]]
        self.half = size // 2
        self.launch(pieces[1])

    def launch(self, send):
        self.coming = swap(send, "dp", self.size, self.bits.pop(0))

    def hop(self):
        self.arrays.append(self.coming)
        self.half //= 2
        self.launch(
            self.line(
                lambda newest: next_send(self.half, [*self.arrays[:-1], newest]), self.arrays[-1]
            )
        )

    def end(self):
        while self.bits:
            self.hop()
        return [*self.arrays, self.coming]


def body_of(dp, tensor):
    n_bits = dp.bit_length() - 1
    all_bits = [1 << k for k in range(n_bits)]

    def order(*start):
        return [1 << k for k in start] + [b for b in all_bits if b.bit_length() - 1 not in start]

    bits_of = {
        0: order(0, 1),
        1: order(1, 0),
        2: order(2, 3),
        3: order(0, 1),
        "out": order(1, 0),
        "query": order(0, 1),
        "key": order(1, 0),
        "value": order(0, 1),
    }

    def body(
        block_input,
        w_query,
        w_key,
        w_value,
        w_out,
        w_gate,
        w_up,
        w_down,
        gain_attn,
        gain_ffn,
        item_lengths,
        cotangent,
    ):
        rows, width = block_input.shape
        heads = w_query.shape[1]
        hidden_units = w_gate.shape[1]
        depth = width // dp
        chunks = 4
        share = hidden_units // chunks
        block = min(256, share)
        line = Line()
        me = lax.axis_index("dp").astype(jnp.int32).reshape(1)
        gain_one, gain_two = gain_attn, gain_ffn

        def summing(name, pieces):
            return Halving(line, pieces, dp, bits_of[name])

        q, k, v, mixed, probs, part = line(
            attention, block_input, gain_one, w_query, w_key, w_value, w_out
        )
        own, peer = both_shares(part, tensor)
        seed, seed_t, normed_t = line(
            seeds, cotangent, block_input, gain_one, dp, head=(item_lengths, me)
        )
        middle, normed_two, normed_two_t = line(
            middles, peer, gain_two, dp, head=(me, block_input, own)
        )
        acts = None
        sums = {}
        for c in range(chunks):
            out = line(
                hidden_chunk,
                normed_two,
                normed_two_t,
                seed,
                seed_t,
                w_gate,
                w_up,
                w_down,
                acts,
                head=(c * share, share // block, block, places(dp, bits_of[c])),
            )
            acts = out[:3]
            sums[c] = summing(c, out[3:])
        hidden, grad_gate_pre, grad_up_pre = acts
        shares = []
        for h in range(HALVES):
            shares.append(
                both_shares(
                    line(normed_two_back, grad_gate_pre, grad_up_pre, w_gate, w_up, head=(h,)),
                    tensor,
                )
            )
            if h == 0:
                sums[0].hop()
        sums[1].hop()
        down = line(hidden_down, hidden, w_down)
        gain_two_sum, middle_grads, saved = 0.0, [], None
        for h, (own, peer) in enumerate(shares):
            out = line(
                middle_back, peer, seed, gain_two, w_out, dp, saved, head=(h, me, middle, own)
            )
            saved = out[:2]
            middle_grads.append(out[2])
            gain_two_sum += out[3]
        middle_t, grad_mixed = saved
        sums["out"] = summing(
            "out",
            line(
                pieces_of,
                middle_t,
                mixed,
                0,
                heads,
                me,
                gain_two_sum,
                head=(places(dp, bits_of["out"]),),
            ),
        )
        gqkv, backs = None, []
        for h in range(HALVES):
            gqkv, part = line(
                attention_back, grad_mixed, w_query, w_key, w_value, gqkv, head=(h, q, k, v, probs)
            )
            backs.append(both_shares(part, tensor))
            if h == 0:
                sums[2].hop()
                sums[0].hop()
        down_own, down_peer = both_shares(after(down, gqkv), tensor)
        for n, name in enumerate(("query", "key")):
            sums[name] = summing(
                name,
                line(pieces_of, normed_t, gqkv, n, heads, head=(places(dp, bits_of[name]),)),
            )
        gain_one_sum, grad_input = 0.0, None
        for h, (own, peer) in enumerate(backs):
            grad_input, part = line(
                input_grad,
                peer,
                gain_one,
                grad_input,
                head=(h, block_input, middle_grads[h], own),
            )
            gain_one_sum += part
        sums["value"] = summing(
            "value",
            line(
                pieces_of,
                normed_t,
                gqkv,
                2,
                heads,
                me,
                gain_one_sum,
                head=(places(dp, bits_of["value"]),),
            ),
        )
        for name in (3, 1, 2, 0, "out"):
            sums[name].hop()
        block_output = line(block_outputs, down_peer, head=(middle, down_own))
        for name in ("query", 3, 1, "key", 2, "out", "value", 3, "out", "query", "key", "value", "query", "key", "value"):
            if sums[name].bits:
                sums[name].hop()
        grads = None
        for c in range(chunks):
            grads = last_hidden(c, chunks, share // block, sums[c].end(), hidden_units, grads)
        grad_out, gains_two = last_head(sums["out"].end(), heads, True)
        (grad_query,) = last_head(sums["query"].end(), heads)
        (grad_key,) = last_head(sums["key"].end(), heads)
        grad_value, gains_one = last_head(sums["value"].end(), heads, True)
        return (
            block_output,
            grad_input,
            grad_query,
            grad_key,
            grad_value,
            grad_out.T,
            grads[0],
            grads[1],
            grads[2].T,
            gains_one[0],
            gains_two[0],
        )

    return body


def solution(mesh):
    placed = (
        P("dp", None),
        P(None, "tensor"),
        P(None, "tensor"),
        P(None, "tensor"),
        P("tensor", None),
        P(None, "tensor"),
        P(None, "tensor"),
        P("tensor", None),
        P(),
        P(),
        P("dp"),
        P("dp", None),
    )
    return jax.shard_map(
        body_of(mesh.shape["dp"], mesh.shape["tensor"]),
        mesh=mesh,
        in_specs=placed,
        out_specs=(
            P("dp", None),
            P("dp", None),
            P("dp", "tensor"),
            P("dp", "tensor"),
            P("dp", "tensor"),
            P("tensor", "dp"),
            P("dp", "tensor"),
            P("dp", "tensor"),
            P("tensor", "dp"),
            P("dp"),
            P("dp"),
        ),
        check_vma=False,
    )
```

```python
import functools
import math

import jax
import jax.numpy as jnp
from jax import lax
from jax.experimental import pallas as pl
from jax.experimental.pallas import tpu as pltpu
from jax.sharding import PartitionSpec as P

HD = 64
POS = 16
SLOT = 32
LANES = 128
TILE = 128
MIB = 1 << 20
HALVES = 2
PARTS = 2
COST = 1e-6

epsilon = 1e-05
f32 = jnp.float32
bf16 = jnp.bfloat16
SCALE = 1.0 / math.sqrt(HD)
ANYWHERE = jax.ShapeDtypeStruct


def nn(left, right):
    return lax.dot_general(left, right, (((1,), (0,)), ((), ())), preferred_element_type=f32)


def nt(left, right):
    return lax.dot_general(left, right, (((1,), (1,)), ((), ())), preferred_element_type=f32)


def tn(left, right):
    return lax.dot_general(left, right, (((0,), (0,)), ((), ())), preferred_element_type=f32)


def call(body, name, grid, ins, outs, scratch=(), vmem=40, scalars=0, aliases=None, cost=None, far=()):
    kernel = pl.pallas_call(
        body,
        grid_spec=pltpu.PrefetchScalarGridSpec(
            num_scalar_prefetch=scalars,
            grid=grid,
            in_specs=ins,
            out_specs=[spec for spec, *_ in outs],
            scratch_shapes=scratch,
        ),
        out_shape=[
            (where[0] if where else pltpu.HBM)(shape, dtype) for _, shape, dtype, *where in outs
        ],
        input_output_aliases=aliases or {},
        compiler_params=pltpu.CompilerParams(vmem_limit_bytes=vmem * MIB),
        cost_estimate=pl.CostEstimate(
            flops=int(cost[0] * COST), bytes_accessed=int(cost[1] * COST), transcendentals=0
        ),
        name=name,
    )

    def run(*args):
        return kernel(
            *(
                pltpu.with_memory_space_constraint(arg, pltpu.HBM) if n - scalars in far else arg
                for n, arg in enumerate(args)
            )
        )

    return run


def rows_of(block, width):
    return pl.BlockSpec((block, width), lambda i, *_: (i, 0))


def whole(*shape):
    return pl.BlockSpec(shape, lambda *_: (0,) * len(shape))


def row_of(gain_ref):
    return gain_ref[...].astype(f32).reshape(1, -1)


def inverse_rms(values):
    return lax.rsqrt(jnp.mean(values * values, axis=1, keepdims=True) + epsilon)


def exchanged(index, size):
    if size < 4:
        return index
    return index // 4 * 4 + index % 2 * 2 + index // 2 % 2


def relative(place_ref, g, size):
    apart = g ^ place_ref[0]
    if size < 4:
        return apart
    other = (apart & ~3) | ((apart & 1) << 1) | ((apart >> 1) & 1)
    return jnp.where(place_ref[1] == 1, other, apart)


def put_transposed(ref, place_ref, values):
    parts, depth, _ = ref.shape
    turned = values.T
    for g in range(parts):
        ref[relative(place_ref, g, parts)] = turned[g * depth : (g + 1) * depth]


def pair_mask():
    rows = lax.broadcasted_iota(jnp.int32, (TILE, 2 * TILE), 0)
    keys = lax.broadcasted_iota(jnp.int32, (TILE, 2 * TILE), 1) & (TILE - 1)
    return (rows // POS == keys // POS) & (keys <= rows)


def two_heads(values):
    first = lax.broadcasted_iota(jnp.int32, values.shape, 1) < HD
    zero = jnp.zeros_like(values)
    return jnp.concatenate(
        [jnp.where(first, values, zero), jnp.where(first, zero, values)], axis=0
    )


def one_pair(values):
    first = lax.broadcasted_iota(jnp.int32, (TILE, LANES), 1) < HD
    return jnp.where(first, values[:TILE], values[TILE:])


def per_head(op, values):
    both = [
        jnp.broadcast_to(op(values[:, s : s + TILE], axis=1, keepdims=True), (TILE, TILE))
        for s in (0, TILE)
    ]
    return jnp.concatenate(both, axis=1)


def probs_of(queries, keys, mask):
    scores = jnp.where(mask, nt(queries, keys) * SCALE, -1e30)
    powers = jnp.exp(scores - per_head(jnp.max, scores))
    return powers / per_head(jnp.sum, powers)


def pairs_of(rows, width):
    return [
        (pl.ds(t * TILE, TILE), pl.ds(p * LANES, LANES))
        for t in range(rows // TILE)
        for p in range(width // LANES)
    ]


def wide(lanes):
    return pl.ds(lanes.start // LANES * 2 * TILE, 2 * TILE)


def attention_body(
    x_ref, gain_ref, wq_ref, wk_ref, wv_ref, wo_ref, q_ref, k_ref, v_ref, m_ref, p_ref, part_ref
):
    normed = normed_of(x_ref, gain_ref)
    q_ref[...] = nn(normed, wq_ref[...]).astype(bf16)
    k_ref[...] = nn(normed, wk_ref[...]).astype(bf16)
    v_ref[...] = nn(normed, wv_ref[...]).astype(bf16)
    mask = pair_mask()
    for at in pairs_of(*q_ref.shape):
        probs = probs_of(q_ref[at], two_heads(k_ref[at]), mask).astype(bf16)
        p_ref[at[0], wide(at[1])] = probs
        m_ref[at] = nn(probs, two_heads(v_ref[at])).astype(bf16)
    part_ref[...] = nn(m_ref[...], wo_ref[...]).astype(bf16)


def attention(x, gain, wq, wk, wv, wo):
    rows, width = x.shape
    heads = wq.shape[1]
    block = 256
    outs = [(rows_of(block, heads), (rows, heads), bf16)] * 4
    spread = 2 * TILE * heads // LANES
    outs += [(rows_of(block, spread), (rows, spread), bf16)]
    outs += [(rows_of(block, width), (rows, width), bf16, ANYWHERE)]
    return call(
        attention_body,
        "attention_forward",
        (rows // block,),
        [rows_of(block, width), whole(width)]
        + [whole(width, heads)] * 3
        + [whole(heads, width)],
        outs,
        vmem=24,
        cost=(8 * rows * width * heads, 12 * MIB),
        far=(0, 2, 3, 4, 5),
    )(x, gain, wq, wk, wv, wo)


def seed_body(lengths_ref, me_ref, cot_ref, x_ref, gain_ref, seed_ref, turned_ref, normed_ref):
    block = cot_ref.shape[0]
    first = pl.program_id(0) * block
    length = lengths_ref[first // (SLOT * POS)]
    row = lax.broadcasted_iota(jnp.int32, cot_ref.shape, 0) + first % (SLOT * POS)
    cot = cot_ref[...].astype(f32)
    seed = jnp.where(row // POS < length, cot, 0.0).astype(bf16)
    seed_ref[...] = seed
    put_transposed(turned_ref, me_ref, seed)
    put_transposed(normed_ref, me_ref, normed_of(x_ref, gain_ref))


def normed_of(x_ref, gain_ref):
    values = x_ref[...].astype(f32)
    return (values * inverse_rms(values) * row_of(gain_ref)).astype(bf16)


def turned_out(parts, depth, rows, block):
    return (
        pl.BlockSpec((parts, depth, block), lambda i, *_: (0, 0, i)),
        (parts, depth, rows),
        bf16,
    )


def seeds(lengths, me, cot, x, gain, parts):
    rows, width = cot.shape
    block = 256
    turned = turned_out(parts, width // parts, rows, block)
    return call(
        seed_body,
        "seed_rows",
        (rows // block,),
        [rows_of(block, width)] * 2 + [whole(width)],
        [(rows_of(block, width), (rows, width), bf16, pltpu.VMEM), (*turned, pltpu.VMEM), turned],
        vmem=16,
        scalars=2,
        far=(0, 1),
        cost=(4 * rows * width, 6 * MIB),
    )(lengths, me, cot, x, gain)


def middle_body(me_ref, x_ref, own_ref, peer_ref, gain_ref, middle_ref, normed_ref, turned_ref):
    middle = x_ref[...].astype(f32) + (own_ref[...].astype(f32) + peer_ref[...].astype(f32))
    middle_ref[...] = middle.astype(bf16)
    normed = (middle * inverse_rms(middle) * row_of(gain_ref)).astype(bf16)
    normed_ref[...] = normed
    put_transposed(turned_ref, me_ref, normed)


def middles(me, x, own, peer, gain, parts):
    rows, width = x.shape
    block = 256
    return call(
        middle_body,
        "middle_rows",
        (rows // block,),
        [rows_of(block, width)] * 3 + [whole(width)],
        [
            (rows_of(block, width), (rows, width), bf16),
            (rows_of(block, width), (rows, width), bf16, pltpu.VMEM),
            (*turned_out(parts, width // parts, rows, block), pltpu.VMEM),
        ],
        vmem=24,
        scalars=1,
        cost=(8 * rows * width, 14 * MIB),
    )(me, x, own, peer, gain)


def places(parts, bits):
    count = len(bits)
    return [
        sum(bit for n, bit in enumerate(bits) if place >> (count - 1 - n) & 1)
        for place in range(parts)
    ]


def put_pieces(keep_ref, send_ref, column, values, order, first):
    half, _, depth, _ = keep_ref.shape
    low = values.astype(bf16)
    for n in range(values.shape[0] // depth):
        place = order.index(first + n)
        ref, at = (keep_ref, place) if place < half else (send_ref, place - half)
        for c in range(values.shape[1] // LANES):
            ref[at, column + c] = low[
                n * depth : (n + 1) * depth, c * LANES : (c + 1) * LANES
            ]


def product_pieces(keep_ref, send_ref, column, turned_ref, right, order):
    parts, depth, rows = turned_ref.shape
    group = max(1, 256 // depth)
    for first in range(0, parts, group):
        left = turned_ref[pl.ds(first, group)].reshape(group * depth, rows)
        put_pieces(keep_ref, send_ref, column, nn(left, right), order, first)


def resident():
    return pl.BlockSpec(memory_space=pltpu.VMEM)


def hidden_body(order, first, block, first_call, *refs):
    (n_ref, nt_ref, s_ref, st_ref, wg_ref, wu_ref, wd_ref) = refs[:7]
    h_ref, gg_ref, gu_ref, keep_ref, send_ref = refs[7 if first_call else 10 :]
    rows = n_ref.shape[0]
    step = min(256, rows)
    here = pl.ds(pl.multiple_of(first + pl.program_id(0) * block, block), block)
    for r in range(0, rows, step):
        at = pl.ds(r, step)
        gate = nn(n_ref[at], wg_ref[:, here])
        up = nn(n_ref[at], wu_ref[:, here])
        back = nt(s_ref[at], wd_ref[...])
        sig = 1.0 / (1.0 + jnp.exp(-gate))
        silu = gate * sig
        h_ref[at, here] = (silu * up).astype(bf16)
        gg_ref[at, here] = (back * up * (sig * (1.0 + gate * (1.0 - sig)))).astype(bf16)
        gu_ref[at, here] = (back * silu).astype(bf16)
    columns = block // LANES
    product_pieces(keep_ref, send_ref, 0, nt_ref, gg_ref[:, here], order)
    product_pieces(keep_ref, send_ref, columns, nt_ref, gu_ref[:, here], order)
    product_pieces(keep_ref, send_ref, 2 * columns, st_ref, h_ref[:, here], order)


def hidden_chunk(first, steps, block, order, normed, normed_t, seed, seed_t, wg, wu, wd, earlier):
    rows, width = normed.shape
    parts, depth, _ = normed_t.shape
    hidden = wg.shape[1]
    groups = 3 * block // LANES
    pieces = (
        pl.BlockSpec((parts // 2, groups, depth, LANES), lambda j: (0, j, 0, 0)),
        (parts // 2, steps * groups, depth, LANES),
        bf16,
    )
    args = [normed, normed_t, seed, seed_t, wg, wu, wd]
    ins = [resident()] * 6
    ins.append(pl.BlockSpec((block, width), lambda j: (first // block + j, 0)))
    aliases = {}
    if earlier is not None:
        aliases = {7: 0, 8: 1, 9: 2}
        args += list(earlier)
        ins += [resident()] * 3
    return call(
        functools.partial(hidden_body, order, first, block, earlier is None),
        "hidden_units",
        (steps,),
        ins,
        [(resident(), (rows, hidden), bf16, pltpu.VMEM)] * 3 + [pieces, (*pieces, ANYWHERE)],
        vmem=13,
        far=(6,),
        aliases=aliases,
        cost=(12 * rows * width * block * steps, 20 * MIB),
    )(*args)


def back_body(first, gg_ref, gu_ref, wg_ref, wu_ref, *part_refs):
    rows = part_refs[0].shape[0]
    here = pl.ds(first, rows * len(part_refs))
    part = nt(gg_ref[here], wg_ref[...]) + nt(gu_ref[here], wu_ref[...])
    for n, ref in enumerate(part_refs):
        ref[...] = part[n * rows : (n + 1) * rows].astype(bf16)


def normed_two_back(half, gg, gu, wg, wu):
    rows, hidden = gg.shape
    rows //= HALVES
    width = wg.shape[0]
    block = 256
    weights = pl.BlockSpec((block, hidden), lambda j: (j, 0))
    piece = rows // PARTS
    out = (pl.BlockSpec((piece, block), lambda j: (0, j)), (piece, width), bf16, ANYWHERE)
    return call(
        functools.partial(back_body, half * rows),
        "normed_two_back",
        (width // block,),
        [resident()] * 2 + [weights] * 2,
        [out] * PARTS,
        vmem=20,
        cost=(4 * rows * width * hidden, 14 * MIB),
    )(gg, gu, wg, wu)


def down_body(h_ref, wd_ref, *part_refs):
    part = nn(h_ref[...], wd_ref[...])
    rows = part_refs[0].shape[0]
    for n, ref in enumerate(part_refs):
        ref[...] = part[n * rows : (n + 1) * rows].astype(bf16)


def hidden_down(hidden, wd):
    rows, units = hidden.shape
    width = wd.shape[1]
    block = 256
    piece = rows // PARTS
    out = (pl.BlockSpec((piece, block), lambda j: (0, j)), (piece, width), bf16, ANYWHERE)
    return call(
        down_body,
        "hidden_down",
        (width // block,),
        [resident(), pl.BlockSpec((units, block), lambda j: (0, j))],
        [out] * PARTS,
        vmem=20,
        cost=(2 * rows * width * units, 10 * MIB),
    )(hidden, wd)


def add_up(ref, part):
    @pl.when(pl.program_id(0) == 0)
    def _():
        ref[...] = part

    @pl.when(pl.program_id(0) > 0)
    def _():
        ref[...] += part


def shares_sum(pairs, scratch_ref):
    for n in range(PARTS):

        @pl.when(pl.program_id(0) == n)
        def _():
            scratch_ref[...] = pairs[n][...].astype(f32) + pairs[PARTS + n][...].astype(f32)

    return scratch_ref[...]


def middle_back_body(me_ref, mid_ref, seed_ref, gain_ref, wo_ref, *refs):
    turned_ref, mixed_ref, grad_ref, sum_ref, scratch_ref = refs[-5:]
    upstream = shares_sum(refs, scratch_ref)
    middle = mid_ref[...].astype(f32)
    inverse = inverse_rms(middle)
    scaled = middle * inverse
    add_up(sum_ref, jnp.sum(upstream * scaled, axis=0, keepdims=True))
    weighted = upstream * row_of(gain_ref)
    grad_middle = seed_ref[...].astype(f32) + inverse * (
        weighted - scaled * jnp.mean(weighted * scaled, axis=1, keepdims=True)
    )
    low = grad_middle.astype(bf16)
    grad_ref[...] = low
    mixed_ref[...] = nt(low, wo_ref[...]).astype(bf16)
    put_transposed(turned_ref, me_ref, low)


def middle_back(half, me, middle, seed, gain, wo, parts, shares, earlier):
    rows, width = middle.shape
    heads = wo.shape[0]
    share = rows // HALVES
    block = share // PARTS
    depth = width // parts
    there = lambda n: pl.BlockSpec((block, n), lambda i, *_: (half * PARTS + i, 0))
    ins = [there(width)] * 2 + [whole(width), whole(heads, width)]
    ins += [whole(block, width)] * (2 * PARTS)
    args = [me, middle, seed, gain, wo, *shares]
    aliases = {}
    if earlier is not None:
        ins += [pl.BlockSpec(memory_space=pl.ANY)] * 2
        aliases = {len(args) + n: n for n in range(2)}
        args += list(earlier)
    return call(
        middle_back_body,
        "middle_backward",
        (PARTS,),
        ins,
        [
            (
                pl.BlockSpec((parts, depth, block), lambda i, *_: (0, 0, half * PARTS + i)),
                (parts, depth, rows),
                bf16,
            ),
            (there(heads), (rows, heads), bf16),
            (rows_of(block, width), (share, width), bf16),
            (whole(1, width), (1, width), f32),
        ],
        scratch=[pltpu.VMEM((block, width), f32)],
        vmem=24,
        scalars=1,
        aliases=aliases,
        cost=(2 * share * width * heads, 9 * MIB),
    )(*args)


def attention_back_body(q_ref, k_ref, v_ref, p_ref, mixed_ref, wq_ref, wk_ref, wv_ref, *refs):
    gqkv_ref, *part_refs = refs[-1 - PARTS :]
    heads = q_ref.shape[1]
    for at in pairs_of(*q_ref.shape):
        rows, lanes = at
        queries, grads = q_ref[at], mixed_ref[at]
        keys, values = two_heads(k_ref[at]), two_heads(v_ref[at])
        low = p_ref[rows, wide(lanes)]
        probs = low.astype(f32)
        grad_probs = nt(grads, values)
        grad_values = one_pair(tn(low, grads))
        inner = per_head(jnp.sum, grad_probs * probs)
        grad_scores = (probs * (grad_probs - inner)).astype(bf16)
        grad_queries = nn(grad_scores, keys) * SCALE
        grad_keys = one_pair(tn(grad_scores, queries)) * SCALE
        for n, grad in enumerate((grad_queries, grad_keys, grad_values)):
            gqkv_ref[rows, pl.ds(n * heads + lanes.start, LANES)] = grad.astype(bf16)
    part = nt(gqkv_ref[:, :heads], wq_ref[...])
    part += nt(gqkv_ref[:, heads : 2 * heads], wk_ref[...])
    part += nt(gqkv_ref[:, 2 * heads :], wv_ref[...])
    for n, ref in enumerate(part_refs):

        @pl.when(pl.program_id(0) == n)
        def _():
            ref[...] = part.astype(bf16)


def attention_back(half, q, k, v, probs, grad_mixed, wq, wk, wv, earlier):
    rows, heads = q.shape
    width = wq.shape[0]
    share = rows // HALVES
    block = share // PARTS
    there = lambda n: pl.BlockSpec((block, n), lambda i: (half * PARTS + i, 0))
    ins = [there(heads)] * 3 + [there(probs.shape[1]), there(heads)] + [whole(width, heads)] * 3
    args = [q, k, v, probs, grad_mixed, wq, wk, wv]
    aliases = {}
    if earlier is not None:
        ins.append(pl.BlockSpec(memory_space=pl.ANY))
        aliases = {len(args): 0}
        args.append(earlier)
    return call(
        attention_back_body,
        "attention_backward",
        (PARTS,),
        ins,
        [
            (there(3 * heads), (rows, 3 * heads), bf16, ANYWHERE),
            *[(whole(block, width), (block, width), bf16, ANYWHERE)] * PARTS,
        ],
        vmem=32,
        far=(4,),
        aliases=aliases,
        cost=(6 * share * width * heads, 9 * MIB),
    )(*args)


def query_key_body(order, turned_ref, right_ref, keep_ref, send_ref):
    product_pieces(keep_ref, send_ref, 0, turned_ref, right_ref[...], order)


def query_key_pieces(order, turned, right, heads):
    parts, depth, rows = turned.shape
    groups = heads // LANES
    pieces = (
        pl.BlockSpec((parts // 2, groups, depth, LANES), lambda j: (0, j, 0, 0)),
        (parts // 2, 2 * groups, depth, LANES),
        bf16,
    )
    return call(
        functools.partial(query_key_body, order),
        "query_key_grads",
        (2,),
        [whole(parts, depth, rows), pl.BlockSpec((rows, heads), lambda j: (0, j))],
        [pieces, (*pieces, ANYWHERE)],
        vmem=24,
        cost=(4 * rows * parts * depth * heads, 6 * MIB),
    )(turned, right)


def value_out_body(order, value_ref, right_ref, out_ref, mixed_ref, me_ref, *refs):
    *gain_refs, keep_ref, send_ref = refs
    groups = right_ref.shape[1] // LANES
    product_pieces(keep_ref, send_ref, 0, value_ref, right_ref[...], order)
    product_pieces(keep_ref, send_ref, groups, out_ref, mixed_ref[...], order)
    first, second = (sum(ref[...] for ref in gain_refs[n::2]) for n in range(2))
    row = lax.broadcasted_iota(jnp.int32, (LANES, first.shape[1]), 0)
    both = jnp.where(row == 0, first, jnp.where(row == 1, second, 0.0))
    turned = both.T.astype(bf16)
    half, _, depth, _ = keep_ref.shape
    bits = [order[1 << n] for n in reversed(range((2 * half).bit_length() - 1))]
    for g in range(2 * half):
        apart = relative(me_ref, g, 2 * half)
        place = 0
        for bit in bits:
            place = 2 * place + (apart & bit != 0).astype(jnp.int32)
        piece = turned[g * depth : (g + 1) * depth]

        @pl.when(place < half)
        def _():
            keep_ref[jnp.minimum(place, half - 1), 2 * groups] = piece

        @pl.when(place >= half)
        def _():
            send_ref[jnp.maximum(place - half, 0), 2 * groups] = piece


def value_out_pieces(order, turned, right, out_turned, mixed, me, *gains):
    parts, depth, rows = turned.shape
    heads = mixed.shape[1]
    shape = (parts // 2, 2 * heads // LANES + 1, depth, LANES)
    return call(
        functools.partial(value_out_body, order),
        "value_out_grads",
        (1,),
        [
            whole(parts, depth, rows),
            pl.BlockSpec((rows, heads), lambda j: (0, 2)),
            whole(parts, depth, rows),
            whole(rows, heads),
            pl.BlockSpec(memory_space=pltpu.SMEM),
            *[whole(1, parts * depth)] * len(gains),
        ],
        [(whole(*shape), shape, bf16), (whole(*shape), shape, bf16, ANYWHERE)],
        vmem=32,
        cost=(4 * rows * parts * depth * heads, 8 * MIB),
    )(turned, right, out_turned, mixed, me, *gains)


def input_grad_body(x_ref, gm_ref, gain_ref, *refs):
    out_ref, sum_ref, scratch_ref = refs[-3:]
    inputs = x_ref[...].astype(f32)
    inverse = inverse_rms(inputs)
    scaled = inputs * inverse
    upstream = shares_sum(refs, scratch_ref)
    add_up(sum_ref, jnp.sum(upstream * scaled, axis=0, keepdims=True))
    weighted = upstream * row_of(gain_ref)
    out_ref[...] = (
        gm_ref[...].astype(f32)
        + inverse * (weighted - scaled * jnp.mean(weighted * scaled, axis=1, keepdims=True))
    ).astype(bf16)


def input_grad(half, x, grad_middle, gain, shares, earlier):
    rows, width = x.shape
    block = rows // HALVES // PARTS
    there = pl.BlockSpec((block, width), lambda i: (half * PARTS + i, 0))
    ins = [there, rows_of(block, width), whole(width)] + [whole(block, width)] * (2 * PARTS)
    args = [x, grad_middle, gain, *shares]
    aliases = {}
    if earlier is not None:
        ins.append(pl.BlockSpec(memory_space=pl.ANY))
        aliases = {len(args): 0}
        args.append(earlier)
    return call(
        input_grad_body,
        "input_grad",
        (PARTS,),
        ins,
        [(there, (rows, width), bf16), (whole(1, width), (1, width), f32)],
        scratch=[pltpu.VMEM((block, width), f32)],
        vmem=24,
        aliases=aliases,
        cost=(10 * rows // HALVES * width, 6 * MIB),
    )(*args)


def total_of(refs):
    total = refs[0][0].astype(f32)
    for ref in refs[1:]:
        total += ref[0].astype(f32)
    return total


def last_hidden_body(count, block, first_call, *refs):
    total = total_of(refs[:count])
    outs = refs[count if first_call else count + 3 :]
    third = block // LANES
    for c in range(total.shape[0]):
        n, at = c // third % 3, (c // (3 * third) * third + c % third) * LANES
        outs[n][:, at : at + LANES] = total[c]


def last_hidden(first, arrays, steps, block, hidden, earlier):
    _, groups, depth, _ = arrays[0].shape
    at_once = math.gcd(first // block, steps)
    steps //= at_once
    ins = [pl.BlockSpec((1, groups // steps, depth, LANES), lambda j: (0, j, 0, 0))] * len(arrays)
    args = list(arrays)
    aliases = {}
    if earlier is not None:
        ins += [pl.BlockSpec(memory_space=pl.ANY)] * 3
        aliases = {len(arrays) + n: n for n in range(3)}
        args += list(earlier)
    wide = block * at_once
    out = (pl.BlockSpec((depth, wide), lambda j: (0, first // wide + j)), (depth, hidden), f32)
    return call(
        functools.partial(last_hidden_body, len(arrays), block, earlier is None),
        "hidden_grads_out",
        (steps,),
        ins,
        [out] * 3,
        vmem=16,
        aliases=aliases,
        cost=(6 * groups * depth * LANES, MIB),
    )(*args)


def last_heads_body(count, *refs):
    total = total_of(refs[:count])
    outs = refs[count:]
    groups = outs[0].shape[1] // LANES
    for n, ref in enumerate(outs[:2]):
        for c in range(groups):
            ref[:, c * LANES : (c + 1) * LANES] = total[n * groups + c]
    if len(outs) > 2:
        turned = total[2 * groups].T
        for n, ref in enumerate(outs[2:]):
            ref[...] = turned[n]


def last_heads(arrays, heads):
    _, groups, depth, _ = arrays[0].shape
    shapes = [(depth, heads)] * 2
    if groups * LANES > 2 * heads:
        shapes += [(depth,)] * 2
    return call(
        functools.partial(last_heads_body, len(arrays)),
        "head_grads_out",
        (1,),
        [pl.BlockSpec((1, groups, depth, LANES), lambda j: (0, 0, 0, 0))] * len(arrays),
        [(whole(*shape), shape, f32) for shape in shapes],
        vmem=16,
        cost=(6 * groups * depth * LANES, MIB),
    )(*arrays)


def block_output_body(mid_ref, *refs):
    out_ref, scratch_ref = refs[-2:]
    out_ref[...] = (mid_ref[...].astype(f32) + shares_sum(refs, scratch_ref)).astype(bf16)


def block_outputs(middle, shares):
    rows, width = middle.shape
    block = rows // PARTS
    return call(
        block_output_body,
        "block_output",
        (PARTS,),
        [rows_of(block, width)] + [whole(block, width)] * (2 * PARTS),
        [(rows_of(block, width), (rows, width), bf16)],
        scratch=[pltpu.VMEM((block, width), f32)],
        vmem=24,
        cost=(3 * rows * width, 10 * MIB),
    )(middle, *shares)[0]


def swap(array, axis, size, bit):
    return lax.ppermute(array, axis, [(i, i ^ bit) for i in range(size)])


def hop_swap(array, dp, tensor, bit):
    bits = [exchanged(bit, dp) if t % 2 else bit for t in range(tensor)]
    pairs = [
        (i * tensor + t, (i ^ bits[t]) * tensor + t) for i in range(dp) for t in range(tensor)
    ]
    return lax.ppermute(array, ("dp", "tensor"), pairs)


def both_shares(partial, size):
    bit = 1
    while 2 * bit < size:
        other = swap(partial, "tensor", size, bit)
        partial = (partial.astype(f32) + other.astype(f32)).astype(bf16)
        bit *= 2
    return partial, swap(partial, "tensor", size, bit)


def after(value, *others):
    return lax.optimization_barrier((value, *others))[0]


def next_send_body(*refs):
    total = refs[0][...].astype(f32)
    for ref in refs[1:-1]:
        total += ref[...].astype(f32)
    refs[-1][...] = total.astype(bf16)


def next_send(half, arrays):
    _, *rest = arrays[0].shape
    block = max(1, half // 2)
    steps = half // block
    return call(
        next_send_body,
        "next_send",
        (steps,),
        [pl.BlockSpec((block, *rest), lambda i: (steps + i, 0, 0, 0))] * len(arrays),
        [(pl.BlockSpec((block, *rest), lambda i: (i, 0, 0, 0)), (half, *rest), bf16, ANYWHERE)],
        vmem=16,
        cost=(half * math.prod(rest), MIB),
    )(*arrays)[0]


class Line:
    def __init__(self):
        self.last = None

    def __call__(self, kernel, waits, *args):
        if self.last is not None:
            waits, _ = lax.optimization_barrier((waits, self.last))
        out = kernel(waits, *args)
        self.last = jax.tree.leaves(out)[-1]
        return out


class Halving:
    def __init__(self, line, pieces, sizes, bits):
        self.line, self.sizes, self.bits = line, sizes, list(bits)
        self.arrays = [pieces[0]]
        self.half = sizes[0] // 2
        self.launch(pieces[1])

    def launch(self, send):
        self.coming = hop_swap(send, *self.sizes, self.bits.pop(0))

    def hop(self):
        self.arrays.append(self.coming)
        self.half //= 2
        self.launch(
            self.line(
                lambda newest: next_send(self.half, [*self.arrays[:-1], newest]), self.arrays[-1]
            )
        )

    def end(self, kernel, *rest):
        return self.line(lambda newest: kernel([*self.arrays, newest], *rest), self.coming)


STEPS = (
    "attn", "seed", "mid", "H0", "H1", "ntA", "ntB", "mbA", "mbB", "abA", "h:0", "abB", "igA",
    "QK", "igB", "VO", "h:1", "h:0", "down", "h:QK", "h:VO", "h:1", "h:QK", "h:VO", "h:0", "h:VO",
    "h:1", "h:QK", "e:QK", "bo", "e:1", "e:0", "e:VO",
)


class Layer:
    def __init__(self, args, dp, tensor, bits_of):
        (
            self.x, self.wq, self.wk, self.wv, self.wo, self.wg, self.wu, self.wd,
            self.gain_one, self.gain_two, self.lengths, self.cot,
        ) = args
        self.dp, self.tensor, self.bits_of = dp, tensor, bits_of
        self.heads, self.units = self.wq.shape[1], self.wg.shape[1]
        self.line, self.sums = Line(), {}
        self.block = 256 if self.units >= 2048 else LANES
        blocks = self.units // self.block
        shares = [blocks * n // 8 for n in (5,)]
        self.shares = [*shares, blocks - sum(shares)]
        self.me = jnp.stack([lax.axis_index("dp"), lax.axis_index("tensor") % 2]).astype(jnp.int32)
        self.acts = self.saved = self.gqkv = self.grads = self.grad_input = None
        self.mid_shares, self.in_shares, self.middle_grads, self.gain_sums = [], [], [], {}

    def order(self, name):
        return places(self.dp, self.bits_of[name])

    def begin(self, name, pieces):
        self.sums[name] = Halving(self.line, pieces, (self.dp, self.tensor), self.bits_of[name])

    def shared(self, parts):
        both = [both_shares(part, self.tensor) for part in parts]
        return [own for own, _ in both] + [peer for _, peer in both]

    def attention(self):
        self.q, self.k, self.v, self.mixed, self.probs, part = attention(
            self.x, self.gain_one, self.wq, self.wk, self.wv, self.wo
        )
        self.line.last = part
        self.own, self.peer = both_shares(part, self.tensor)

    def seeds(self):
        self.seed, self.seed_t, self.normed_t = self.line(
            lambda cot: seeds(self.lengths, self.me, cot, self.x, self.gain_one, self.dp), self.cot
        )

    def middles(self):
        self.middle, self.normed, self.normed_two_t = self.line(
            lambda peer: middles(self.me, self.x, self.own, peer, self.gain_two, self.dp), self.peer
        )

    def hidden(self, c):
        *acts, keep, send = self.line(
            lambda normed: hidden_chunk(
                self.block * sum(self.shares[:c]), self.shares[c], self.block, self.order(c),
                normed, self.normed_two_t, self.seed, self.seed_t, self.wg, self.wu, self.wd, self.acts,
            ),
            self.normed,
        )
        self.acts = acts
        self.begin(c, (keep, send))

    def normed_back(self, half):
        parts = self.line(
            lambda gg: normed_two_back(half, gg, self.acts[2], self.wg, self.wu), self.acts[1]
        )
        self.mid_shares.append(self.shared(parts))

    def down(self):
        self.down_shares = self.shared(
            self.line(lambda hidden: hidden_down(hidden, self.wd), self.acts[0])
        )

    def output(self):
        self.block_output = self.line(
            lambda shares: block_outputs(self.middle, shares), self.down_shares
        )

    def middle_back(self, half):
        *self.saved, grad, self.gain_sums["two", half] = self.line(
            lambda shares: middle_back(
                half, self.me, self.middle, self.seed, self.gain_two, self.wo, self.dp, shares, self.saved
            ),
            self.mid_shares[half],
        )
        self.middle_grads.append(grad)

    def attention_back(self, half):
        self.gqkv, *parts = self.line(
            lambda grad_mixed: attention_back(
                half, self.q, self.k, self.v, self.probs, grad_mixed, self.wq, self.wk, self.wv, self.gqkv
            ),
            self.saved[1],
        )
        self.in_shares.append(self.shared(parts))

    def query_key(self):
        self.begin(
            "qk",
            self.line(
                lambda gqkv: query_key_pieces(self.order("qk"), self.normed_t, gqkv, self.heads),
                self.gqkv,
            ),
        )

    def input_back(self, half):
        self.grad_input, self.gain_sums["one", half] = self.line(
            lambda shares: input_grad(
                half, self.x, self.middle_grads[half], self.gain_one, shares, self.grad_input
            ),
            self.in_shares[half],
        )

    def value_out(self):
        gains = [self.gain_sums[name, half] for half in range(HALVES) for name in ("one", "two")]
        self.begin(
            "vo",
            self.line(
                lambda gqkv: value_out_pieces(
                    self.order("vo"), self.normed_t, gqkv, self.saved[0], self.mixed, self.me, *gains
                ),
                self.gqkv,
            ),
        )

    def hop(self, name):
        if self.sums[name].bits:
            self.sums[name].hop()

    def end(self, name):
        one = self.sums[name]
        while one.bits:
            one.hop()
        if name == "qk":
            self.grad_query, self.grad_key = one.end(last_heads, self.heads)
        elif name == "vo":
            self.grad_value, self.grad_out, *self.gains = one.end(last_heads, self.heads)
        else:
            first = self.block * sum(self.shares[:name])
            self.grads = one.end(
                lambda arrays: last_hidden(
                    first, arrays, self.shares[name], self.block, self.units, self.grads
                )
            )

    def run(self):
        calls = {
            "attn": self.attention, "seed": self.seeds, "mid": self.middles, "down": self.down,
            "bo": self.output, "QK": self.query_key, "VO": self.value_out,
        }
        halves = {
            "nt": self.normed_back, "mb": self.middle_back,
            "ab": self.attention_back, "ig": self.input_back,
        }
        for step in STEPS:
            if step in calls:
                calls[step]()
            elif step[:2] in halves:
                halves[step[:2]]("AB".index(step[2:]))
            elif step[0] == "H":
                self.hidden(int(step[1:]))
            else:
                name = step[2:].lower()
                name = int(name) if name.isdigit() else name
                (self.hop if step[0] == "h" else self.end)(name)
        return (
            self.block_output,
            self.grad_input,
            self.grad_query,
            self.grad_key,
            self.grad_value,
            self.grad_out.T,
            self.grads[0],
            self.grads[1],
            self.grads[2].T,
            *self.gains,
        )


def body_of(dp, tensor):
    n_bits = dp.bit_length() - 1

    def order(*start):
        return [1 << k for k in start if k < n_bits] + [1 << k for k in range(n_bits) if k not in start]

    bits_of = {
        0: order(0, 1, 3, 2),
        1: order(2, 0, 1, 3),
        "qk": order(0, 2, 3, 1),
        "vo": order(0, 1, 2, 3),
    }

    def body(*args):
        return Layer(args, dp, tensor, bits_of).run()

    return body


def solution(mesh):
    placed = (
        P("dp", None),
        P(None, "tensor"),
        P(None, "tensor"),
        P(None, "tensor"),
        P("tensor", None),
        P(None, "tensor"),
        P(None, "tensor"),
        P("tensor", None),
        P(),
        P(),
        P("dp"),
        P("dp", None),
    )
    return jax.shard_map(
        body_of(mesh.shape["dp"], mesh.shape["tensor"]),
        mesh=mesh,
        in_specs=placed,
        out_specs=(
            P("dp", None),
            P("dp", None),
            P("dp", "tensor"),
            P("dp", "tensor"),
            P("dp", "tensor"),
            P("tensor", "dp"),
            P("dp", "tensor"),
            P("dp", "tensor"),
            P("tensor", "dp"),
            P("dp"),
            P("dp"),
        ),
        check_vma=False,
    )
```

```python
import functools
import math

import jax
import jax.numpy as jnp
from jax import lax
from jax.experimental import pallas as pl
from jax.experimental.pallas import tpu as pltpu
from jax.sharding import PartitionSpec as P

HD = 64
POS = 16
SLOT = 32
LANES = 128
TILE = 128
MIB = 1 << 20
HALVES = 2
PARTS = 2
COST = 1e-6
SLACK = {}

epsilon = 1e-05
f32 = jnp.float32
bf16 = jnp.bfloat16
SCALE = 1.0 / math.sqrt(HD)
ANYWHERE = jax.ShapeDtypeStruct


def nn(left, right):
    return lax.dot_general(left, right, (((1,), (0,)), ((), ())), preferred_element_type=f32)


def nt(left, right):
    return lax.dot_general(left, right, (((1,), (1,)), ((), ())), preferred_element_type=f32)


def tn(left, right):
    return lax.dot_general(left, right, (((0,), (0,)), ((), ())), preferred_element_type=f32)


def call(body, name, grid, ins, outs, scratch=(), vmem=40, scalars=0, aliases=None, cost=None, far=()):
    kernel = pl.pallas_call(
        body,
        grid_spec=pltpu.PrefetchScalarGridSpec(
            num_scalar_prefetch=scalars,
            grid=grid,
            in_specs=ins,
            out_specs=[spec for spec, *_ in outs],
            scratch_shapes=scratch,
        ),
        out_shape=[
            (where[0] if where else pltpu.HBM)(shape, dtype) for _, shape, dtype, *where in outs
        ],
        input_output_aliases=aliases or {},
        compiler_params=pltpu.CompilerParams(vmem_limit_bytes=vmem * MIB),
        cost_estimate=pl.CostEstimate(
            flops=int(cost[0] * COST + SLACK.get(name, 0)), bytes_accessed=0, transcendentals=0
        ),
        name=name,
    )

    def run(*args):
        return kernel(
            *(
                pltpu.with_memory_space_constraint(arg, pltpu.HBM) if n - scalars in far else arg
                for n, arg in enumerate(args)
            )
        )

    return run


def rows_of(block, width):
    return pl.BlockSpec((block, width), lambda i, *_: (i, 0))


def whole(*shape):
    return pl.BlockSpec(shape, lambda *_: (0,) * len(shape))


def row_of(gain_ref):
    return gain_ref[...].astype(f32).reshape(1, -1)


def inverse_rms(values):
    return lax.rsqrt(jnp.mean(values * values, axis=1, keepdims=True) + epsilon)


def exchanged(index, size):
    low, high = (1, 4) if size >= 16 else (1, 0)
    if size < 4:
        return index
    moved = low | high
    kept = index & ~(3 * moved)
    return kept | (index & moved) << 1 | index >> 1 & moved


def relative(place_ref, g, size):
    apart = g ^ place_ref[0]
    return jnp.where(place_ref[1] == 1, exchanged(apart, size), apart)


def put_transposed(ref, place_ref, values):
    parts, depth, _ = ref.shape
    turned = values.T
    for g in range(parts):
        ref[relative(place_ref, g, parts)] = turned[g * depth : (g + 1) * depth]


def pair_mask():
    rows = lax.broadcasted_iota(jnp.int32, (TILE, 2 * TILE), 0)
    keys = lax.broadcasted_iota(jnp.int32, (TILE, 2 * TILE), 1) & (TILE - 1)
    return (rows // POS == keys // POS) & (keys <= rows)


def two_heads(values):
    first = lax.broadcasted_iota(jnp.int32, values.shape, 1) < HD
    zero = jnp.zeros_like(values)
    return jnp.concatenate(
        [jnp.where(first, values, zero), jnp.where(first, zero, values)], axis=0
    )


def one_pair(values):
    first = lax.broadcasted_iota(jnp.int32, (TILE, LANES), 1) < HD
    return jnp.where(first, values[:TILE], values[TILE:])


def per_head(op, values):
    both = [
        jnp.broadcast_to(op(values[:, s : s + TILE], axis=1, keepdims=True), (TILE, TILE))
        for s in (0, TILE)
    ]
    return jnp.concatenate(both, axis=1)


def probs_of(queries, keys, mask):
    scores = jnp.where(mask, nt(queries, keys) * SCALE, -1e30)
    powers = jnp.exp(scores - per_head(jnp.max, scores))
    return powers / per_head(jnp.sum, powers)


def pairs_of(rows, width):
    return [
        (pl.ds(t * TILE, TILE), pl.ds(p * LANES, LANES))
        for t in range(rows // TILE)
        for p in range(width // LANES)
    ]


def wide(lanes):
    return pl.ds(lanes.start // LANES * 2 * TILE, 2 * TILE)


def attention_body(
    x_ref, gain_ref, wq_ref, wk_ref, wv_ref, wo_ref, q_ref, k_ref, v_ref, m_ref, p_ref, part_ref
):
    normed = normed_of(x_ref, gain_ref)
    q_ref[...] = nn(normed, wq_ref[...]).astype(bf16)
    k_ref[...] = nn(normed, wk_ref[...]).astype(bf16)
    v_ref[...] = nn(normed, wv_ref[...]).astype(bf16)
    mask = pair_mask()
    for at in pairs_of(*q_ref.shape):
        probs = probs_of(q_ref[at], two_heads(k_ref[at]), mask).astype(bf16)
        p_ref[at[0], wide(at[1])] = probs
        m_ref[at] = nn(probs, two_heads(v_ref[at])).astype(bf16)
    part_ref[...] = nn(m_ref[...], wo_ref[...]).astype(bf16)


def attention(x, gain, wq, wk, wv, wo):
    rows, width = x.shape
    heads = wq.shape[1]
    block = 256
    outs = [(rows_of(block, heads), (rows, heads), bf16)] * 4
    spread = 2 * TILE * heads // LANES
    outs += [(rows_of(block, spread), (rows, spread), bf16)]
    outs += [(rows_of(block, width), (rows, width), bf16, ANYWHERE)]
    return call(
        attention_body,
        "attention_forward",
        (rows // block,),
        [rows_of(block, width), whole(width)]
        + [whole(width, heads)] * 3
        + [whole(heads, width)],
        outs,
        vmem=24,
        cost=(8 * rows * width * heads, 12 * MIB),
        far=(0, 2, 3, 4, 5),
    )(x, gain, wq, wk, wv, wo)


def seed_body(lengths_ref, me_ref, cot_ref, x_ref, gain_ref, seed_ref, turned_ref, normed_ref):
    block = cot_ref.shape[0]
    first = pl.program_id(0) * block
    length = lengths_ref[first // (SLOT * POS)]
    row = lax.broadcasted_iota(jnp.int32, cot_ref.shape, 0) + first % (SLOT * POS)
    cot = cot_ref[...].astype(f32)
    seed = jnp.where(row // POS < length, cot, 0.0).astype(bf16)
    seed_ref[...] = seed
    put_transposed(turned_ref, me_ref, seed)
    put_transposed(normed_ref, me_ref, normed_of(x_ref, gain_ref))


def normed_of(x_ref, gain_ref):
    values = x_ref[...].astype(f32)
    return (values * inverse_rms(values) * row_of(gain_ref)).astype(bf16)


def turned_out(parts, depth, rows, block):
    return (
        pl.BlockSpec((parts, depth, block), lambda i, *_: (0, 0, i)),
        (parts, depth, rows),
        bf16,
    )


def seeds(lengths, me, cot, x, gain, parts):
    rows, width = cot.shape
    block = 256
    turned = turned_out(parts, width // parts, rows, block)
    return call(
        seed_body,
        "seed_rows",
        (rows // block,),
        [rows_of(block, width)] * 2 + [whole(width)],
        [(rows_of(block, width), (rows, width), bf16, pltpu.VMEM), (*turned, pltpu.VMEM), turned],
        vmem=16,
        scalars=2,
        far=(0, 1),
        cost=(4 * rows * width, 6 * MIB),
    )(lengths, me, cot, x, gain)


def middle_body(me_ref, x_ref, own_ref, peer_ref, gain_ref, middle_ref, normed_ref, turned_ref):
    middle = x_ref[...].astype(f32) + (own_ref[...].astype(f32) + peer_ref[...].astype(f32))
    middle_ref[...] = middle.astype(bf16)
    normed = (middle * inverse_rms(middle) * row_of(gain_ref)).astype(bf16)
    normed_ref[...] = normed
    put_transposed(turned_ref, me_ref, normed)


def middles(me, x, own, peer, gain, parts):
    rows, width = x.shape
    block = 256
    return call(
        middle_body,
        "middle_rows",
        (rows // block,),
        [rows_of(block, width)] * 3 + [whole(width)],
        [
            (rows_of(block, width), (rows, width), bf16),
            (rows_of(block, width), (rows, width), bf16, pltpu.VMEM),
            (*turned_out(parts, width // parts, rows, block), pltpu.VMEM),
        ],
        vmem=24,
        scalars=1,
        cost=(8 * rows * width, 14 * MIB),
    )(me, x, own, peer, gain)


def places(parts, bits):
    count = len(bits)
    return [
        sum(bit for n, bit in enumerate(bits) if place >> (count - 1 - n) & 1)
        for place in range(parts)
    ]


def put_pieces(keep_ref, send_ref, column, values, order, first):
    half, _, depth, _ = keep_ref.shape
    low = values.astype(bf16)
    for n in range(values.shape[0] // depth):
        place = order.index(first + n)
        ref, at = (keep_ref, place) if place < half else (send_ref, place - half)
        for c in range(values.shape[1] // LANES):
            ref[at, column + c] = low[
                n * depth : (n + 1) * depth, c * LANES : (c + 1) * LANES
            ]


def product_pieces(keep_ref, send_ref, column, turned_ref, right, order):
    parts, depth, rows = turned_ref.shape
    group = max(1, 256 // depth)
    for first in range(0, parts, group):
        left = turned_ref[pl.ds(first, group)].reshape(group * depth, rows)
        put_pieces(keep_ref, send_ref, column, nn(left, right), order, first)


def resident():
    return pl.BlockSpec(memory_space=pltpu.VMEM)


def hidden_body(order, first, block, first_call, *refs):
    (n_ref, nt_ref, s_ref, st_ref, wg_ref, wu_ref, wd_ref) = refs[:7]
    h_ref, gg_ref, gu_ref, keep_ref, send_ref = refs[7 if first_call else 10 :]
    rows = n_ref.shape[0]
    step = min(256, rows)
    here = pl.ds(pl.multiple_of(first + pl.program_id(0) * block, block), block)
    for r in range(0, rows, step):
        at = pl.ds(r, step)
        gate = nn(n_ref[at], wg_ref[:, here])
        up = nn(n_ref[at], wu_ref[:, here])
        back = nt(s_ref[at], wd_ref[...])
        sig = 1.0 / (1.0 + jnp.exp(-gate))
        silu = gate * sig
        h_ref[at, here] = (silu * up).astype(bf16)
        gg_ref[at, here] = (back * up * (sig * (1.0 + gate * (1.0 - sig)))).astype(bf16)
        gu_ref[at, here] = (back * silu).astype(bf16)
    columns = block // LANES
    product_pieces(keep_ref, send_ref, 0, nt_ref, gg_ref[:, here], order)
    product_pieces(keep_ref, send_ref, columns, nt_ref, gu_ref[:, here], order)
    product_pieces(keep_ref, send_ref, 2 * columns, st_ref, h_ref[:, here], order)


def hidden_chunk(first, steps, block, order, normed, normed_t, seed, seed_t, wg, wu, wd, earlier):
    rows, width = normed.shape
    parts, depth, _ = normed_t.shape
    hidden = wg.shape[1]
    groups = 3 * block // LANES
    pieces = (
        pl.BlockSpec((parts // 2, groups, depth, LANES), lambda j: (0, j, 0, 0)),
        (parts // 2, steps * groups, depth, LANES),
        bf16,
    )
    args = [normed, normed_t, seed, seed_t, wg, wu, wd]
    ins = [resident()] * 6
    ins.append(pl.BlockSpec((block, width), lambda j: (first // block + j, 0)))
    aliases = {}
    if earlier is not None:
        aliases = {7: 0, 8: 1, 9: 2}
        args += list(earlier)
        ins += [resident()] * 3
    return call(
        functools.partial(hidden_body, order, first, block, earlier is None),
        "hidden_units",
        (steps,),
        ins,
        [(resident(), (rows, hidden), bf16, pltpu.VMEM)] * 3 + [pieces, (*pieces, ANYWHERE)],
        vmem=13,
        far=(6,),
        aliases=aliases,
        cost=(12 * rows * width * block * steps, 20 * MIB),
    )(*args)


def back_body(first, gg_ref, gu_ref, wg_ref, wu_ref, *part_refs):
    rows = part_refs[0].shape[0]
    here = pl.ds(first, rows * len(part_refs))
    part = nt(gg_ref[here], wg_ref[...]) + nt(gu_ref[here], wu_ref[...])
    for n, ref in enumerate(part_refs):
        ref[...] = part[n * rows : (n + 1) * rows].astype(bf16)


def normed_two_back(half, gg, gu, wg, wu):
    rows, hidden = gg.shape
    rows //= HALVES
    width = wg.shape[0]
    block = 256
    weights = pl.BlockSpec((block, hidden), lambda j: (j, 0))
    piece = rows // PARTS
    out = (pl.BlockSpec((piece, block), lambda j: (0, j)), (piece, width), bf16, ANYWHERE)
    return call(
        functools.partial(back_body, half * rows),
        "normed_two_back",
        (width // block,),
        [resident()] * 2 + [weights] * 2,
        [out] * PARTS,
        vmem=20,
        cost=(4 * rows * width * hidden, 14 * MIB),
    )(gg, gu, wg, wu)


def down_body(h_ref, wd_ref, *part_refs):
    part = nn(h_ref[...], wd_ref[...])
    rows = part_refs[0].shape[0]
    for n, ref in enumerate(part_refs):
        ref[...] = part[n * rows : (n + 1) * rows].astype(bf16)


def hidden_down(hidden, wd):
    rows, units = hidden.shape
    width = wd.shape[1]
    block = 256
    piece = rows // PARTS
    out = (pl.BlockSpec((piece, block), lambda j: (0, j)), (piece, width), bf16, ANYWHERE)
    return call(
        down_body,
        "hidden_down",
        (width // block,),
        [resident(), pl.BlockSpec((units, block), lambda j: (0, j))],
        [out] * PARTS,
        vmem=20,
        cost=(2 * rows * width * units, 10 * MIB),
    )(hidden, wd)


def add_up(ref, part):
    @pl.when(pl.program_id(0) == 0)
    def _():
        ref[...] = part

    @pl.when(pl.program_id(0) > 0)
    def _():
        ref[...] += part


def shares_sum(pairs, scratch_ref):
    for n in range(PARTS):

        @pl.when(pl.program_id(0) == n)
        def _():
            scratch_ref[...] = pairs[n][...].astype(f32) + pairs[PARTS + n][...].astype(f32)

    return scratch_ref[...]


def middle_back_body(me_ref, mid_ref, seed_ref, gain_ref, wo_ref, *refs):
    turned_ref, mixed_ref, grad_ref, sum_ref, scratch_ref = refs[-5:]
    upstream = shares_sum(refs, scratch_ref)
    middle = mid_ref[...].astype(f32)
    inverse = inverse_rms(middle)
    scaled = middle * inverse
    add_up(sum_ref, jnp.sum(upstream * scaled, axis=0, keepdims=True))
    weighted = upstream * row_of(gain_ref)
    grad_middle = seed_ref[...].astype(f32) + inverse * (
        weighted - scaled * jnp.mean(weighted * scaled, axis=1, keepdims=True)
    )
    low = grad_middle.astype(bf16)
    grad_ref[...] = low
    mixed_ref[...] = nt(low, wo_ref[...]).astype(bf16)
    put_transposed(turned_ref, me_ref, low)


def middle_back(half, me, middle, seed, gain, wo, parts, shares, earlier):
    rows, width = middle.shape
    heads = wo.shape[0]
    share = rows // HALVES
    block = share // PARTS
    depth = width // parts
    there = lambda n: pl.BlockSpec((block, n), lambda i, *_: (half * PARTS + i, 0))
    ins = [there(width)] * 2 + [whole(width), whole(heads, width)]
    ins += [whole(block, width)] * (2 * PARTS)
    args = [me, middle, seed, gain, wo, *shares]
    aliases = {}
    if earlier is not None:
        ins += [pl.BlockSpec(memory_space=pl.ANY)] * 2
        aliases = {len(args) + n: n for n in range(2)}
        args += list(earlier)
    return call(
        middle_back_body,
        "middle_backward",
        (PARTS,),
        ins,
        [
            (
                pl.BlockSpec((parts, depth, block), lambda i, *_: (0, 0, half * PARTS + i)),
                (parts, depth, rows),
                bf16,
            ),
            (there(heads), (rows, heads), bf16),
            (rows_of(block, width), (share, width), bf16),
            (whole(1, width), (1, width), f32),
        ],
        scratch=[pltpu.VMEM((block, width), f32)],
        vmem=24,
        scalars=1,
        aliases=aliases,
        cost=(2 * share * width * heads, 9 * MIB),
    )(*args)


def attention_back_body(q_ref, k_ref, v_ref, p_ref, mixed_ref, wq_ref, wk_ref, wv_ref, *refs):
    gqkv_ref, *part_refs = refs[-1 - PARTS :]
    heads = q_ref.shape[1]
    for at in pairs_of(*q_ref.shape):
        rows, lanes = at
        queries, grads = q_ref[at], mixed_ref[at]
        keys, values = two_heads(k_ref[at]), two_heads(v_ref[at])
        low = p_ref[rows, wide(lanes)]
        probs = low.astype(f32)
        grad_probs = nt(grads, values)
        grad_values = one_pair(tn(low, grads))
        inner = per_head(jnp.sum, grad_probs * probs)
        grad_scores = (probs * (grad_probs - inner)).astype(bf16)
        grad_queries = nn(grad_scores, keys) * SCALE
        grad_keys = one_pair(tn(grad_scores, queries)) * SCALE
        for n, grad in enumerate((grad_queries, grad_keys, grad_values)):
            gqkv_ref[rows, pl.ds(n * heads + lanes.start, LANES)] = grad.astype(bf16)
    part = nt(gqkv_ref[:, :heads], wq_ref[...])
    part += nt(gqkv_ref[:, heads : 2 * heads], wk_ref[...])
    part += nt(gqkv_ref[:, 2 * heads :], wv_ref[...])
    for n, ref in enumerate(part_refs):

        @pl.when(pl.program_id(0) == n)
        def _():
            ref[...] = part.astype(bf16)


def attention_back(half, q, k, v, probs, grad_mixed, wq, wk, wv, earlier):
    rows, heads = q.shape
    width = wq.shape[0]
    share = rows // HALVES
    block = share // PARTS
    there = lambda n: pl.BlockSpec((block, n), lambda i: (half * PARTS + i, 0))
    ins = [there(heads)] * 3 + [there(probs.shape[1]), there(heads)] + [whole(width, heads)] * 3
    args = [q, k, v, probs, grad_mixed, wq, wk, wv]
    aliases = {}
    if earlier is not None:
        ins.append(pl.BlockSpec(memory_space=pl.ANY))
        aliases = {len(args): 0}
        args.append(earlier)
    return call(
        attention_back_body,
        "attention_backward",
        (PARTS,),
        ins,
        [
            (there(3 * heads), (rows, 3 * heads), bf16, ANYWHERE),
            *[(whole(block, width), (block, width), bf16, ANYWHERE)] * PARTS,
        ],
        vmem=32,
        far=(4,),
        aliases=aliases,
        cost=(6 * share * width * heads, 9 * MIB),
    )(*args)


def query_key_body(order, turned_ref, right_ref, keep_ref, send_ref):
    product_pieces(keep_ref, send_ref, 0, turned_ref, right_ref[...], order)


def query_key_pieces(order, turned, right, heads):
    parts, depth, rows = turned.shape
    groups = heads // LANES
    pieces = (
        pl.BlockSpec((parts // 2, groups, depth, LANES), lambda j: (0, j, 0, 0)),
        (parts // 2, 2 * groups, depth, LANES),
        bf16,
    )
    return call(
        functools.partial(query_key_body, order),
        "query_key_grads",
        (2,),
        [whole(parts, depth, rows), pl.BlockSpec((rows, heads), lambda j: (0, j))],
        [pieces, (*pieces, ANYWHERE)],
        vmem=24,
        cost=(4 * rows * parts * depth * heads, 6 * MIB),
    )(turned, right)


def value_out_body(order, value_ref, right_ref, out_ref, mixed_ref, me_ref, *refs):
    *gain_refs, keep_ref, send_ref = refs
    groups = right_ref.shape[1] // LANES
    product_pieces(keep_ref, send_ref, 0, value_ref, right_ref[...], order)
    product_pieces(keep_ref, send_ref, groups, out_ref, mixed_ref[...], order)
    first, second = (sum(ref[...] for ref in gain_refs[n::2]) for n in range(2))
    row = lax.broadcasted_iota(jnp.int32, (LANES, first.shape[1]), 0)
    both = jnp.where(row == 0, first, jnp.where(row == 1, second, 0.0))
    turned = both.T.astype(bf16)
    half, _, depth, _ = keep_ref.shape
    bits = [order[1 << n] for n in reversed(range((2 * half).bit_length() - 1))]
    for g in range(2 * half):
        apart = relative(me_ref, g, 2 * half)
        place = 0
        for bit in bits:
            place = 2 * place + (apart & bit != 0).astype(jnp.int32)
        piece = turned[g * depth : (g + 1) * depth]

        @pl.when(place < half)
        def _():
            keep_ref[jnp.minimum(place, half - 1), 2 * groups] = piece

        @pl.when(place >= half)
        def _():
            send_ref[jnp.maximum(place - half, 0), 2 * groups] = piece


def value_out_pieces(order, turned, right, out_turned, mixed, me, *gains):
    parts, depth, rows = turned.shape
    heads = mixed.shape[1]
    shape = (parts // 2, 2 * heads // LANES + 1, depth, LANES)
    return call(
        functools.partial(value_out_body, order),
        "value_out_grads",
        (1,),
        [
            whole(parts, depth, rows),
            pl.BlockSpec((rows, heads), lambda j: (0, 2)),
            whole(parts, depth, rows),
            whole(rows, heads),
            pl.BlockSpec(memory_space=pltpu.SMEM),
            *[whole(1, parts * depth)] * len(gains),
        ],
        [(whole(*shape), shape, bf16), (whole(*shape), shape, bf16, ANYWHERE)],
        vmem=32,
        cost=(4 * rows * parts * depth * heads, 8 * MIB),
    )(turned, right, out_turned, mixed, me, *gains)


def input_grad_body(x_ref, gm_ref, gain_ref, *refs):
    out_ref, sum_ref, scratch_ref = refs[-3:]
    inputs = x_ref[...].astype(f32)
    inverse = inverse_rms(inputs)
    scaled = inputs * inverse
    upstream = shares_sum(refs, scratch_ref)
    add_up(sum_ref, jnp.sum(upstream * scaled, axis=0, keepdims=True))
    weighted = upstream * row_of(gain_ref)
    out_ref[...] = (
        gm_ref[...].astype(f32)
        + inverse * (weighted - scaled * jnp.mean(weighted * scaled, axis=1, keepdims=True))
    ).astype(bf16)


def input_grad(half, x, grad_middle, gain, shares, earlier):
    rows, width = x.shape
    block = rows // HALVES // PARTS
    there = pl.BlockSpec((block, width), lambda i: (half * PARTS + i, 0))
    ins = [there, rows_of(block, width), whole(width)] + [whole(block, width)] * (2 * PARTS)
    args = [x, grad_middle, gain, *shares]
    aliases = {}
    if earlier is not None:
        ins.append(pl.BlockSpec(memory_space=pl.ANY))
        aliases = {len(args): 0}
        args.append(earlier)
    return call(
        input_grad_body,
        "input_grad",
        (PARTS,),
        ins,
        [(there, (rows, width), bf16), (whole(1, width), (1, width), f32)],
        scratch=[pltpu.VMEM((block, width), f32)],
        vmem=24,
        aliases=aliases,
        cost=(10 * rows // HALVES * width, 6 * MIB),
    )(*args)


def total_of(refs):
    total = refs[0][0].astype(f32)
    for ref in refs[1:]:
        total += ref[0].astype(f32)
    return total


def last_hidden_body(count, block, first_call, *refs):
    total = total_of(refs[:count])
    outs = refs[count if first_call else count + 3 :]
    third = block // LANES
    for c in range(total.shape[0]):
        n, at = c // third % 3, (c // (3 * third) * third + c % third) * LANES
        outs[n][:, at : at + LANES] = total[c]


def last_hidden(first, arrays, steps, block, hidden, earlier):
    _, groups, depth, _ = arrays[0].shape
    at_once = math.gcd(first // block, steps)
    steps //= at_once
    ins = [pl.BlockSpec((1, groups // steps, depth, LANES), lambda j: (0, j, 0, 0))] * len(arrays)
    args = list(arrays)
    aliases = {}
    if earlier is not None:
        ins += [pl.BlockSpec(memory_space=pl.ANY)] * 3
        aliases = {len(arrays) + n: n for n in range(3)}
        args += list(earlier)
    wide = block * at_once
    out = (pl.BlockSpec((depth, wide), lambda j: (0, first // wide + j)), (depth, hidden), f32)
    return call(
        functools.partial(last_hidden_body, len(arrays), block, earlier is None),
        "hidden_grads_out",
        (steps,),
        ins,
        [out] * 3,
        vmem=16,
        aliases=aliases,
        cost=(6 * groups * depth * LANES, MIB),
    )(*args)


def last_heads_body(count, *refs):
    total = total_of(refs[:count])
    outs = refs[count:]
    groups = outs[0].shape[1] // LANES
    for n, ref in enumerate(outs[:2]):
        for c in range(groups):
            ref[:, c * LANES : (c + 1) * LANES] = total[n * groups + c]
    if len(outs) > 2:
        turned = total[2 * groups].T
        for n, ref in enumerate(outs[2:]):
            ref[...] = turned[n]


def last_heads(arrays, heads):
    _, groups, depth, _ = arrays[0].shape
    shapes = [(depth, heads)] * 2
    if groups * LANES > 2 * heads:
        shapes += [(depth,)] * 2
    return call(
        functools.partial(last_heads_body, len(arrays)),
        "head_grads_out",
        (1,),
        [pl.BlockSpec((1, groups, depth, LANES), lambda j: (0, 0, 0, 0))] * len(arrays),
        [(whole(*shape), shape, f32) for shape in shapes],
        vmem=16,
        cost=(6 * groups * depth * LANES, MIB),
    )(*arrays)


def block_output_body(mid_ref, *refs):
    out_ref, scratch_ref = refs[-2:]
    out_ref[...] = (mid_ref[...].astype(f32) + shares_sum(refs, scratch_ref)).astype(bf16)


def block_outputs(middle, shares):
    rows, width = middle.shape
    block = rows // PARTS
    return call(
        block_output_body,
        "block_output",
        (PARTS,),
        [rows_of(block, width)] + [whole(block, width)] * (2 * PARTS),
        [(rows_of(block, width), (rows, width), bf16)],
        scratch=[pltpu.VMEM((block, width), f32)],
        vmem=24,
        cost=(3 * rows * width, 10 * MIB),
    )(middle, *shares)[0]


def swap(array, axis, size, bit):
    return lax.ppermute(array, axis, [(i, i ^ bit) for i in range(size)])


def hop_swap(array, dp, tensor, bit):
    bits = [exchanged(bit, dp) if t % 2 else bit for t in range(tensor)]
    pairs = [
        (i * tensor + t, (i ^ bits[t]) * tensor + t) for i in range(dp) for t in range(tensor)
    ]
    return lax.ppermute(array, ("dp", "tensor"), pairs)


def both_shares(partial, size):
    bit = 1
    while 2 * bit < size:
        other = swap(partial, "tensor", size, bit)
        partial = (partial.astype(f32) + other.astype(f32)).astype(bf16)
        bit *= 2
    return partial, swap(partial, "tensor", size, bit)


def after(value, *others):
    return lax.optimization_barrier((value, *others))[0]


def next_send_body(*refs):
    total = refs[0][...].astype(f32)
    for ref in refs[1:-1]:
        total += ref[...].astype(f32)
    refs[-1][...] = total.astype(bf16)


def next_send(half, arrays):
    _, *rest = arrays[0].shape
    block = max(1, half // 2)
    steps = half // block
    return call(
        next_send_body,
        "next_send",
        (steps,),
        [pl.BlockSpec((block, *rest), lambda i: (steps + i, 0, 0, 0))] * len(arrays),
        [(pl.BlockSpec((block, *rest), lambda i: (i, 0, 0, 0)), (half, *rest), bf16, ANYWHERE)],
        vmem=16,
        cost=(half * math.prod(rest), MIB),
    )(*arrays)[0]


class Line:
    def __init__(self):
        self.last = None

    def __call__(self, kernel, waits, *args):
        if self.last is not None:
            waits, _ = lax.optimization_barrier((waits, self.last))
        out = kernel(waits, *args)
        self.last = jax.tree.leaves(out)[-1]
        return out


class Halving:
    def __init__(self, line, pieces, sizes, bits):
        self.line, self.sizes, self.bits = line, sizes, list(bits)
        self.arrays = [pieces[0]]
        self.half = sizes[0] // 2
        self.launch(pieces[1])

    def launch(self, send):
        self.coming = hop_swap(send, *self.sizes, self.bits.pop(0))

    def hop(self):
        self.arrays.append(self.coming)
        self.half //= 2
        self.launch(
            self.line(
                lambda newest: next_send(self.half, [*self.arrays[:-1], newest]), self.arrays[-1]
            )
        )

    def end(self, kernel, *rest):
        return self.line(lambda newest: kernel([*self.arrays, newest], *rest), self.coming)


STEPS = (
    "attn", "seed", "mid", "H0", "H1", "ntA", "ntB", "mbA", "mbB", "abA", "h:0", "abB", "QK",
    "igA", "h:1", "igB", "VO", "h:0", "h:QK", "h:1", "h:VO", "down", "h:QK", "h:VO", "h:0", "h:VO",
    "h:1", "bo", "e:0", "h:QK", "e:1", "e:VO", "e:QK",
)


class Layer:
    def __init__(self, args, dp, tensor, bits_of):
        (
            self.x, self.wq, self.wk, self.wv, self.wo, self.wg, self.wu, self.wd,
            self.gain_one, self.gain_two, self.lengths, self.cot,
        ) = args
        self.dp, self.tensor, self.bits_of = dp, tensor, bits_of
        self.heads, self.units = self.wq.shape[1], self.wg.shape[1]
        self.line, self.sums = Line(), {}
        self.block = 256 if self.units >= 2048 else LANES
        blocks = self.units // self.block
        shares = [blocks * n // 8 for n in (5,)]
        self.shares = [*shares, blocks - sum(shares)]
        self.me = jnp.stack([lax.axis_index("dp"), lax.axis_index("tensor") % 2]).astype(jnp.int32)
        self.acts = self.saved = self.gqkv = self.grads = self.grad_input = None
        self.mid_shares, self.in_shares, self.middle_grads, self.gain_sums = [], [], [], {}

    def order(self, name):
        return places(self.dp, self.bits_of[name])

    def begin(self, name, pieces):
        self.sums[name] = Halving(self.line, pieces, (self.dp, self.tensor), self.bits_of[name])

    def shared(self, parts):
        both = [both_shares(part, self.tensor) for part in parts]
        return [own for own, _ in both] + [peer for _, peer in both]

    def attention(self):
        self.q, self.k, self.v, self.mixed, self.probs, part = attention(
            self.x, self.gain_one, self.wq, self.wk, self.wv, self.wo
        )
        self.line.last = part
        self.own, self.peer = both_shares(part, self.tensor)

    def seeds(self):
        self.seed, self.seed_t, self.normed_t = self.line(
            lambda cot: seeds(self.lengths, self.me, cot, self.x, self.gain_one, self.dp), self.cot
        )

    def middles(self):
        self.middle, self.normed, self.normed_two_t = self.line(
            lambda peer: middles(self.me, self.x, self.own, peer, self.gain_two, self.dp), self.peer
        )

    def hidden(self, c):
        *acts, keep, send = self.line(
            lambda normed: hidden_chunk(
                self.block * sum(self.shares[:c]), self.shares[c], self.block, self.order(c),
                normed, self.normed_two_t, self.seed, self.seed_t, self.wg, self.wu, self.wd, self.acts,
            ),
            self.normed,
        )
        self.acts = acts
        self.begin(c, (keep, send))

    def normed_back(self, half):
        parts = self.line(
            lambda gg: normed_two_back(half, gg, self.acts[2], self.wg, self.wu), self.acts[1]
        )
        self.mid_shares.append(self.shared(parts))

    def down(self):
        self.down_shares = self.shared(
            self.line(lambda hidden: hidden_down(hidden, self.wd), self.acts[0])
        )

    def output(self):
        self.block_output = self.line(
            lambda shares: block_outputs(self.middle, shares), self.down_shares
        )

    def middle_back(self, half):
        *self.saved, grad, self.gain_sums["two", half] = self.line(
            lambda shares: middle_back(
                half, self.me, self.middle, self.seed, self.gain_two, self.wo, self.dp, shares, self.saved
            ),
            self.mid_shares[half],
        )
        self.middle_grads.append(grad)

    def attention_back(self, half):
        self.gqkv, *parts = self.line(
            lambda grad_mixed: attention_back(
                half, self.q, self.k, self.v, self.probs, grad_mixed, self.wq, self.wk, self.wv, self.gqkv
            ),
            self.saved[1],
        )
        self.in_shares.append(self.shared(parts))

    def query_key(self):
        self.begin(
            "qk",
            self.line(
                lambda gqkv: query_key_pieces(self.order("qk"), self.normed_t, gqkv, self.heads),
                self.gqkv,
            ),
        )

    def input_back(self, half):
        self.grad_input, self.gain_sums["one", half] = self.line(
            lambda shares: input_grad(
                half, self.x, self.middle_grads[half], self.gain_one, shares, self.grad_input
            ),
            self.in_shares[half],
        )

    def value_out(self):
        gains = [self.gain_sums[name, half] for half in range(HALVES) for name in ("one", "two")]
        self.begin(
            "vo",
            self.line(
                lambda gqkv: value_out_pieces(
                    self.order("vo"), self.normed_t, gqkv, self.saved[0], self.mixed, self.me, *gains
                ),
                self.gqkv,
            ),
        )

    def hop(self, name):
        if self.sums[name].bits:
            self.sums[name].hop()

    def end(self, name):
        one = self.sums[name]
        while one.bits:
            one.hop()
        if name == "qk":
            self.grad_query, self.grad_key = one.end(last_heads, self.heads)
        elif name == "vo":
            self.grad_value, self.grad_out, *self.gains = one.end(last_heads, self.heads)
        else:
            first = self.block * sum(self.shares[:name])
            self.grads = one.end(
                lambda arrays: last_hidden(
                    first, arrays, self.shares[name], self.block, self.units, self.grads
                )
            )

    def run(self):
        calls = {
            "attn": self.attention, "seed": self.seeds, "mid": self.middles, "down": self.down,
            "bo": self.output, "QK": self.query_key, "VO": self.value_out,
        }
        halves = {
            "nt": self.normed_back, "mb": self.middle_back,
            "ab": self.attention_back, "ig": self.input_back,
        }
        for step in STEPS:
            if step in calls:
                calls[step]()
            elif step[:2] in halves:
                halves[step[:2]]("AB".index(step[2:]))
            elif step[0] == "H":
                self.hidden(int(step[1:]))
            else:
                name = step[2:].lower()
                name = int(name) if name.isdigit() else name
                (self.hop if step[0] == "h" else self.end)(name)
        return (
            self.block_output,
            self.grad_input,
            self.grad_query,
            self.grad_key,
            self.grad_value,
            self.grad_out.T,
            self.grads[0],
            self.grads[1],
            self.grads[2].T,
            *self.gains,
        )


def body_of(dp, tensor):
    n_bits = dp.bit_length() - 1

    def order(*start):
        return [1 << k for k in start if k < n_bits] + [1 << k for k in range(n_bits) if k not in start]

    bits_of = {
        0: order(0, 1, 2, 3),
        1: order(2, 0, 1, 3),
        "qk": order(2, 0, 1, 3),
        "vo": order(0, 1, 2, 3),
    }

    def body(*args):
        return Layer(args, dp, tensor, bits_of).run()

    return body


def solution(mesh):
    placed = (
        P("dp", None),
        P(None, "tensor"),
        P(None, "tensor"),
        P(None, "tensor"),
        P("tensor", None),
        P(None, "tensor"),
        P(None, "tensor"),
        P("tensor", None),
        P(),
        P(),
        P("dp"),
        P("dp", None),
    )
    return jax.shard_map(
        body_of(mesh.shape["dp"], mesh.shape["tensor"]),
        mesh=mesh,
        in_specs=placed,
        out_specs=(
            P("dp", None),
            P("dp", None),
            P("dp", "tensor"),
            P("dp", "tensor"),
            P("dp", "tensor"),
            P("tensor", "dp"),
            P("dp", "tensor"),
            P("dp", "tensor"),
            P("tensor", "dp"),
            P("dp"),
            P("dp"),
        ),
        check_vma=False,
    )
```

```python
import functools
import math

import jax
import jax.numpy as jnp
from jax import lax
from jax.experimental import pallas as pl
from jax.experimental.pallas import tpu as pltpu
from jax.sharding import PartitionSpec as P

HD = 64
POS = 16
SLOT = 32
LANES = 128
TILE = 128
MIB = 1 << 20
HALVES = 2
PARTS = 2
COST = 1e-6
SLACK = {}

epsilon = 1e-05
f32 = jnp.float32
bf16 = jnp.bfloat16
SCALE = 1.0 / math.sqrt(HD)
ANYWHERE = jax.ShapeDtypeStruct


def nn(left, right):
    return lax.dot_general(left, right, (((1,), (0,)), ((), ())), preferred_element_type=f32)


def nt(left, right):
    return lax.dot_general(left, right, (((1,), (1,)), ((), ())), preferred_element_type=f32)


def tn(left, right):
    return lax.dot_general(left, right, (((0,), (0,)), ((), ())), preferred_element_type=f32)


def call(body, name, grid, ins, outs, scratch=(), vmem=40, scalars=0, aliases=None, cost=None, far=()):
    kernel = pl.pallas_call(
        body,
        grid_spec=pltpu.PrefetchScalarGridSpec(
            num_scalar_prefetch=scalars,
            grid=grid,
            in_specs=ins,
            out_specs=[spec for spec, *_ in outs],
            scratch_shapes=scratch,
        ),
        out_shape=[
            (where[0] if where else pltpu.HBM)(shape, dtype) for _, shape, dtype, *where in outs
        ],
        input_output_aliases=aliases or {},
        compiler_params=pltpu.CompilerParams(vmem_limit_bytes=vmem * MIB),
        cost_estimate=pl.CostEstimate(
            flops=int(cost[0] * COST + SLACK.get(name, 0)), bytes_accessed=0, transcendentals=0
        ),
        name=name,
    )

    def run(*args):
        return kernel(
            *(
                pltpu.with_memory_space_constraint(arg, pltpu.HBM) if n - scalars in far else arg
                for n, arg in enumerate(args)
            )
        )

    return run


def rows_of(block, width):
    return pl.BlockSpec((block, width), lambda i, *_: (i, 0))


def whole(*shape):
    return pl.BlockSpec(shape, lambda *_: (0,) * len(shape))


def row_of(gain_ref):
    return gain_ref[...].astype(f32).reshape(1, -1)


def inverse_rms(values):
    return lax.rsqrt(jnp.mean(values * values, axis=1, keepdims=True) + epsilon)


def exchanged(index, size):
    low, high = (1, 4) if size >= 16 else (1, 0)
    if size < 4:
        return index
    moved = low | high
    kept = index & ~(3 * moved)
    return kept | (index & moved) << 1 | index >> 1 & moved


def relative(place_ref, g, size):
    apart = g ^ place_ref[0]
    return jnp.where(place_ref[1] == 1, exchanged(apart, size), apart)


def put_transposed(ref, place_ref, values):
    parts, depth, _ = ref.shape
    turned = values.T
    for g in range(parts):
        ref[relative(place_ref, g, parts)] = turned[g * depth : (g + 1) * depth]


def pair_mask():
    rows = lax.broadcasted_iota(jnp.int32, (TILE, 2 * TILE), 0)
    keys = lax.broadcasted_iota(jnp.int32, (TILE, 2 * TILE), 1) & (TILE - 1)
    return (rows // POS == keys // POS) & (keys <= rows)


def two_heads(values):
    first = lax.broadcasted_iota(jnp.int32, values.shape, 1) < HD
    zero = jnp.zeros_like(values)
    return jnp.concatenate(
        [jnp.where(first, values, zero), jnp.where(first, zero, values)], axis=0
    )


def one_pair(values):
    first = lax.broadcasted_iota(jnp.int32, (TILE, LANES), 1) < HD
    return jnp.where(first, values[:TILE], values[TILE:])


def per_head(op, values):
    both = [
        jnp.broadcast_to(op(values[:, s : s + TILE], axis=1, keepdims=True), (TILE, TILE))
        for s in (0, TILE)
    ]
    return jnp.concatenate(both, axis=1)


def probs_of(queries, keys, mask):
    scores = jnp.where(mask, nt(queries, keys) * SCALE, -1e30)
    powers = jnp.exp(scores - per_head(jnp.max, scores))
    return powers / per_head(jnp.sum, powers)


def pairs_of(rows, width):
    return [
        (pl.ds(t * TILE, TILE), pl.ds(p * LANES, LANES))
        for t in range(rows // TILE)
        for p in range(width // LANES)
    ]


def wide(lanes):
    return pl.ds(lanes.start // LANES * 2 * TILE, 2 * TILE)


def attention_body(
    x_ref, gain_ref, wq_ref, wk_ref, wv_ref, wo_ref, q_ref, k_ref, v_ref, m_ref, p_ref, part_ref
):
    normed = normed_of(x_ref, gain_ref)
    q_ref[...] = nn(normed, wq_ref[...]).astype(bf16)
    k_ref[...] = nn(normed, wk_ref[...]).astype(bf16)
    v_ref[...] = nn(normed, wv_ref[...]).astype(bf16)
    mask = pair_mask()
    for at in pairs_of(*q_ref.shape):
        probs = probs_of(q_ref[at], two_heads(k_ref[at]), mask).astype(bf16)
        p_ref[at[0], wide(at[1])] = probs
        m_ref[at] = nn(probs, two_heads(v_ref[at])).astype(bf16)
    part_ref[...] = nn(m_ref[...], wo_ref[...]).astype(bf16)


def attention(x, gain, wq, wk, wv, wo):
    rows, width = x.shape
    heads = wq.shape[1]
    block = 256
    outs = [(rows_of(block, heads), (rows, heads), bf16)] * 4
    spread = 2 * TILE * heads // LANES
    outs += [(rows_of(block, spread), (rows, spread), bf16)]
    outs += [(rows_of(block, width), (rows, width), bf16, ANYWHERE)]
    return call(
        attention_body,
        "attention_forward",
        (rows // block,),
        [rows_of(block, width), whole(width)]
        + [whole(width, heads)] * 3
        + [whole(heads, width)],
        outs,
        vmem=24,
        cost=(8 * rows * width * heads, 12 * MIB),
        far=(0, 2, 3, 4, 5),
    )(x, gain, wq, wk, wv, wo)


def seed_body(lengths_ref, me_ref, cot_ref, x_ref, gain_ref, seed_ref, turned_ref, normed_ref):
    block = cot_ref.shape[0]
    first = pl.program_id(0) * block
    length = lengths_ref[first // (SLOT * POS)]
    row = lax.broadcasted_iota(jnp.int32, cot_ref.shape, 0) + first % (SLOT * POS)
    cot = cot_ref[...].astype(f32)
    seed = jnp.where(row // POS < length, cot, 0.0).astype(bf16)
    seed_ref[...] = seed
    put_transposed(turned_ref, me_ref, seed)
    put_transposed(normed_ref, me_ref, normed_of(x_ref, gain_ref))


def normed_of(x_ref, gain_ref):
    values = x_ref[...].astype(f32)
    return (values * inverse_rms(values) * row_of(gain_ref)).astype(bf16)


def turned_out(parts, depth, rows, block):
    return (
        pl.BlockSpec((parts, depth, block), lambda i, *_: (0, 0, i)),
        (parts, depth, rows),
        bf16,
    )


def seeds(lengths, me, cot, x, gain, parts):
    rows, width = cot.shape
    block = 256
    turned = turned_out(parts, width // parts, rows, block)
    return call(
        seed_body,
        "seed_rows",
        (rows // block,),
        [rows_of(block, width)] * 2 + [whole(width)],
        [(rows_of(block, width), (rows, width), bf16, pltpu.VMEM), (*turned, pltpu.VMEM), turned],
        vmem=16,
        scalars=2,
        far=(0, 1),
        cost=(4 * rows * width, 6 * MIB),
    )(lengths, me, cot, x, gain)


def middle_body(me_ref, x_ref, own_ref, peer_ref, gain_ref, middle_ref, normed_ref, turned_ref):
    middle = x_ref[...].astype(f32) + (own_ref[...].astype(f32) + peer_ref[...].astype(f32))
    middle_ref[...] = middle.astype(bf16)
    normed = (middle * inverse_rms(middle) * row_of(gain_ref)).astype(bf16)
    normed_ref[...] = normed
    put_transposed(turned_ref, me_ref, normed)


def middles(me, x, own, peer, gain, parts):
    rows, width = x.shape
    block = 256
    return call(
        middle_body,
        "middle_rows",
        (rows // block,),
        [rows_of(block, width)] * 3 + [whole(width)],
        [
            (rows_of(block, width), (rows, width), bf16),
            (rows_of(block, width), (rows, width), bf16, pltpu.VMEM),
            (*turned_out(parts, width // parts, rows, block), pltpu.VMEM),
        ],
        vmem=24,
        scalars=1,
        cost=(8 * rows * width, 14 * MIB),
    )(me, x, own, peer, gain)


def places(parts, bits):
    count = len(bits)
    return [
        sum(bit for n, bit in enumerate(bits) if place >> (count - 1 - n) & 1)
        for place in range(parts)
    ]


def put_pieces(keep_ref, send_ref, column, values, order, first):
    half, _, depth, _ = keep_ref.shape
    low = values.astype(bf16)
    for n in range(values.shape[0] // depth):
        place = order.index(first + n)
        ref, at = (keep_ref, place) if place < half else (send_ref, place - half)
        for c in range(values.shape[1] // LANES):
            ref[at, column + c] = low[
                n * depth : (n + 1) * depth, c * LANES : (c + 1) * LANES
            ]


def product_pieces(keep_ref, send_ref, column, turned_ref, right, order):
    parts, depth, rows = turned_ref.shape
    group = max(1, 256 // depth)
    for first in range(0, parts, group):
        left = turned_ref[pl.ds(first, group)].reshape(group * depth, rows)
        put_pieces(keep_ref, send_ref, column, nn(left, right), order, first)


def resident():
    return pl.BlockSpec(memory_space=pltpu.VMEM)


def hidden_body(order, first, block, first_call, *refs):
    (n_ref, nt_ref, s_ref, st_ref, wg_ref, wu_ref, wd_ref) = refs[:7]
    h_ref, gg_ref, gu_ref, keep_ref, send_ref = refs[7 if first_call else 10 :]
    rows = n_ref.shape[0]
    step = min(256, rows)
    here = pl.ds(pl.multiple_of(first + pl.program_id(0) * block, block), block)
    for r in range(0, rows, step):
        at = pl.ds(r, step)
        gate = nn(n_ref[at], wg_ref[:, here])
        up = nn(n_ref[at], wu_ref[:, here])
        back = nt(s_ref[at], wd_ref[...])
        sig = 1.0 / (1.0 + jnp.exp(-gate))
        silu = gate * sig
        h_ref[at] = (silu * up).astype(bf16)
        gg_ref[at, here] = (back * up * (sig * (1.0 + gate * (1.0 - sig)))).astype(bf16)
        gu_ref[at, here] = (back * silu).astype(bf16)
    columns = block // LANES
    product_pieces(keep_ref, send_ref, 0, nt_ref, gg_ref[:, here], order)
    product_pieces(keep_ref, send_ref, columns, nt_ref, gu_ref[:, here], order)
    product_pieces(keep_ref, send_ref, 2 * columns, st_ref, h_ref[...], order)


def hidden_chunk(first, steps, block, order, normed, normed_t, seed, seed_t, wg, wu, wd, earlier):
    rows, width = normed.shape
    parts, depth, _ = normed_t.shape
    hidden = wg.shape[1]
    groups = 3 * block // LANES
    pieces = (
        pl.BlockSpec((parts // 2, groups, depth, LANES), lambda j: (0, j, 0, 0)),
        (parts // 2, steps * groups, depth, LANES),
        bf16,
    )
    args = [normed, normed_t, seed, seed_t, wg, wu, wd]
    ins = [resident()] * 6
    ins.append(pl.BlockSpec((block, width), lambda j: (first // block + j, 0)))
    aliases = {}
    if earlier is not None:
        aliases = {7: 0, 8: 1, 9: 2}
        args += list(earlier)
        ins += [pl.BlockSpec(memory_space=pl.ANY)] + [resident()] * 2
    return call(
        functools.partial(hidden_body, order, first, block, earlier is None),
        "hidden_units",
        (steps,),
        ins,
        [
            (pl.BlockSpec((rows, block), lambda j: (0, first // block + j)), (rows, hidden), bf16),
            *[(resident(), (rows, hidden), bf16, pltpu.VMEM)] * 2,
            pieces,
            (*pieces, ANYWHERE),
        ],
        vmem=14,
        far=(6,),
        aliases=aliases,
        cost=(12 * rows * width * block * steps, 20 * MIB),
    )(*args)


def back_body(first, gg_ref, gu_ref, wg_ref, wu_ref, *part_refs):
    rows = part_refs[0].shape[0]
    here = pl.ds(first, rows * len(part_refs))
    part = nt(gg_ref[here], wg_ref[...]) + nt(gu_ref[here], wu_ref[...])
    for n, ref in enumerate(part_refs):
        ref[...] = part[n * rows : (n + 1) * rows].astype(bf16)


def normed_two_back(half, gg, gu, wg, wu):
    rows, hidden = gg.shape
    rows //= HALVES
    width = wg.shape[0]
    block = 256
    weights = pl.BlockSpec((block, hidden), lambda j: (j, 0))
    piece = rows // PARTS
    out = (pl.BlockSpec((piece, block), lambda j: (0, j)), (piece, width), bf16, ANYWHERE)
    return call(
        functools.partial(back_body, half * rows),
        "normed_two_back",
        (width // block,),
        [resident()] * 2 + [weights] * 2,
        [out] * PARTS,
        vmem=20,
        cost=(4 * rows * width * hidden, 14 * MIB),
    )(gg, gu, wg, wu)


def down_body(h_ref, wd_ref, *part_refs):
    part = nn(h_ref[...], wd_ref[...])
    rows = part_refs[0].shape[0]
    for n, ref in enumerate(part_refs):
        ref[...] = part[n * rows : (n + 1) * rows].astype(bf16)


def hidden_down(hidden, wd):
    rows, units = hidden.shape
    width = wd.shape[1]
    block = 256
    piece = rows // PARTS
    out = (pl.BlockSpec((piece, block), lambda j: (0, j)), (piece, width), bf16, ANYWHERE)
    return call(
        down_body,
        "hidden_down",
        (width // block,),
        [whole(rows, units), pl.BlockSpec((units, block), lambda j: (0, j))],
        [out] * PARTS,
        vmem=24,
        cost=(2 * rows * width * units, 10 * MIB),
    )(hidden, wd)


def add_up(ref, part):
    @pl.when(pl.program_id(0) == 0)
    def _():
        ref[...] = part

    @pl.when(pl.program_id(0) > 0)
    def _():
        ref[...] += part


def shares_sum(pairs, scratch_ref):
    for n in range(PARTS):

        @pl.when(pl.program_id(0) == n)
        def _():
            scratch_ref[...] = pairs[n][...].astype(f32) + pairs[PARTS + n][...].astype(f32)

    return scratch_ref[...]


def middle_back_body(me_ref, mid_ref, seed_ref, gain_ref, wo_ref, *refs):
    turned_ref, mixed_ref, grad_ref, sum_ref, scratch_ref = refs[-5:]
    upstream = shares_sum(refs, scratch_ref)
    middle = mid_ref[...].astype(f32)
    inverse = inverse_rms(middle)
    scaled = middle * inverse
    add_up(sum_ref, jnp.sum(upstream * scaled, axis=0, keepdims=True))
    weighted = upstream * row_of(gain_ref)
    grad_middle = seed_ref[...].astype(f32) + inverse * (
        weighted - scaled * jnp.mean(weighted * scaled, axis=1, keepdims=True)
    )
    low = grad_middle.astype(bf16)
    grad_ref[...] = low
    mixed_ref[...] = nt(low, wo_ref[...]).astype(bf16)
    put_transposed(turned_ref, me_ref, low)


def middle_back(half, me, middle, seed, gain, wo, parts, shares, earlier):
    rows, width = middle.shape
    heads = wo.shape[0]
    share = rows // HALVES
    block = share // PARTS
    depth = width // parts
    there = lambda n: pl.BlockSpec((block, n), lambda i, *_: (half * PARTS + i, 0))
    ins = [there(width)] * 2 + [whole(width), whole(heads, width)]
    ins += [whole(block, width)] * (2 * PARTS)
    args = [me, middle, seed, gain, wo, *shares]
    aliases = {}
    if earlier is not None:
        ins += [pl.BlockSpec(memory_space=pl.ANY)] * 2
        aliases = {len(args) + n: n for n in range(2)}
        args += list(earlier)
    return call(
        middle_back_body,
        "middle_backward",
        (PARTS,),
        ins,
        [
            (
                pl.BlockSpec((parts, depth, block), lambda i, *_: (0, 0, half * PARTS + i)),
                (parts, depth, rows),
                bf16,
            ),
            (there(heads), (rows, heads), bf16),
            (rows_of(block, width), (share, width), bf16),
            (whole(1, width), (1, width), f32, ANYWHERE),
        ],
        scratch=[pltpu.VMEM((block, width), f32)],
        vmem=24,
        scalars=1,
        aliases=aliases,
        cost=(2 * share * width * heads, 9 * MIB),
    )(*args)


def attention_back_body(q_ref, k_ref, v_ref, p_ref, mixed_ref, wq_ref, wk_ref, wv_ref, *refs):
    gqkv_ref, *part_refs = refs[-1 - PARTS :]
    heads = q_ref.shape[1]
    for at in pairs_of(*q_ref.shape):
        rows, lanes = at
        queries, grads = q_ref[at], mixed_ref[at]
        keys, values = two_heads(k_ref[at]), two_heads(v_ref[at])
        low = p_ref[rows, wide(lanes)]
        probs = low.astype(f32)
        grad_probs = nt(grads, values)
        grad_values = one_pair(tn(low, grads))
        inner = per_head(jnp.sum, grad_probs * probs)
        grad_scores = (probs * (grad_probs - inner)).astype(bf16)
        grad_queries = nn(grad_scores, keys) * SCALE
        grad_keys = one_pair(tn(grad_scores, queries)) * SCALE
        for n, grad in enumerate((grad_queries, grad_keys, grad_values)):
            gqkv_ref[rows, pl.ds(n * heads + lanes.start, LANES)] = grad.astype(bf16)
    part = nt(gqkv_ref[:, :heads], wq_ref[...])
    part += nt(gqkv_ref[:, heads : 2 * heads], wk_ref[...])
    part += nt(gqkv_ref[:, 2 * heads :], wv_ref[...])
    for n, ref in enumerate(part_refs):

        @pl.when(pl.program_id(0) == n)
        def _():
            ref[...] = part.astype(bf16)


def attention_back(half, q, k, v, probs, grad_mixed, wq, wk, wv, earlier):
    rows, heads = q.shape
    width = wq.shape[0]
    share = rows // HALVES
    block = share // PARTS
    there = lambda n: pl.BlockSpec((block, n), lambda i: (half * PARTS + i, 0))
    ins = [there(heads)] * 3 + [there(probs.shape[1]), there(heads)] + [whole(width, heads)] * 3
    args = [q, k, v, probs, grad_mixed, wq, wk, wv]
    aliases = {}
    if earlier is not None:
        ins.append(pl.BlockSpec(memory_space=pl.ANY))
        aliases = {len(args): 0}
        args.append(earlier)
    return call(
        attention_back_body,
        "attention_backward",
        (PARTS,),
        ins,
        [
            (there(3 * heads), (rows, 3 * heads), bf16, ANYWHERE),
            *[(whole(block, width), (block, width), bf16, ANYWHERE)] * PARTS,
        ],
        vmem=32,
        far=(4,),
        aliases=aliases,
        cost=(6 * share * width * heads, 9 * MIB),
    )(*args)


def query_key_body(order, turned_ref, right_ref, keep_ref, send_ref):
    product_pieces(keep_ref, send_ref, 0, turned_ref, right_ref[...], order)


def query_key_pieces(order, turned, right, heads):
    parts, depth, rows = turned.shape
    groups = heads // LANES
    pieces = (
        pl.BlockSpec((parts // 2, groups, depth, LANES), lambda j: (0, j, 0, 0)),
        (parts // 2, 2 * groups, depth, LANES),
        bf16,
    )
    return call(
        functools.partial(query_key_body, order),
        "query_key_grads",
        (2,),
        [whole(parts, depth, rows), pl.BlockSpec((rows, heads), lambda j: (0, j))],
        [pieces, (*pieces, ANYWHERE)],
        vmem=24,
        cost=(4 * rows * parts * depth * heads, 6 * MIB),
    )(turned, right)


def value_out_body(order, value_ref, right_ref, out_ref, mixed_ref, me_ref, *refs):
    *gain_refs, keep_ref, send_ref = refs
    groups = right_ref.shape[1] // LANES
    product_pieces(keep_ref, send_ref, 0, value_ref, right_ref[...], order)
    product_pieces(keep_ref, send_ref, groups, out_ref, mixed_ref[...], order)
    first, second = (sum(ref[...] for ref in gain_refs[n::2]) for n in range(2))
    row = lax.broadcasted_iota(jnp.int32, (LANES, first.shape[1]), 0)
    both = jnp.where(row == 0, first, jnp.where(row == 1, second, 0.0))
    turned = both.T.astype(bf16)
    half, _, depth, _ = keep_ref.shape
    bits = [order[1 << n] for n in reversed(range((2 * half).bit_length() - 1))]
    for g in range(2 * half):
        apart = relative(me_ref, g, 2 * half)
        place = 0
        for bit in bits:
            place = 2 * place + (apart & bit != 0).astype(jnp.int32)
        piece = turned[g * depth : (g + 1) * depth]

        @pl.when(place < half)
        def _():
            keep_ref[jnp.minimum(place, half - 1), 2 * groups] = piece

        @pl.when(place >= half)
        def _():
            send_ref[jnp.maximum(place - half, 0), 2 * groups] = piece


def value_out_pieces(order, turned, right, out_turned, mixed, me, *gains):
    parts, depth, rows = turned.shape
    heads = mixed.shape[1]
    shape = (parts // 2, 2 * heads // LANES + 1, depth, LANES)
    return call(
        functools.partial(value_out_body, order),
        "value_out_grads",
        (1,),
        [
            whole(parts, depth, rows),
            pl.BlockSpec((rows, heads), lambda j: (0, 2)),
            whole(parts, depth, rows),
            whole(rows, heads),
            pl.BlockSpec(memory_space=pltpu.SMEM),
            *[whole(1, parts * depth)] * len(gains),
        ],
        [(whole(*shape), shape, bf16), (whole(*shape), shape, bf16, ANYWHERE)],
        vmem=32,
        cost=(4 * rows * parts * depth * heads, 8 * MIB),
    )(turned, right, out_turned, mixed, me, *gains)


def input_grad_body(x_ref, gm_ref, gain_ref, *refs):
    out_ref, sum_ref, scratch_ref = refs[-3:]
    inputs = x_ref[...].astype(f32)
    inverse = inverse_rms(inputs)
    scaled = inputs * inverse
    upstream = shares_sum(refs, scratch_ref)
    add_up(sum_ref, jnp.sum(upstream * scaled, axis=0, keepdims=True))
    weighted = upstream * row_of(gain_ref)
    out_ref[...] = (
        gm_ref[...].astype(f32)
        + inverse * (weighted - scaled * jnp.mean(weighted * scaled, axis=1, keepdims=True))
    ).astype(bf16)


def input_grad(half, x, grad_middle, gain, shares, earlier):
    rows, width = x.shape
    block = rows // HALVES // PARTS
    there = pl.BlockSpec((block, width), lambda i: (half * PARTS + i, 0))
    ins = [there, rows_of(block, width), whole(width)] + [whole(block, width)] * (2 * PARTS)
    args = [x, grad_middle, gain, *shares]
    aliases = {}
    if earlier is not None:
        ins.append(pl.BlockSpec(memory_space=pl.ANY))
        aliases = {len(args): 0}
        args.append(earlier)
    return call(
        input_grad_body,
        "input_grad",
        (PARTS,),
        ins,
        [(there, (rows, width), bf16), (whole(1, width), (1, width), f32, ANYWHERE)],
        scratch=[pltpu.VMEM((block, width), f32)],
        vmem=24,
        aliases=aliases,
        cost=(10 * rows // HALVES * width, 6 * MIB),
    )(*args)


def total_of(refs):
    total = refs[0][0].astype(f32)
    for ref in refs[1:]:
        total += ref[0].astype(f32)
    return total


def last_hidden_body(count, block, first_call, *refs):
    total = total_of(refs[:count])
    outs = refs[count if first_call else count + 3 :]
    third = block // LANES
    for c in range(total.shape[0]):
        n, at = c // third % 3, (c // (3 * third) * third + c % third) * LANES
        outs[n][:, at : at + LANES] = total[c]


def last_hidden(first, arrays, steps, block, hidden, earlier):
    _, groups, depth, _ = arrays[0].shape
    at_once = math.gcd(first // block, steps)
    steps //= at_once
    ins = [pl.BlockSpec((1, groups // steps, depth, LANES), lambda j: (0, j, 0, 0))] * len(arrays)
    args = list(arrays)
    aliases = {}
    if earlier is not None:
        ins += [pl.BlockSpec(memory_space=pl.ANY)] * 3
        aliases = {len(arrays) + n: n for n in range(3)}
        args += list(earlier)
    wide = block * at_once
    out = (pl.BlockSpec((depth, wide), lambda j: (0, first // wide + j)), (depth, hidden), f32)
    return call(
        functools.partial(last_hidden_body, len(arrays), block, earlier is None),
        "hidden_grads_out",
        (steps,),
        ins,
        [out] * 3,
        vmem=16,
        aliases=aliases,
        cost=(6 * groups * depth * LANES, MIB),
    )(*args)


def last_heads_body(count, *refs):
    total = total_of(refs[:count])
    outs = refs[count:]
    groups = outs[0].shape[1] // LANES
    for n, ref in enumerate(outs[:2]):
        for c in range(groups):
            ref[:, c * LANES : (c + 1) * LANES] = total[n * groups + c]
    if len(outs) > 2:
        turned = total[2 * groups].T
        for n, ref in enumerate(outs[2:]):
            ref[...] = turned[n]


def last_heads(arrays, heads):
    _, groups, depth, _ = arrays[0].shape
    shapes = [(depth, heads)] * 2
    if groups * LANES > 2 * heads:
        shapes += [(depth,)] * 2
    return call(
        functools.partial(last_heads_body, len(arrays)),
        "head_grads_out",
        (1,),
        [pl.BlockSpec((1, groups, depth, LANES), lambda j: (0, 0, 0, 0))] * len(arrays),
        [(whole(*shape), shape, f32) for shape in shapes],
        vmem=16,
        cost=(6 * groups * depth * LANES, MIB),
    )(*arrays)


def block_output_body(mid_ref, *refs):
    out_ref, scratch_ref = refs[-2:]
    out_ref[...] = (mid_ref[...].astype(f32) + shares_sum(refs, scratch_ref)).astype(bf16)


def block_outputs(middle, shares):
    rows, width = middle.shape
    block = rows // PARTS
    return call(
        block_output_body,
        "block_output",
        (PARTS,),
        [rows_of(block, width)] + [whole(block, width)] * (2 * PARTS),
        [(rows_of(block, width), (rows, width), bf16)],
        scratch=[pltpu.VMEM((block, width), f32)],
        vmem=24,
        cost=(3 * rows * width, 10 * MIB),
    )(middle, *shares)[0]


def swap(array, axis, size, bit):
    return lax.ppermute(array, axis, [(i, i ^ bit) for i in range(size)])


def hop_swap(array, dp, tensor, bit):
    bits = [exchanged(bit, dp) if t % 2 else bit for t in range(tensor)]
    pairs = [
        (i * tensor + t, (i ^ bits[t]) * tensor + t) for i in range(dp) for t in range(tensor)
    ]
    return lax.ppermute(array, ("dp", "tensor"), pairs)


def both_shares(partial, size):
    bit = 1
    while 2 * bit < size:
        other = swap(partial, "tensor", size, bit)
        partial = (partial.astype(f32) + other.astype(f32)).astype(bf16)
        bit *= 2
    return partial, swap(partial, "tensor", size, bit)


def after(value, *others):
    return lax.optimization_barrier((value, *others))[0]


def next_send_body(*refs):
    total = refs[0][...].astype(f32)
    for ref in refs[1:-1]:
        total += ref[...].astype(f32)
    refs[-1][...] = total.astype(bf16)


def next_send(half, arrays):
    _, *rest = arrays[0].shape
    block = max(1, half // 2)
    steps = half // block
    return call(
        next_send_body,
        "next_send",
        (steps,),
        [pl.BlockSpec((block, *rest), lambda i: (steps + i, 0, 0, 0))] * len(arrays),
        [(pl.BlockSpec((block, *rest), lambda i: (i, 0, 0, 0)), (half, *rest), bf16, ANYWHERE)],
        vmem=16,
        cost=(half * math.prod(rest), MIB),
    )(*arrays)[0]


class Line:
    def __init__(self):
        self.last = None

    def __call__(self, kernel, waits, *args):
        if self.last is not None:
            waits, _ = lax.optimization_barrier((waits, self.last))
        out = kernel(waits, *args)
        self.last = jax.tree.leaves(out)[-1]
        return out


class Halving:
    def __init__(self, line, pieces, sizes, bits):
        self.line, self.sizes, self.bits = line, sizes, list(bits)
        self.arrays = [pieces[0]]
        self.half = sizes[0] // 2
        self.launch(pieces[1])

    def launch(self, send):
        self.coming = hop_swap(send, *self.sizes, self.bits.pop(0))

    def hop(self):
        self.arrays.append(self.coming)
        self.half //= 2
        self.launch(
            self.line(
                lambda newest: next_send(self.half, [*self.arrays[:-1], newest]), self.arrays[-1]
            )
        )

    def end(self, kernel, *rest):
        return self.line(lambda newest: kernel([*self.arrays, newest], *rest), self.coming)


STEPS = (
    "attn", "seed", "mid", "H0", "H1", "ntA", "ntB", "mbA", "mbB", "abA", "h:0", "abB", "QK",
    "igA", "h:1", "igB", "VO", "h:0", "h:QK", "h:1", "h:VO", "down", "h:QK", "h:VO", "h:0", "h:VO",
    "h:1", "bo", "e:0", "h:QK", "e:1", "e:VO", "e:QK",
)


class Layer:
    def __init__(self, args, dp, tensor, bits_of):
        (
            self.x, self.wq, self.wk, self.wv, self.wo, self.wg, self.wu, self.wd,
            self.gain_one, self.gain_two, self.lengths, self.cot,
        ) = args
        self.dp, self.tensor, self.bits_of = dp, tensor, bits_of
        self.heads, self.units = self.wq.shape[1], self.wg.shape[1]
        self.line, self.sums = Line(), {}
        self.block = 256 if self.units >= 2048 else LANES
        blocks = self.units // self.block
        shares = [blocks * n // 8 for n in (5,)]
        self.shares = [*shares, blocks - sum(shares)]
        self.me = jnp.stack([lax.axis_index("dp"), lax.axis_index("tensor") % 2]).astype(jnp.int32)
        self.acts = self.saved = self.gqkv = self.grads = self.grad_input = None
        self.mid_shares, self.in_shares, self.middle_grads, self.gain_sums = [], [], [], {}

    def order(self, name):
        return places(self.dp, self.bits_of[name])

    def begin(self, name, pieces):
        self.sums[name] = Halving(self.line, pieces, (self.dp, self.tensor), self.bits_of[name])

    def shared(self, parts):
        both = [both_shares(part, self.tensor) for part in parts]
        return [own for own, _ in both] + [peer for _, peer in both]

    def attention(self):
        self.q, self.k, self.v, self.mixed, self.probs, part = attention(
            self.x, self.gain_one, self.wq, self.wk, self.wv, self.wo
        )
        self.line.last = part
        self.own, self.peer = both_shares(part, self.tensor)

    def seeds(self):
        self.seed, self.seed_t, self.normed_t = self.line(
            lambda cot: seeds(self.lengths, self.me, cot, self.x, self.gain_one, self.dp), self.cot
        )

    def middles(self):
        self.middle, self.normed, self.normed_two_t = self.line(
            lambda peer: middles(self.me, self.x, self.own, peer, self.gain_two, self.dp), self.peer
        )

    def hidden(self, c):
        *acts, keep, send = self.line(
            lambda normed: hidden_chunk(
                self.block * sum(self.shares[:c]), self.shares[c], self.block, self.order(c),
                normed, self.normed_two_t, self.seed, self.seed_t, self.wg, self.wu, self.wd, self.acts,
            ),
            self.normed,
        )
        self.acts = acts
        self.begin(c, (keep, send))

    def normed_back(self, half):
        parts = self.line(
            lambda gg: normed_two_back(half, gg, self.acts[2], self.wg, self.wu), self.acts[1]
        )
        self.mid_shares.append(self.shared(parts))

    def down(self):
        self.down_shares = self.shared(
            self.line(lambda hidden: hidden_down(hidden, self.wd), self.acts[0])
        )

    def output(self):
        self.block_output = self.line(
            lambda shares: block_outputs(self.middle, shares), self.down_shares
        )

    def middle_back(self, half):
        *self.saved, grad, self.gain_sums["two", half] = self.line(
            lambda shares: middle_back(
                half, self.me, self.middle, self.seed, self.gain_two, self.wo, self.dp, shares, self.saved
            ),
            self.mid_shares[half],
        )
        self.middle_grads.append(grad)

    def attention_back(self, half):
        self.gqkv, *parts = self.line(
            lambda grad_mixed: attention_back(
                half, self.q, self.k, self.v, self.probs, grad_mixed, self.wq, self.wk, self.wv, self.gqkv
            ),
            self.saved[1],
        )
        self.in_shares.append(self.shared(parts))

    def query_key(self):
        self.begin(
            "qk",
            self.line(
                lambda gqkv: query_key_pieces(self.order("qk"), self.normed_t, gqkv, self.heads),
                self.gqkv,
            ),
        )

    def input_back(self, half):
        self.grad_input, self.gain_sums["one", half] = self.line(
            lambda shares: input_grad(
                half, self.x, self.middle_grads[half], self.gain_one, shares, self.grad_input
            ),
            self.in_shares[half],
        )

    def value_out(self):
        gains = [self.gain_sums[name, half] for half in range(HALVES) for name in ("one", "two")]
        self.begin(
            "vo",
            self.line(
                lambda gqkv: value_out_pieces(
                    self.order("vo"), self.normed_t, gqkv, self.saved[0], self.mixed, self.me, *gains
                ),
                self.gqkv,
            ),
        )

    def hop(self, name):
        if self.sums[name].bits:
            self.sums[name].hop()

    def end(self, name):
        one = self.sums[name]
        while one.bits:
            one.hop()
        if name == "qk":
            self.grad_query, self.grad_key = one.end(last_heads, self.heads)
        elif name == "vo":
            self.grad_value, self.grad_out, *self.gains = one.end(last_heads, self.heads)
        else:
            first = self.block * sum(self.shares[:name])
            self.grads = one.end(
                lambda arrays: last_hidden(
                    first, arrays, self.shares[name], self.block, self.units, self.grads
                )
            )

    def run(self):
        calls = {
            "attn": self.attention, "seed": self.seeds, "mid": self.middles, "down": self.down,
            "bo": self.output, "QK": self.query_key, "VO": self.value_out,
        }
        halves = {
            "nt": self.normed_back, "mb": self.middle_back,
            "ab": self.attention_back, "ig": self.input_back,
        }
        for step in STEPS:
            if step in calls:
                calls[step]()
            elif step[:2] in halves:
                halves[step[:2]]("AB".index(step[2:]))
            elif step[0] == "H":
                self.hidden(int(step[1:]))
            else:
                name = step[2:].lower()
                name = int(name) if name.isdigit() else name
                (self.hop if step[0] == "h" else self.end)(name)
        return (
            self.block_output,
            self.grad_input,
            self.grad_query,
            self.grad_key,
            self.grad_value,
            self.grad_out.T,
            self.grads[0],
            self.grads[1],
            self.grads[2].T,
            *self.gains,
        )


def body_of(dp, tensor):
    n_bits = dp.bit_length() - 1

    def order(*start):
        return [1 << k for k in start if k < n_bits] + [1 << k for k in range(n_bits) if k not in start]

    bits_of = {
        0: order(0, 1, 2, 3),
        1: order(2, 0, 1, 3),
        "qk": order(2, 0, 1, 3),
        "vo": order(0, 1, 2, 3),
    }

    def body(*args):
        return Layer(args, dp, tensor, bits_of).run()

    return body


def solution(mesh):
    placed = (
        P("dp", None),
        P(None, "tensor"),
        P(None, "tensor"),
        P(None, "tensor"),
        P("tensor", None),
        P(None, "tensor"),
        P(None, "tensor"),
        P("tensor", None),
        P(),
        P(),
        P("dp"),
        P("dp", None),
    )
    return jax.shard_map(
        body_of(mesh.shape["dp"], mesh.shape["tensor"]),
        mesh=mesh,
        in_specs=placed,
        out_specs=(
            P("dp", None),
            P("dp", None),
            P("dp", "tensor"),
            P("dp", "tensor"),
            P("dp", "tensor"),
            P("tensor", "dp"),
            P("dp", "tensor"),
            P("dp", "tensor"),
            P("tensor", "dp"),
            P("dp"),
            P("dp"),
        ),
        check_vma=False,
    )
```

```python
import functools
import math

import jax
import jax.numpy as jnp
from jax import lax
from jax.experimental import pallas as pl
from jax.experimental.pallas import tpu as pltpu
from jax.sharding import PartitionSpec as P

HD = 64
POS = 16
SLOT = 32
LANES = 128
TILE = 128
MIB = 1 << 20
HALVES = 2
PARTS = 2
COST = 1e-6
SLACK = {}

epsilon = 1e-05
f32 = jnp.float32
bf16 = jnp.bfloat16
SCALE = 1.0 / math.sqrt(HD)
ANYWHERE = jax.ShapeDtypeStruct


def nn(left, right):
    return lax.dot_general(left, right, (((1,), (0,)), ((), ())), preferred_element_type=f32)


def nt(left, right):
    return lax.dot_general(left, right, (((1,), (1,)), ((), ())), preferred_element_type=f32)


def tn(left, right):
    return lax.dot_general(left, right, (((0,), (0,)), ((), ())), preferred_element_type=f32)


def call(body, name, grid, ins, outs, scratch=(), vmem=40, scalars=0, aliases=None, cost=None, far=()):
    kernel = pl.pallas_call(
        body,
        grid_spec=pltpu.PrefetchScalarGridSpec(
            num_scalar_prefetch=scalars,
            grid=grid,
            in_specs=ins,
            out_specs=[spec for spec, *_ in outs],
            scratch_shapes=scratch,
        ),
        out_shape=[
            (where[0] if where else pltpu.HBM)(shape, dtype) for _, shape, dtype, *where in outs
        ],
        input_output_aliases=aliases or {},
        compiler_params=pltpu.CompilerParams(vmem_limit_bytes=vmem * MIB),
        cost_estimate=pl.CostEstimate(
            flops=int(cost[0] * COST + SLACK.get(name, 0)), bytes_accessed=0, transcendentals=0
        ),
        name=name,
    )

    def run(*args):
        return kernel(
            *(
                pltpu.with_memory_space_constraint(arg, pltpu.HBM) if n - scalars in far else arg
                for n, arg in enumerate(args)
            )
        )

    return run


def rows_of(block, width):
    return pl.BlockSpec((block, width), lambda i, *_: (i, 0))


def whole(*shape):
    return pl.BlockSpec(shape, lambda *_: (0,) * len(shape))


def row_of(gain_ref):
    return gain_ref[...].astype(f32).reshape(1, -1)


def inverse_rms(values):
    return lax.rsqrt(jnp.mean(values * values, axis=1, keepdims=True) + epsilon)


def exchanged(index, size):
    low, high = (1, 4) if size >= 16 else (1, 0)
    if size < 4:
        return index
    moved = low | high
    kept = index & ~(3 * moved)
    return kept | (index & moved) << 1 | index >> 1 & moved


def relative(place_ref, g, size):
    apart = g ^ place_ref[0]
    return jnp.where(place_ref[1] == 1, exchanged(apart, size), apart)


def put_transposed(ref, place_ref, values):
    parts, depth, _ = ref.shape
    turned = values.T
    for g in range(parts):
        ref[relative(place_ref, g, parts)] = turned[g * depth : (g + 1) * depth]


def pair_mask():
    rows = lax.broadcasted_iota(jnp.int32, (TILE, 2 * TILE), 0)
    keys = lax.broadcasted_iota(jnp.int32, (TILE, 2 * TILE), 1) & (TILE - 1)
    return (rows // POS == keys // POS) & (keys <= rows)


def two_heads(values):
    first = lax.broadcasted_iota(jnp.int32, values.shape, 1) < HD
    zero = jnp.zeros_like(values)
    return jnp.concatenate(
        [jnp.where(first, values, zero), jnp.where(first, zero, values)], axis=0
    )


def one_pair(values):
    first = lax.broadcasted_iota(jnp.int32, (TILE, LANES), 1) < HD
    return jnp.where(first, values[:TILE], values[TILE:])


def per_head(op, values):
    both = [
        jnp.broadcast_to(op(values[:, s : s + TILE], axis=1, keepdims=True), (TILE, TILE))
        for s in (0, TILE)
    ]
    return jnp.concatenate(both, axis=1)


def probs_of(queries, keys, mask):
    scores = jnp.where(mask, nt(queries, keys) * SCALE, -1e30)
    powers = jnp.exp(scores - per_head(jnp.max, scores))
    return powers / per_head(jnp.sum, powers)


def pairs_of(rows, width):
    return [
        (pl.ds(t * TILE, TILE), pl.ds(p * LANES, LANES))
        for t in range(rows // TILE)
        for p in range(width // LANES)
    ]


def wide(lanes):
    return pl.ds(lanes.start // LANES * 2 * TILE, 2 * TILE)


def attention_body(
    x_ref, gain_ref, wq_ref, wk_ref, wv_ref, wo_ref, q_ref, k_ref, v_ref, m_ref, p_ref, part_ref
):
    normed = normed_of(x_ref, gain_ref)
    q_ref[...] = nn(normed, wq_ref[...]).astype(bf16)
    k_ref[...] = nn(normed, wk_ref[...]).astype(bf16)
    v_ref[...] = nn(normed, wv_ref[...]).astype(bf16)
    mask = pair_mask()
    for at in pairs_of(*q_ref.shape):
        probs = probs_of(q_ref[at], two_heads(k_ref[at]), mask).astype(bf16)
        p_ref[at[0], wide(at[1])] = probs
        m_ref[at] = nn(probs, two_heads(v_ref[at])).astype(bf16)
    part_ref[...] = nn(m_ref[...], wo_ref[...]).astype(bf16)


def attention(x, gain, wq, wk, wv, wo):
    rows, width = x.shape
    heads = wq.shape[1]
    block = 256
    outs = [(rows_of(block, heads), (rows, heads), bf16)] * 4
    spread = 2 * TILE * heads // LANES
    outs += [(rows_of(block, spread), (rows, spread), bf16)]
    outs += [(rows_of(block, width), (rows, width), bf16, ANYWHERE)]
    return call(
        attention_body,
        "attention_forward",
        (rows // block,),
        [rows_of(block, width), whole(width)]
        + [whole(width, heads)] * 3
        + [whole(heads, width)],
        outs,
        vmem=24,
        cost=(8 * rows * width * heads, 12 * MIB),
        far=(0, 1, 2, 3, 4, 5),
    )(x, gain, wq, wk, wv, wo)


def seed_body(lengths_ref, me_ref, cot_ref, x_ref, gain_ref, seed_ref, turned_ref, normed_ref):
    block = cot_ref.shape[0]
    first = pl.program_id(0) * block
    length = lengths_ref[first // (SLOT * POS)]
    row = lax.broadcasted_iota(jnp.int32, cot_ref.shape, 0) + first % (SLOT * POS)
    cot = cot_ref[...].astype(f32)
    seed = jnp.where(row // POS < length, cot, 0.0).astype(bf16)
    seed_ref[...] = seed
    put_transposed(turned_ref, me_ref, seed)
    put_transposed(normed_ref, me_ref, normed_of(x_ref, gain_ref))


def normed_of(x_ref, gain_ref):
    values = x_ref[...].astype(f32)
    return (values * inverse_rms(values) * row_of(gain_ref)).astype(bf16)


def turned_out(parts, depth, rows, block):
    return (
        pl.BlockSpec((parts, depth, block), lambda i, *_: (0, 0, i)),
        (parts, depth, rows),
        bf16,
    )


def seeds(lengths, me, cot, x, gain, parts):
    rows, width = cot.shape
    block = 256
    turned = turned_out(parts, width // parts, rows, block)
    return call(
        seed_body,
        "seed_rows",
        (rows // block,),
        [rows_of(block, width)] * 2 + [whole(width)],
        [(rows_of(block, width), (rows, width), bf16, pltpu.VMEM), (*turned, pltpu.VMEM), turned],
        vmem=16,
        scalars=2,
        far=(0, 1),
        cost=(4 * rows * width, 6 * MIB),
    )(lengths, me, cot, x, gain)


def middle_body(me_ref, x_ref, own_ref, peer_ref, gain_ref, middle_ref, normed_ref, turned_ref):
    middle = x_ref[...].astype(f32) + (own_ref[...].astype(f32) + peer_ref[...].astype(f32))
    middle_ref[...] = middle.astype(bf16)
    normed = (middle * inverse_rms(middle) * row_of(gain_ref)).astype(bf16)
    normed_ref[...] = normed
    put_transposed(turned_ref, me_ref, normed)


def middles(me, x, own, peer, gain, parts):
    rows, width = x.shape
    block = 256
    return call(
        middle_body,
        "middle_rows",
        (rows // block,),
        [rows_of(block, width)] * 3 + [whole(width)],
        [
            (rows_of(block, width), (rows, width), bf16),
            (rows_of(block, width), (rows, width), bf16, pltpu.VMEM),
            (*turned_out(parts, width // parts, rows, block), pltpu.VMEM),
        ],
        vmem=24,
        scalars=1,
        cost=(8 * rows * width, 14 * MIB),
    )(me, x, own, peer, gain)


def places(parts, bits):
    count = len(bits)
    return [
        sum(bit for n, bit in enumerate(bits) if place >> (count - 1 - n) & 1)
        for place in range(parts)
    ]


def put_pieces(keep_ref, send_ref, column, values, order, first):
    half, _, depth, _ = keep_ref.shape
    low = values.astype(bf16)
    for n in range(values.shape[0] // depth):
        place = order.index(first + n)
        ref, at = (keep_ref, place) if place < half else (send_ref, place - half)
        for c in range(values.shape[1] // LANES):
            ref[at, column + c] = low[
                n * depth : (n + 1) * depth, c * LANES : (c + 1) * LANES
            ]


def product_pieces(keep_ref, send_ref, column, turned_ref, right, order):
    parts, depth, rows = turned_ref.shape
    group = max(1, 256 // depth)
    for first in range(0, parts, group):
        left = turned_ref[pl.ds(first, group)].reshape(group * depth, rows)
        put_pieces(keep_ref, send_ref, column, nn(left, right), order, first)


def resident():
    return pl.BlockSpec(memory_space=pltpu.VMEM)


def hidden_body(order, first, block, first_call, *refs):
    (n_ref, nt_ref, s_ref, st_ref, wg_ref, wu_ref, wd_ref) = refs[:7]
    h_ref, gg_ref, gu_ref, keep_ref, send_ref = refs[7 if first_call else 10 :]
    rows = n_ref.shape[0]
    step = min(256, rows)
    here = pl.ds(pl.multiple_of(first + pl.program_id(0) * block, block), block)
    for r in range(0, rows, step):
        at = pl.ds(r, step)
        gate = nn(n_ref[at], wg_ref[:, here])
        up = nn(n_ref[at], wu_ref[:, here])
        back = nt(s_ref[at], wd_ref[...])
        sig = 1.0 / (1.0 + jnp.exp(-gate))
        silu = gate * sig
        h_ref[at] = (silu * up).astype(bf16)
        gg_ref[at, here] = (back * up * (sig * (1.0 + gate * (1.0 - sig)))).astype(bf16)
        gu_ref[at, here] = (back * silu).astype(bf16)
    columns = block // LANES
    product_pieces(keep_ref, send_ref, 0, nt_ref, gg_ref[:, here], order)
    product_pieces(keep_ref, send_ref, columns, nt_ref, gu_ref[:, here], order)
    product_pieces(keep_ref, send_ref, 2 * columns, st_ref, h_ref[...], order)


def hidden_chunk(first, steps, block, order, normed, normed_t, seed, seed_t, wg, wu, wd, earlier):
    rows, width = normed.shape
    parts, depth, _ = normed_t.shape
    hidden = wg.shape[1]
    groups = 3 * block // LANES
    pieces = (
        pl.BlockSpec((parts // 2, groups, depth, LANES), lambda j: (0, j, 0, 0)),
        (parts // 2, steps * groups, depth, LANES),
        bf16,
    )
    args = [normed, normed_t, seed, seed_t, wg, wu, wd]
    ins = [resident()] * 6
    ins.append(pl.BlockSpec((block, width), lambda j: (first // block + j, 0)))
    aliases = {}
    if earlier is not None:
        aliases = {7: 0, 8: 1, 9: 2}
        args += list(earlier)
        ins += [pl.BlockSpec(memory_space=pl.ANY)] + [resident()] * 2
    return call(
        functools.partial(hidden_body, order, first, block, earlier is None),
        "hidden_units",
        (steps,),
        ins,
        [
            (pl.BlockSpec((rows, block), lambda j: (0, first // block + j)), (rows, hidden), bf16),
            *[(resident(), (rows, hidden), bf16, pltpu.VMEM)] * 2,
            pieces,
            (*pieces, ANYWHERE),
        ],
        vmem=14,
        far=(6,),
        aliases=aliases,
        cost=(12 * rows * width * block * steps, 20 * MIB),
    )(*args)


def back_body(first, gg_ref, gu_ref, wg_ref, wu_ref, *part_refs):
    rows = part_refs[0].shape[0]
    here = pl.ds(first, rows * len(part_refs))
    part = nt(gg_ref[here], wg_ref[...]) + nt(gu_ref[here], wu_ref[...])
    for n, ref in enumerate(part_refs):
        ref[...] = part[n * rows : (n + 1) * rows].astype(bf16)


def normed_two_back(half, gg, gu, wg, wu):
    rows, hidden = gg.shape
    rows //= HALVES
    width = wg.shape[0]
    block = 256
    weights = pl.BlockSpec((block, hidden), lambda j: (j, 0))
    piece = rows // PARTS
    out = (pl.BlockSpec((piece, block), lambda j: (0, j)), (piece, width), bf16, ANYWHERE)
    return call(
        functools.partial(back_body, half * rows),
        "normed_two_back",
        (width // block,),
        [resident()] * 2 + [weights] * 2,
        [out] * PARTS,
        vmem=20,
        cost=(4 * rows * width * hidden, 14 * MIB),
    )(gg, gu, wg, wu)


def down_body(h_ref, wd_ref, *part_refs):
    part = nn(h_ref[...], wd_ref[...])
    rows = part_refs[0].shape[0]
    for n, ref in enumerate(part_refs):
        ref[...] = part[n * rows : (n + 1) * rows].astype(bf16)


def hidden_down(hidden, wd):
    rows, units = hidden.shape
    width = wd.shape[1]
    block = 256
    piece = rows // PARTS
    out = (pl.BlockSpec((piece, block), lambda j: (0, j)), (piece, width), bf16, ANYWHERE)
    return call(
        down_body,
        "hidden_down",
        (width // block,),
        [whole(rows, units), pl.BlockSpec((units, block), lambda j: (0, j))],
        [out] * PARTS,
        vmem=24,
        cost=(2 * rows * width * units, 10 * MIB),
    )(hidden, wd)


def add_up(ref, part):
    @pl.when(pl.program_id(0) == 0)
    def _():
        ref[...] = part

    @pl.when(pl.program_id(0) > 0)
    def _():
        ref[...] += part


def shares_sum(pairs, scratch_ref):
    for n in range(PARTS):

        @pl.when(pl.program_id(0) == n)
        def _():
            scratch_ref[...] = pairs[n][...].astype(f32) + pairs[PARTS + n][...].astype(f32)

    return scratch_ref[...]


def middle_back_body(me_ref, mid_ref, seed_ref, gain_ref, wo_ref, *refs):
    turned_ref, mixed_ref, grad_ref, sum_ref, scratch_ref = refs[-5:]
    upstream = shares_sum(refs, scratch_ref)
    middle = mid_ref[...].astype(f32)
    inverse = inverse_rms(middle)
    scaled = middle * inverse
    add_up(sum_ref, jnp.sum(upstream * scaled, axis=0, keepdims=True))
    weighted = upstream * row_of(gain_ref)
    grad_middle = seed_ref[...].astype(f32) + inverse * (
        weighted - scaled * jnp.mean(weighted * scaled, axis=1, keepdims=True)
    )
    low = grad_middle.astype(bf16)
    grad_ref[...] = low
    mixed_ref[...] = nt(low, wo_ref[...]).astype(bf16)
    put_transposed(turned_ref, me_ref, low)


def middle_back(half, me, middle, seed, gain, wo, parts, shares, earlier):
    rows, width = middle.shape
    heads = wo.shape[0]
    share = rows // HALVES
    block = share // PARTS
    depth = width // parts
    there = lambda n: pl.BlockSpec((block, n), lambda i, *_: (half * PARTS + i, 0))
    ins = [there(width)] * 2 + [whole(width), whole(heads, width)]
    ins += [whole(block, width)] * (2 * PARTS)
    args = [me, middle, seed, gain, wo, *shares]
    aliases = {}
    if earlier is not None:
        ins += [pl.BlockSpec(memory_space=pl.ANY)] * 2
        aliases = {len(args) + n: n for n in range(2)}
        args += list(earlier)
    return call(
        middle_back_body,
        "middle_backward",
        (PARTS,),
        ins,
        [
            (
                pl.BlockSpec((parts, depth, block), lambda i, *_: (0, 0, half * PARTS + i)),
                (parts, depth, rows),
                bf16,
            ),
            (there(heads), (rows, heads), bf16),
            (rows_of(block, width), (share, width), bf16),
            (whole(1, width), (1, width), f32, ANYWHERE),
        ],
        scratch=[pltpu.VMEM((block, width), f32)],
        vmem=24,
        scalars=1,
        aliases=aliases,
        cost=(2 * share * width * heads, 9 * MIB),
    )(*args)


def attention_back_body(q_ref, k_ref, v_ref, p_ref, mixed_ref, wq_ref, wk_ref, wv_ref, *refs):
    gqkv_ref, *part_refs = refs[-1 - PARTS :]
    heads = q_ref.shape[1]
    for at in pairs_of(*q_ref.shape):
        rows, lanes = at
        queries, grads = q_ref[at], mixed_ref[at]
        keys, values = two_heads(k_ref[at]), two_heads(v_ref[at])
        low = p_ref[rows, wide(lanes)]
        probs = low.astype(f32)
        grad_probs = nt(grads, values)
        grad_values = one_pair(tn(low, grads))
        inner = per_head(jnp.sum, grad_probs * probs)
        grad_scores = (probs * (grad_probs - inner)).astype(bf16)
        grad_queries = nn(grad_scores, keys) * SCALE
        grad_keys = one_pair(tn(grad_scores, queries)) * SCALE
        for n, grad in enumerate((grad_queries, grad_keys, grad_values)):
            gqkv_ref[rows, pl.ds(n * heads + lanes.start, LANES)] = grad.astype(bf16)
    part = nt(gqkv_ref[:, :heads], wq_ref[...])
    part += nt(gqkv_ref[:, heads : 2 * heads], wk_ref[...])
    part += nt(gqkv_ref[:, 2 * heads :], wv_ref[...])
    for n, ref in enumerate(part_refs):

        @pl.when(pl.program_id(0) == n)
        def _():
            ref[...] = part.astype(bf16)


def attention_back(half, q, k, v, probs, grad_mixed, wq, wk, wv, earlier):
    rows, heads = q.shape
    width = wq.shape[0]
    share = rows // HALVES
    block = share // PARTS
    there = lambda n: pl.BlockSpec((block, n), lambda i: (half * PARTS + i, 0))
    ins = [there(heads)] * 3 + [there(probs.shape[1]), there(heads)] + [whole(width, heads)] * 3
    args = [q, k, v, probs, grad_mixed, wq, wk, wv]
    aliases = {}
    if earlier is not None:
        ins.append(pl.BlockSpec(memory_space=pl.ANY))
        aliases = {len(args): 0}
        args.append(earlier)
    return call(
        attention_back_body,
        "attention_backward",
        (PARTS,),
        ins,
        [
            (there(3 * heads), (rows, 3 * heads), bf16, ANYWHERE),
            *[(whole(block, width), (block, width), bf16, ANYWHERE)] * PARTS,
        ],
        vmem=32,
        far=(4,),
        aliases=aliases,
        cost=(6 * share * width * heads, 9 * MIB),
    )(*args)


def query_key_body(order, turned_ref, right_ref, keep_ref, send_ref):
    product_pieces(keep_ref, send_ref, 0, turned_ref, right_ref[...], order)


def query_key_pieces(order, turned, right, heads):
    parts, depth, rows = turned.shape
    groups = heads // LANES
    pieces = (
        pl.BlockSpec((parts // 2, groups, depth, LANES), lambda j: (0, j, 0, 0)),
        (parts // 2, 2 * groups, depth, LANES),
        bf16,
    )
    return call(
        functools.partial(query_key_body, order),
        "query_key_grads",
        (2,),
        [whole(parts, depth, rows), pl.BlockSpec((rows, heads), lambda j: (0, j))],
        [pieces, (*pieces, ANYWHERE)],
        vmem=24,
        cost=(4 * rows * parts * depth * heads, 6 * MIB),
    )(turned, right)


def value_out_body(order, value_ref, right_ref, out_ref, mixed_ref, me_ref, *refs):
    *gain_refs, keep_ref, send_ref = refs
    groups = right_ref.shape[1] // LANES
    product_pieces(keep_ref, send_ref, 0, value_ref, right_ref[...], order)
    product_pieces(keep_ref, send_ref, groups, out_ref, mixed_ref[...], order)
    first, second = (sum(ref[...] for ref in gain_refs[n::2]) for n in range(2))
    row = lax.broadcasted_iota(jnp.int32, (LANES, first.shape[1]), 0)
    both = jnp.where(row == 0, first, jnp.where(row == 1, second, 0.0))
    turned = both.T.astype(bf16)
    half, _, depth, _ = keep_ref.shape
    bits = [order[1 << n] for n in reversed(range((2 * half).bit_length() - 1))]
    for g in range(2 * half):
        apart = relative(me_ref, g, 2 * half)
        place = 0
        for bit in bits:
            place = 2 * place + (apart & bit != 0).astype(jnp.int32)
        piece = turned[g * depth : (g + 1) * depth]

        @pl.when(place < half)
        def _():
            keep_ref[jnp.minimum(place, half - 1), 2 * groups] = piece

        @pl.when(place >= half)
        def _():
            send_ref[jnp.maximum(place - half, 0), 2 * groups] = piece


def value_out_pieces(order, turned, right, out_turned, mixed, me, *gains):
    parts, depth, rows = turned.shape
    heads = mixed.shape[1]
    shape = (parts // 2, 2 * heads // LANES + 1, depth, LANES)
    return call(
        functools.partial(value_out_body, order),
        "value_out_grads",
        (1,),
        [
            whole(parts, depth, rows),
            pl.BlockSpec((rows, heads), lambda j: (0, 2)),
            whole(parts, depth, rows),
            whole(rows, heads),
            pl.BlockSpec(memory_space=pltpu.SMEM),
            *[whole(1, parts * depth)] * len(gains),
        ],
        [(whole(*shape), shape, bf16), (whole(*shape), shape, bf16, ANYWHERE)],
        vmem=32,
        cost=(4 * rows * parts * depth * heads, 8 * MIB),
    )(turned, right, out_turned, mixed, me, *gains)


def input_grad_body(x_ref, gm_ref, gain_ref, *refs):
    out_ref, sum_ref, scratch_ref = refs[-3:]
    inputs = x_ref[...].astype(f32)
    inverse = inverse_rms(inputs)
    scaled = inputs * inverse
    upstream = shares_sum(refs, scratch_ref)
    add_up(sum_ref, jnp.sum(upstream * scaled, axis=0, keepdims=True))
    weighted = upstream * row_of(gain_ref)
    out_ref[...] = (
        gm_ref[...].astype(f32)
        + inverse * (weighted - scaled * jnp.mean(weighted * scaled, axis=1, keepdims=True))
    ).astype(bf16)


def input_grad(half, x, grad_middle, gain, shares, earlier):
    rows, width = x.shape
    block = rows // HALVES // PARTS
    there = pl.BlockSpec((block, width), lambda i: (half * PARTS + i, 0))
    ins = [there, rows_of(block, width), whole(width)] + [whole(block, width)] * (2 * PARTS)
    args = [x, grad_middle, gain, *shares]
    aliases = {}
    if earlier is not None:
        ins.append(pl.BlockSpec(memory_space=pl.ANY))
        aliases = {len(args): 0}
        args.append(earlier)
    return call(
        input_grad_body,
        "input_grad",
        (PARTS,),
        ins,
        [(there, (rows, width), bf16), (whole(1, width), (1, width), f32, ANYWHERE)],
        scratch=[pltpu.VMEM((block, width), f32)],
        vmem=24,
        aliases=aliases,
        cost=(10 * rows // HALVES * width, 6 * MIB),
    )(*args)


def total_of(refs):
    total = refs[0][0].astype(f32)
    for ref in refs[1:]:
        total += ref[0].astype(f32)
    return total


def last_hidden_body(count, block, first_call, *refs):
    total = total_of(refs[:count])
    outs = refs[count if first_call else count + 3 :]
    third = block // LANES
    for c in range(total.shape[0]):
        n, at = c // third % 3, (c // (3 * third) * third + c % third) * LANES
        outs[n][:, at : at + LANES] = total[c]


def last_hidden(first, arrays, steps, block, hidden, earlier):
    _, groups, depth, _ = arrays[0].shape
    at_once = math.gcd(first // block, steps)
    steps //= at_once
    ins = [pl.BlockSpec((1, groups // steps, depth, LANES), lambda j: (0, j, 0, 0))] * len(arrays)
    args = list(arrays)
    aliases = {}
    if earlier is not None:
        ins += [pl.BlockSpec(memory_space=pl.ANY)] * 3
        aliases = {len(arrays) + n: n for n in range(3)}
        args += list(earlier)
    wide = block * at_once
    out = (pl.BlockSpec((depth, wide), lambda j: (0, first // wide + j)), (depth, hidden), f32)
    return call(
        functools.partial(last_hidden_body, len(arrays), block, earlier is None),
        "hidden_grads_out",
        (steps,),
        ins,
        [out] * 3,
        vmem=16,
        aliases=aliases,
        cost=(6 * groups * depth * LANES, MIB),
    )(*args)


def last_heads_body(count, *refs):
    total = total_of(refs[:count])
    outs = refs[count:]
    groups = outs[0].shape[1] // LANES
    for n, ref in enumerate(outs[:2]):
        for c in range(groups):
            ref[:, c * LANES : (c + 1) * LANES] = total[n * groups + c]
    if len(outs) > 2:
        turned = total[2 * groups].T
        for n, ref in enumerate(outs[2:]):
            ref[...] = turned[n]


def last_heads(arrays, heads):
    _, groups, depth, _ = arrays[0].shape
    shapes = [(depth, heads)] * 2
    if groups * LANES > 2 * heads:
        shapes += [(depth,)] * 2
    return call(
        functools.partial(last_heads_body, len(arrays)),
        "head_grads_out",
        (1,),
        [pl.BlockSpec((1, groups, depth, LANES), lambda j: (0, 0, 0, 0))] * len(arrays),
        [(whole(*shape), shape, f32) for shape in shapes],
        vmem=16,
        cost=(6 * groups * depth * LANES, MIB),
    )(*arrays)


def block_output_body(mid_ref, *refs):
    out_ref, scratch_ref = refs[-2:]
    out_ref[...] = (mid_ref[...].astype(f32) + shares_sum(refs, scratch_ref)).astype(bf16)


def block_outputs(middle, shares):
    rows, width = middle.shape
    block = rows // PARTS
    return call(
        block_output_body,
        "block_output",
        (PARTS,),
        [rows_of(block, width)] + [whole(block, width)] * (2 * PARTS),
        [(rows_of(block, width), (rows, width), bf16)],
        scratch=[pltpu.VMEM((block, width), f32)],
        vmem=24,
        cost=(3 * rows * width, 10 * MIB),
    )(middle, *shares)[0]


def swap(array, axis, size, bit):
    return lax.ppermute(array, axis, [(i, i ^ bit) for i in range(size)])


def hop_swap(array, dp, tensor, bit):
    bits = [exchanged(bit, dp) if t % 2 else bit for t in range(tensor)]
    pairs = [
        (i * tensor + t, (i ^ bits[t]) * tensor + t) for i in range(dp) for t in range(tensor)
    ]
    return lax.ppermute(array, ("dp", "tensor"), pairs)


def both_shares(partial, size):
    bit = 1
    while 2 * bit < size:
        other = swap(partial, "tensor", size, bit)
        partial = (partial.astype(f32) + other.astype(f32)).astype(bf16)
        bit *= 2
    return partial, swap(partial, "tensor", size, bit)


def after(value, *others):
    return lax.optimization_barrier((value, *others))[0]


def next_send_body(*refs):
    total = refs[0][...].astype(f32)
    for ref in refs[1:-1]:
        total += ref[...].astype(f32)
    refs[-1][...] = total.astype(bf16)


def next_send(half, arrays):
    _, *rest = arrays[0].shape
    block = max(1, half // 2)
    steps = half // block
    return call(
        next_send_body,
        "next_send",
        (steps,),
        [pl.BlockSpec((block, *rest), lambda i: (steps + i, 0, 0, 0))] * len(arrays),
        [(pl.BlockSpec((block, *rest), lambda i: (i, 0, 0, 0)), (half, *rest), bf16, ANYWHERE)],
        vmem=16,
        cost=(half * math.prod(rest), MIB),
    )(*arrays)[0]


class Line:
    def __init__(self):
        self.last = None

    def __call__(self, kernel, waits, *args):
        if self.last is not None:
            waits, _ = lax.optimization_barrier((waits, self.last))
        out = kernel(waits, *args)
        self.last = jax.tree.leaves(out)[-1]
        return out


class Halving:
    def __init__(self, line, pieces, sizes, bits):
        self.line, self.sizes, self.bits = line, sizes, list(bits)
        self.arrays = [pieces[0]]
        self.half = sizes[0] // 2
        self.launch(pieces[1])

    def launch(self, send):
        self.coming = hop_swap(send, *self.sizes, self.bits.pop(0))

    def hop(self):
        self.arrays.append(self.coming)
        self.half //= 2
        self.launch(
            self.line(
                lambda newest: next_send(self.half, [*self.arrays[:-1], newest]), self.arrays[-1]
            )
        )

    def end(self, kernel, *rest):
        return self.line(lambda newest: kernel([*self.arrays, newest], *rest), self.coming)


STEPS = (
    "attn", "seed", "mid", "H0", "H1", "ntA", "ntB", "mbA", "mbB", "abA", "h:0", "abB", "QK",
    "igA", "h:1", "igB", "VO", "h:0", "h:QK", "h:1", "h:VO", "down", "h:QK", "h:VO", "h:0", "h:VO",
    "h:1", "bo", "e:0", "h:QK", "e:1", "e:VO", "e:QK",
)


class Layer:
    def __init__(self, args, dp, tensor, bits_of):
        (
            self.x, self.wq, self.wk, self.wv, self.wo, self.wg, self.wu, self.wd,
            self.gain_one, self.gain_two, self.lengths, self.cot,
        ) = args
        self.dp, self.tensor, self.bits_of = dp, tensor, bits_of
        self.heads, self.units = self.wq.shape[1], self.wg.shape[1]
        self.line, self.sums = Line(), {}
        self.block = 256 if self.units >= 2048 else LANES
        blocks = self.units // self.block
        shares = [blocks * n // 8 for n in (5,)]
        self.shares = [*shares, blocks - sum(shares)]
        self.me = jnp.stack([lax.axis_index("dp"), lax.axis_index("tensor") % 2]).astype(jnp.int32)
        self.acts = self.saved = self.gqkv = self.grads = self.grad_input = None
        self.mid_shares, self.in_shares, self.middle_grads, self.gain_sums = [], [], [], {}

    def order(self, name):
        return places(self.dp, self.bits_of[name])

    def begin(self, name, pieces):
        self.sums[name] = Halving(self.line, pieces, (self.dp, self.tensor), self.bits_of[name])

    def shared(self, parts):
        both = [both_shares(part, self.tensor) for part in parts]
        return [own for own, _ in both] + [peer for _, peer in both]

    def attention(self):
        self.q, self.k, self.v, self.mixed, self.probs, part = attention(
            self.x, self.gain_one, self.wq, self.wk, self.wv, self.wo
        )
        self.line.last = part
        self.own, self.peer = both_shares(part, self.tensor)

    def seeds(self):
        self.seed, self.seed_t, self.normed_t = self.line(
            lambda cot: seeds(self.lengths, self.me, cot, self.x, self.gain_one, self.dp), self.cot
        )

    def middles(self):
        self.middle, self.normed, self.normed_two_t = self.line(
            lambda peer: middles(self.me, self.x, self.own, peer, self.gain_two, self.dp), self.peer
        )

    def hidden(self, c):
        *acts, keep, send = self.line(
            lambda normed: hidden_chunk(
                self.block * sum(self.shares[:c]), self.shares[c], self.block, self.order(c),
                normed, self.normed_two_t, self.seed, self.seed_t, self.wg, self.wu, self.wd, self.acts,
            ),
            self.normed,
        )
        self.acts = acts
        self.begin(c, (keep, send))

    def normed_back(self, half):
        parts = self.line(
            lambda gg: normed_two_back(half, gg, self.acts[2], self.wg, self.wu), self.acts[1]
        )
        self.mid_shares.append(self.shared(parts))

    def down(self):
        self.down_shares = self.shared(
            self.line(lambda hidden: hidden_down(hidden, self.wd), self.acts[0])
        )

    def output(self):
        self.block_output = self.line(
            lambda shares: block_outputs(self.middle, shares), self.down_shares
        )

    def middle_back(self, half):
        *self.saved, grad, self.gain_sums["two", half] = self.line(
            lambda shares: middle_back(
                half, self.me, self.middle, self.seed, self.gain_two, self.wo, self.dp, shares, self.saved
            ),
            self.mid_shares[half],
        )
        self.middle_grads.append(grad)

    def attention_back(self, half):
        self.gqkv, *parts = self.line(
            lambda grad_mixed: attention_back(
                half, self.q, self.k, self.v, self.probs, grad_mixed, self.wq, self.wk, self.wv, self.gqkv
            ),
            self.saved[1],
        )
        self.in_shares.append(self.shared(parts))

    def query_key(self):
        self.begin(
            "qk",
            self.line(
                lambda gqkv: query_key_pieces(self.order("qk"), self.normed_t, gqkv, self.heads),
                self.gqkv,
            ),
        )

    def input_back(self, half):
        self.grad_input, self.gain_sums["one", half] = self.line(
            lambda shares: input_grad(
                half, self.x, self.middle_grads[half], self.gain_one, shares, self.grad_input
            ),
            self.in_shares[half],
        )

    def value_out(self):
        gains = [self.gain_sums[name, half] for half in range(HALVES) for name in ("one", "two")]
        self.begin(
            "vo",
            self.line(
                lambda gqkv: value_out_pieces(
                    self.order("vo"), self.normed_t, gqkv, self.saved[0], self.mixed, self.me, *gains
                ),
                self.gqkv,
            ),
        )

    def hop(self, name):
        if self.sums[name].bits:
            self.sums[name].hop()

    def end(self, name):
        one = self.sums[name]
        while one.bits:
            one.hop()
        if name == "qk":
            self.grad_query, self.grad_key = one.end(last_heads, self.heads)
        elif name == "vo":
            self.grad_value, self.grad_out, *self.gains = one.end(last_heads, self.heads)
        else:
            first = self.block * sum(self.shares[:name])
            self.grads = one.end(
                lambda arrays: last_hidden(
                    first, arrays, self.shares[name], self.block, self.units, self.grads
                )
            )

    def run(self):
        calls = {
            "attn": self.attention, "seed": self.seeds, "mid": self.middles, "down": self.down,
            "bo": self.output, "QK": self.query_key, "VO": self.value_out,
        }
        halves = {
            "nt": self.normed_back, "mb": self.middle_back,
            "ab": self.attention_back, "ig": self.input_back,
        }
        for step in STEPS:
            if step in calls:
                calls[step]()
            elif step[:2] in halves:
                halves[step[:2]]("AB".index(step[2:]))
            elif step[0] == "H":
                self.hidden(int(step[1:]))
            else:
                name = step[2:].lower()
                name = int(name) if name.isdigit() else name
                (self.hop if step[0] == "h" else self.end)(name)
        return (
            self.block_output,
            self.grad_input,
            self.grad_query,
            self.grad_key,
            self.grad_value,
            self.grad_out.T,
            self.grads[0],
            self.grads[1],
            self.grads[2].T,
            *self.gains,
        )


def body_of(dp, tensor):
    n_bits = dp.bit_length() - 1

    def order(*start):
        return [1 << k for k in start if k < n_bits] + [1 << k for k in range(n_bits) if k not in start]

    bits_of = {
        0: order(0, 1, 2, 3),
        1: order(2, 0, 1, 3),
        "qk": order(2, 0, 1, 3),
        "vo": order(0, 1, 2, 3),
    }

    def body(*args):
        return Layer(args, dp, tensor, bits_of).run()

    return body


def solution(mesh):
    placed = (
        P("dp", None),
        P(None, "tensor"),
        P(None, "tensor"),
        P(None, "tensor"),
        P("tensor", None),
        P(None, "tensor"),
        P(None, "tensor"),
        P("tensor", None),
        P(),
        P(),
        P("dp"),
        P("dp", None),
    )
    return jax.shard_map(
        body_of(mesh.shape["dp"], mesh.shape["tensor"]),
        mesh=mesh,
        in_specs=placed,
        out_specs=(
            P("dp", None),
            P("dp", None),
            P("dp", "tensor"),
            P("dp", "tensor"),
            P("dp", "tensor"),
            P("tensor", "dp"),
            P("dp", "tensor"),
            P("dp", "tensor"),
            P("tensor", "dp"),
            P("dp"),
            P("dp"),
        ),
        check_vma=False,
    )
```
